32 devices in a mesh: fsdp: 2 (over core), ctx: 4 (over z), tp: 4 (over y, x).
Axes of the slice: x: 2, y: 2, z: 4, core: 2. Of those that a mesh axis runs over, the one named last changes fastest.
Arguments:
- hidden_in: bfloat16 [8, 256, 1536], P('fsdp', 'ctx'), may hold values from -6 to 6
- segment_ids: int32 [8, 256], P('fsdp', 'ctx'), may hold values from 0 to 5, as said below
- doc_starts: int32 [8, 4], P('fsdp', 'ctx'), may hold values from 0 to 129, as said below
- norm1_gain: bfloat16 [1536], P(('fsdp', 'ctx')), may hold values from 0.5 to 1.5
- w_query: bfloat16 [1536, 1536], P(('fsdp', 'ctx'), 'tp'), may hold values from -0.15625 to 0.15625
- w_key: bfloat16 [1536, 1536], P(('fsdp', 'ctx'), 'tp'), may hold values from -0.15625 to 0.15625
- w_value: bfloat16 [1536, 1536], P(('fsdp', 'ctx'), 'tp'), may hold values from -0.15625 to 0.15625
- w_house: bfloat16 [1536, 1536], P(('fsdp', 'ctx'), 'tp'), may hold values from -0.15625 to 0.15625
- w_beta: bfloat16 [1536, 12], P(('fsdp', 'ctx'), 'tp'), may hold values from -0.5 to 0.5
- w_out: bfloat16 [1536, 1536], P(('fsdp', 'ctx'), 'tp'), may hold values from -0.625 to 0.625
- norm2_gain: bfloat16 [1536], P(('fsdp', 'ctx')), may hold values from 0.5 to 1.5
- w_gate: bfloat16 [1536, 4096], P(('fsdp', 'ctx'), 'tp'), may hold values from -0.15625 to 0.15625
- w_up: bfloat16 [1536, 4096], P(('fsdp', 'ctx'), 'tp'), may hold values from -0.15625 to 0.15625
- w_down: bfloat16 [1536, 4096], P(('fsdp', 'ctx'), 'tp'), may hold values from -0.09375 to 0.09375
- output_grad: bfloat16 [8, 256, 1536], P('fsdp', 'ctx'), may hold values from -6 to 6
Outputs:
- block_out: bfloat16 [8, 256, 1536], P('fsdp', 'ctx')
- input_grad: bfloat16 [8, 256, 1536], P('fsdp', 'ctx')
- norm1_gain_grad: float32 [1536], P(('fsdp', 'ctx'))
- w_query_grad: float32 [1536, 1536], P(('fsdp', 'ctx'), 'tp')
- w_key_grad: float32 [1536, 1536], P(('fsdp', 'ctx'), 'tp')
- w_value_grad: float32 [1536, 1536], P(('fsdp', 'ctx'), 'tp')
- w_house_grad: float32 [1536, 1536], P(('fsdp', 'ctx'), 'tp')
- w_beta_grad: float32 [1536, 12], P(('fsdp', 'ctx'), 'tp')
- w_out_grad: float32 [1536, 1536], P(('fsdp', 'ctx'), 'tp')
- norm2_gain_grad: float32 [1536], P(('fsdp', 'ctx'))
- w_gate_grad: float32 [1536, 4096], P(('fsdp', 'ctx'), 'tp')
- w_up_grad: float32 [1536, 4096], P(('fsdp', 'ctx'), 'tp')
- w_down_grad: float32 [1536, 4096], P(('fsdp', 'ctx'), 'tp')
The draws below stay inside these ranges and needn't reach their ends.
Inputs may be any that keep to these rules, and one draw needn't show every extreme that they name: `segment_ids`: ids never fall along a sequence; each sequence holds 6 documents, numbered in order from 0; the last document of each sequence begins one position after the first position of its second-to-last group and runs to the end. `doc_starts`: for group c of 64 positions, the position within the sequence where the document that holds position c * 64 begins, as given by segment_ids; it is at most c * 64.
All inputs are finite; a program needn't handle non-finite values.
Results may differ from the reference program's by a relative error of at most 0.02.
Values may be sent and summed in bfloat16 or wider, within the bound.
No kernel may reach another device: no remote copies, remote signals or barrier semaphores. Data moves between devices by JAX's collectives and lax.ppermute only.
A program may use at most 128 MiB of HBM per device.

```python
import math
import jax
import jax.numpy as jnp
from jax import lax

D = 1536
HEADS = 12
DH = 128
FF = 4096
GROUP = 64
DOCS = 6
LEN = 256
SEQS = 8


def doc_cuts(key):

    def one_sequence(seq_key):
        picks = jax.random.permutation(seq_key, 31)[:DOCS - 2] + 1
        ordered = jnp.sort(picks).astype(jnp.int32)
        rank = jnp.arange(DOCS - 2, dtype=jnp.int32)
        inner = (LEN - 2 * GROUP - DOCS) * ordered * ordered * ordered // 29791 + rank + 1
        final = jnp.full((1,), LEN - 2 * GROUP + 1, dtype=jnp.int32)
        return jnp.concatenate([inner.astype(jnp.int32), final], axis=0)
    seq_keys = jax.random.split(jax.random.fold_in(key, 7), SEQS)
    return jax.vmap(one_sequence)(seq_keys)


def draw_segment_ids(key, part):
    cuts = doc_cuts(key)
    positions = jnp.arange(LEN, dtype=jnp.int32)
    return jnp.sum((cuts[:, None, :] <= positions[None, :, None]).astype(jnp.int32), axis=-1).astype(jnp.int32)


def draw_doc_starts(key, part):
    cuts = doc_cuts(key)
    firsts = jnp.arange(LEN // GROUP, dtype=jnp.int32) * GROUP
    inside = cuts[:, None, :] <= firsts[None, :, None]
    return jnp.max(jnp.where(inside, cuts[:, None, :], 0), axis=-1).astype(jnp.int32)


def draw_w_beta(key, part):
    scale_key, entry_key = jax.random.split(jax.random.fold_in(key, 11))
    log_scale = jax.random.uniform(scale_key, (HEADS,), jnp.float32, math.log(1.5), math.log(7.0))
    entries = jax.random.normal(entry_key, (D, HEADS), jnp.float32)
    spread = jnp.exp(log_scale) / math.sqrt(D)
    return jnp.clip(entries * spread[None, :], -0.5, 0.5).astype(jnp.bfloat16)


def strengthened(drawn, rng, source, target, shards_of, factor):
    def block_of(dim):
        return (jnp.arange(drawn.shape[dim]) // (drawn.shape[dim] // shards_of)).reshape((-1,) + (1,) * (drawn.ndim - 1 - dim))

    one_side = jax.random.permutation(rng, shards_of)[block_of(target)]
    far = (block_of(target) + shards_of // 2) % shards_of
    return jnp.where((block_of(source) == one_side) | (block_of(source) == far), factor * drawn, drawn)


def block_levels(own_key, dims, cuts, low, largest):
    factor_of, own = 1.0, jax.random.fold_in(own_key, 6)
    for dim, parts in cuts:
        draws = jnp.exp(jax.random.uniform(jax.random.fold_in(own, dim), (parts,), jnp.float32, low / len(cuts), largest / len(cuts)))
        factor_of = factor_of * jnp.repeat(draws, dims[dim] // parts).reshape([-1 if axis == dim else 1 for axis in range(len(dims))])
    return factor_of


def bell_draw(own_key, shape, scale, bound, shards=(), kind=jnp.bfloat16):
    factor_of = block_levels(own_key, shape, shards, -0.22, 0.18) if shards else 1.0
    values = jax.random.normal(own_key, shape, jnp.float32) * scale * factor_of
    return jnp.minimum(jnp.maximum(values, -bound), bound).astype(kind)


def gaussian_with(stream_key, dims, deviation, most, cuts, heavy, kind=jnp.bfloat16):
    result = deviation * jax.random.normal(stream_key, dims, jnp.float32)
    if cuts:
        result = result * block_levels(stream_key, dims, cuts, -0.22, 0.18)
    return jnp.clip(strengthened(result, jax.random.fold_in(stream_key, 3), *heavy), -most, most).astype(kind)


def setup_inputs(seed: int = 0) -> dict:
    seeds = jax.random.split(jax.random.key(seed), 16)
    hidden_in = gaussian_with(seeds[0], (SEQS, LEN, D), 1.0, 6.0, ((0, 2), (1, 4)), (1, 2, 4, 2.0))
    segment_ids = draw_segment_ids(jax.random.fold_in(seeds[15], 71), 0)
    doc_starts = draw_doc_starts(jax.random.fold_in(seeds[15], 71), 0)
    norm1_gain = jnp.clip(1.0 + 0.1 * jax.random.normal(seeds[3], (D,), jnp.float32), 0.5, 1.5).astype(jnp.bfloat16)
    w_query = bell_draw(seeds[4], (D, HEADS * DH), D ** -0.5, 0.15625, ((0, 8), (1, 4)))
    w_key = bell_draw(seeds[5], (D, HEADS * DH), D ** -0.5, 0.15625, ((0, 8), (1, 4)))
    w_value = bell_draw(seeds[6], (D, HEADS * DH), D ** -0.5, 0.15625, ((0, 8), (1, 4)))
    w_house = bell_draw(seeds[7], (D, HEADS * DH), D ** -0.5, 0.15625, ((0, 8), (1, 4)))
    w_beta = draw_w_beta(jax.random.fold_in(seeds[15], 71), 0)
    w_out = bell_draw(seeds[9], (D, HEADS * DH), (HEADS * DH // 16) ** -0.5, 0.625, ((0, 8), (1, 4)))
    norm2_gain = jnp.clip(1.0 + 0.1 * jax.random.normal(seeds[10], (D,), jnp.float32), 0.5, 1.5).astype(jnp.bfloat16)
    w_gate = bell_draw(seeds[11], (D, FF), D ** -0.5, 0.15625, ((0, 8), (1, 4)))
    w_up = bell_draw(seeds[12], (D, FF), D ** -0.5, 0.15625, ((0, 8), (1, 4)))
    w_down = bell_draw(seeds[13], (D, FF), FF ** -0.5, 0.09375, ((0, 8), (1, 4)))
    output_grad = gaussian_with(seeds[14], (SEQS, LEN, D), 1.0, 6.0, ((0, 2), (1, 4)), (1, 2, 4, 2.0))
    return dict(hidden_in=hidden_in, segment_ids=segment_ids, doc_starts=doc_starts, norm1_gain=norm1_gain, w_query=w_query, w_key=w_key, w_value=w_value, w_house=w_house, w_beta=w_beta, w_out=w_out, norm2_gain=norm2_gain, w_gate=w_gate, w_up=w_up, w_down=w_down, output_grad=output_grad)


EPSILON = 1e-06
HIGHEST = lax.Precision.HIGHEST
NEGATIVE = -1e+30

@jax.custom_vjp
def low(v):
    return lax.optimization_barrier(v.astype(jnp.bfloat16)).astype(jnp.float32)

@jax.custom_vjp
def low_back(v):
    return v

def low_keep(v):
    return (low(v), None)

def low_pass(kept, grad):
    return (grad,)

def back_keep(v):
    return (v, None)

def back_low(kept, grad):
    return (low(grad),)
low.defvjp(low_keep, low_pass)
low_back.defvjp(back_keep, back_low)

def group_algebra(queries, key_rows, house, betas):
    length = queries.shape[0]
    scaling = 1.0 / math.sqrt(queries.shape[1])
    row_index = lax.broadcasted_iota(jnp.int32, (length, length), 0)
    column_index = lax.broadcasted_iota(jnp.int32, (length, length), 1)
    strict_below = row_index > column_index
    house_gram = jnp.dot(house, house.T, precision=HIGHEST)
    system = jnp.where(strict_below, house_gram, 0.0) + jnp.diag(1.0 / betas)
    identity = jnp.eye(length, dtype=house.dtype)
    inverse = jax.scipy.linalg.solve_triangular(system, identity, lower=True)
    query_house = jnp.where(row_index >= column_index, jnp.dot(queries, house.T, precision=HIGHEST), 0.0)
    house_key = jnp.where(strict_below, jnp.dot(house, key_rows.T, precision=HIGHEST), 0.0)
    query_side = jnp.dot(query_house, inverse, precision=HIGHEST)
    key_side = jnp.dot(inverse, house_key, precision=HIGHEST)
    scores = (jnp.dot(queries, key_rows.T, precision=HIGHEST) - jnp.dot(query_side, house_key, precision=HIGHEST)) * scaling
    query_bar = queries - jnp.dot(query_side, house, precision=HIGHEST)
    key_bar = key_rows - jnp.dot(key_side.T, house, precision=HIGHEST)
    inner = jnp.dot(inverse, house, precision=HIGHEST)
    factor = jnp.eye(house.shape[1], dtype=house.dtype) - jnp.dot(house.T, inner, precision=HIGHEST)
    return (scores, query_bar, key_bar, factor)

def local_map(queries, key_rows, house_raw, beta_logits):
    house = house_raw * lax.rsqrt(lax.optimization_barrier(jnp.sum(house_raw * house_raw, axis=-1, keepdims=True)) + EPSILON)
    betas = 2.0 * jax.nn.sigmoid(beta_logits)
    return jax.vmap(jax.vmap(group_algebra))(queries, key_rows, house, betas)

def doc_starts_local(segment_ids, group_first, first_position):
    offsets = lax.broadcasted_iota(jnp.int32, segment_ids.shape, segment_ids.ndim - 1)
    previous = jnp.concatenate([segment_ids[..., :1], segment_ids[..., :-1]], axis=-1)
    boundary = (offsets > 0) & (segment_ids != previous)
    marks = jnp.where(boundary, offsets + first_position, -1)
    return jnp.maximum(lax.cummax(marks, axis=segment_ids.ndim - 1), group_first)

def shift_groups(tensor, distance):
    filler = jnp.zeros_like(tensor[:, :distance])
    return jnp.concatenate([filler, tensor[:, :-distance]], axis=1)

def attend_sequence(queries, key_rows, values, house_raw, beta_logits, segment_ids, group_starts):
    group_count = group_starts.shape[0]
    length = segment_ids.shape[0] // group_count
    head_count = beta_logits.shape[1]
    head_width = queries.shape[1] // head_count
    scaling = 1.0 / math.sqrt(head_width)

    def split_heads(tensor):
        return tensor.reshape(group_count, length, head_count, head_width).transpose(2, 0, 1, 3)
    beta_groups = beta_logits.reshape(group_count, length, head_count).transpose(2, 0, 1)
    scores_local, query_bar, key_bar, factors = local_map(split_heads(queries), split_heads(key_rows), split_heads(house_raw), beta_groups)
    key_send = low(key_bar)
    value_groups = split_heads(values)
    group_ids = (jnp.arange(group_count, dtype=jnp.int32) * length)[:, None]
    starts = doc_starts_local(segment_ids.reshape(group_count, length), group_starts[:, None], group_ids)
    offsets = jnp.arange(length, dtype=jnp.int32)
    local_mask = (offsets[None, :] <= offsets[:, None])[None] & (offsets[None, None, :] + group_ids[:, :, None] >= starts[:, :, None])
    score_list = [jnp.where(local_mask[None], scores_local, NEGATIVE)]
    value_list = [value_groups]
    carried = jnp.broadcast_to(jnp.eye(head_width, dtype=factors.dtype), factors.shape)
    for distance in range(1, group_count):
        if distance > 1:
            moved = jnp.einsum('hcab,hcbd->hcad', factors, carried, precision=HIGHEST)
            carried = shift_groups(moved, 1)
        query_rot = low(jnp.einsum('hcqa,hcab->hcqb', query_bar, carried, precision=HIGHEST))
        hop_keys = shift_groups(key_send, distance)
        cross = low_back(jnp.einsum('hcqd,hckd->hcqk', query_rot, hop_keys, precision=HIGHEST) * scaling)
        key_pos = group_ids - distance * length + offsets[None, :]
        hop_mask = key_pos[:, None, :] >= starts[:, :, None]
        score_list.append(jnp.where(hop_mask[None], cross, NEGATIVE))
        value_list.append(shift_groups(value_groups, distance))
    all_scores = jnp.concatenate(score_list, axis=-1)
    probs_low = low(jax.nn.softmax(all_scores, axis=-1))
    attn = jnp.zeros(value_groups.shape, dtype=value_groups.dtype)
    for distance in range(group_count):
        piece = probs_low[..., distance * length:(distance + 1) * length]
        attn = attn + jnp.einsum('hcqk,hckd->hcqd', piece, value_list[distance], precision=HIGHEST)
    return attn.transpose(1, 2, 0, 3).reshape(group_count * length, head_count * head_width)

def matmul(inputs, weight):
    return jnp.einsum('std,df->stf', inputs, weight, precision=HIGHEST)

def layer(hidden_in, norm1_gain, w_query, w_key, w_value, w_house, w_beta, w_out, norm2_gain, w_gate, w_up, w_down, segment_ids, doc_starts):
    normed_one = hidden_in * lax.rsqrt(lax.optimization_barrier(jnp.mean(hidden_in * hidden_in, axis=-1, keepdims=True)) + EPSILON)
    h_one = low(normed_one * norm1_gain)
    queries = low_back(matmul(h_one, w_query))
    key_rows = low_back(matmul(h_one, w_key))
    values = low(low_back(matmul(h_one, w_value)))
    house_raw = low_back(matmul(h_one, w_house))
    beta_logits = low_back(matmul(h_one, w_beta))
    attend = jax.checkpoint(attend_sequence)
    attn = lax.map(lambda bundle: attend(*bundle), (queries, key_rows, values, house_raw, beta_logits, segment_ids, doc_starts))
    attn_low = low(low_back(attn))
    middle = hidden_in + low_back(jnp.einsum('stf,df->std', attn_low, w_out, precision=HIGHEST))
    normed_two = middle * lax.rsqrt(lax.optimization_barrier(jnp.mean(middle * middle, axis=-1, keepdims=True)) + EPSILON)
    h_two = low(normed_two * norm2_gain)
    gate_proj = low_back(matmul(h_two, w_gate))
    up_proj = low_back(matmul(h_two, w_up))
    hidden = low(jax.nn.silu(gate_proj) * up_proj)
    return middle + low_back(jnp.einsum('stf,df->std', hidden, w_down, precision=HIGHEST))

def reference(hidden_in, segment_ids, doc_starts, norm1_gain, w_query, w_key, w_value, w_house, w_beta, w_out, norm2_gain, w_gate, w_up, w_down, output_grad):
    floats = [array_in.astype(jnp.float32) for array_in in (hidden_in, norm1_gain, w_query, w_key, w_value, w_house, w_beta, w_out, norm2_gain, w_gate, w_up, w_down)]

    def forward(*params):
        return layer(*params, segment_ids, doc_starts)
    block_out, pullback = jax.vjp(forward, *floats)
    grads = pullback(output_grad.astype(jnp.float32))
    return (block_out.astype(jnp.bfloat16), grads[0].astype(jnp.bfloat16), grads[1], grads[2], grads[3], grads[4], grads[5], grads[6], grads[7], grads[8], grads[9], grads[10], grads[11])
```

```python
import math

import jax
import jax.numpy as jnp
from jax import lax
from jax.sharding import PartitionSpec as P

EPSILON = 1e-06
HIGHEST = lax.Precision.HIGHEST
NEGATIVE = -1e30


def passed_along(block, axis, distance):
    devices = range(lax.axis_size(axis))
    route = [(i - distance, i) for i in devices if i - distance in devices]
    return lax.ppermute(block, axis, route)


def group_algebra(queries, key_rows, house, betas):
    length = queries.shape[0]
    scaling = 1.0 / math.sqrt(queries.shape[1])
    row_index = lax.broadcasted_iota(jnp.int32, (length, length), 0)
    column_index = lax.broadcasted_iota(jnp.int32, (length, length), 1)
    strict_below = row_index > column_index
    house_gram = jnp.dot(house, house.T, precision=HIGHEST)
    system = jnp.where(strict_below, house_gram, 0.0) + jnp.diag(1.0 / betas)
    identity = jnp.eye(length, dtype=house.dtype)
    inverse = jax.scipy.linalg.solve_triangular(system, identity, lower=True)
    query_house = jnp.where(
        row_index >= column_index, jnp.dot(queries, house.T, precision=HIGHEST), 0.0
    )
    house_key = jnp.where(strict_below, jnp.dot(house, key_rows.T, precision=HIGHEST), 0.0)
    query_side = jnp.dot(query_house, inverse, precision=HIGHEST)
    key_side = jnp.dot(inverse, house_key, precision=HIGHEST)
    scores = (
        jnp.dot(queries, key_rows.T, precision=HIGHEST)
        - jnp.dot(query_side, house_key, precision=HIGHEST)
    ) * scaling
    query_bar = queries - jnp.dot(query_side, house, precision=HIGHEST)
    key_bar = key_rows - jnp.dot(key_side.T, house, precision=HIGHEST)
    inner = jnp.dot(inverse, house, precision=HIGHEST)
    factor = jnp.eye(house.shape[1], dtype=house.dtype) - jnp.dot(house.T, inner, precision=HIGHEST)
    return (scores, query_bar, key_bar, factor)


def local_map(queries, key_rows, house_raw, beta_logits):
    house = house_raw * lax.rsqrt(jnp.sum(house_raw * house_raw, axis=-1, keepdims=True) + EPSILON)
    betas = 2.0 * jax.nn.sigmoid(beta_logits)
    return jax.vmap(jax.vmap(group_algebra))(queries, key_rows, house, betas)


def doc_starts_local(segment_ids, group_first, first_position):
    length = segment_ids.shape[-1]
    previous = jnp.concatenate([segment_ids[..., :1], segment_ids[..., :-1]], axis=-1)
    offsets = lax.broadcasted_iota(jnp.int32, segment_ids.shape, segment_ids.ndim - 1)
    boundary = (offsets > 0) & (segment_ids != previous)
    marks = jnp.where(boundary, offsets + first_position, -1)
    row_index = lax.broadcasted_iota(jnp.int32, (length, length), 0)
    column_index = lax.broadcasted_iota(jnp.int32, (length, length), 1)
    seen = jnp.where(column_index <= row_index, marks[..., None, :], -1)
    return jnp.maximum(jnp.max(seen, axis=-1), group_first)


def norm_rows(values):
    factor = lax.rsqrt(jnp.mean(values * values, axis=-1, keepdims=True) + EPSILON)
    return (values * factor, factor)


def norm_back(gradient, normed, factor, norm_gain):
    scaled = gradient * norm_gain
    return factor * (scaled - normed * jnp.mean(scaled * normed, axis=-1, keepdims=True))


def split_heads(tensor, head_count):
    seq_count, length, total_width = tensor.shape
    return tensor.reshape(seq_count, length, head_count, total_width // head_count).transpose(
        0, 2, 1, 3
    )


def join_heads(tensor):
    seq_count, head_count, length, head_width = tensor.shape
    return tensor.transpose(0, 2, 1, 3).reshape(seq_count, length, head_count * head_width)


def project(inputs, weight):
    return jnp.einsum("scd,df->scf", inputs, weight, preferred_element_type=jnp.float32)


def project_back(gradient, weight):
    return jnp.einsum("scf,df->scd", gradient, weight, preferred_element_type=jnp.float32)


def weight_grad(inputs, gradient):
    return jnp.einsum("scd,scf->df", inputs, gradient, preferred_element_type=jnp.float32)


def cross_scores(query_rot, key_low, scaling):
    return (
        jnp.einsum("shqd,shkd->shqk", query_rot, key_low, preferred_element_type=jnp.float32)
        * scaling
    )


def weighted_values(weights, values_in):
    return jnp.einsum("shqk,shkd->shqd", weights, values_in, preferred_element_type=jnp.float32)


def shards(
    hidden_in,
    segment_ids,
    doc_starts,
    norm1_gain,
    w_query,
    w_key,
    w_value,
    w_house,
    w_beta,
    w_out,
    norm2_gain,
    w_gate,
    w_up,
    w_down,
    output_grad,
):
    gathered = (
        lax.all_gather(norm1_gain, ("fsdp", "ctx"), axis=0, tiled=True),
        lax.all_gather(w_query, ("fsdp", "ctx"), axis=0, tiled=True),
        lax.all_gather(w_key, ("fsdp", "ctx"), axis=0, tiled=True),
        lax.all_gather(w_value, ("fsdp", "ctx"), axis=0, tiled=True),
        lax.all_gather(w_house, ("fsdp", "ctx"), axis=0, tiled=True),
        lax.all_gather(w_beta, ("fsdp", "ctx"), axis=0, tiled=True),
        lax.all_gather(w_out, ("fsdp", "ctx"), axis=0, tiled=True),
        lax.all_gather(norm2_gain, ("fsdp", "ctx"), axis=0, tiled=True),
        lax.all_gather(w_gate, ("fsdp", "ctx"), axis=0, tiled=True),
        lax.all_gather(w_up, ("fsdp", "ctx"), axis=0, tiled=True),
        lax.all_gather(w_down, ("fsdp", "ctx"), axis=0, tiled=True),
    )
    (
        gain_one,
        query_full,
        key_full,
        value_full,
        house_full,
        beta_full,
        out_full,
        gain_two,
        gate_full,
        up_full,
        down_full,
    ) = gathered
    gain_one_f = gain_one.astype(jnp.float32)
    gain_two_f = gain_two.astype(jnp.float32)
    head_count = beta_full.shape[1]
    length = hidden_in.shape[1]
    residual = hidden_in.astype(jnp.float32)
    normed_one, factor_one = norm_rows(residual)
    h_one = (normed_one * gain_one_f).astype(jnp.bfloat16)
    queries = split_heads(project(h_one, query_full), head_count)
    key_rows = split_heads(project(h_one, key_full), head_count)
    values_low = split_heads(project(h_one, value_full).astype(jnp.bfloat16), head_count)
    house_raw = split_heads(project(h_one, house_full), head_count)
    beta_logits = project(h_one, beta_full).transpose(0, 2, 1)
    (scores_local, query_bar, key_bar, factors), local_back = jax.vjp(
        local_map, queries, key_rows, house_raw, beta_logits
    )
    scaling = 1.0 / math.sqrt(queries.shape[-1])
    chain_index = lax.axis_index("ctx")
    hop_total = lax.axis_size("ctx") - 1
    first_position = chain_index * length
    starts = doc_starts_local(segment_ids, doc_starts, first_position)
    offsets = jnp.arange(length, dtype=jnp.int32)
    causal = (offsets[None, :] <= offsets[:, None])[None]
    local_mask = (causal & (offsets[None, None, :] + first_position >= starts[:, :, None]))[:, None]

    def hop_mask(distance):
        key_pos = (chain_index - distance) * length + offsets
        return (key_pos[None, None, :] >= starts[:, :, None])[:, None]

    masked_local = jnp.where(local_mask, scores_local, NEGATIVE)
    local_max = jnp.max(masked_local, axis=-1)
    local_sum = jnp.sum(jnp.exp(masked_local - local_max[..., None]), axis=-1)
    key_send = key_bar.astype(jnp.bfloat16)
    identity = jnp.broadcast_to(jnp.eye(factors.shape[-1], dtype=jnp.float32), factors.shape)
    stack_rot = jnp.zeros((hop_total,) + query_bar.shape, jnp.bfloat16)
    stack_factors = jnp.zeros((hop_total,) + factors.shape, jnp.float32)

    def rotate(hop_step, hop_keys, chain, run_max, run_sum):
        query_rot = jnp.einsum("shqa,shab->shqb", query_bar, chain, precision=HIGHEST).astype(
            jnp.bfloat16
        )
        masked = jnp.where(
            hop_mask(hop_step + 1), cross_scores(query_rot, hop_keys, scaling), NEGATIVE
        )
        new_max = jnp.maximum(run_max, jnp.max(masked, axis=-1))
        new_sum = run_sum * jnp.exp(run_max - new_max) + jnp.sum(
            jnp.exp(masked - new_max[..., None]), axis=-1
        )
        return (query_rot, new_max, new_sum)

    stack_keys = jnp.zeros((hop_total,) + key_send.shape, jnp.bfloat16)
    stack_values = jnp.zeros((hop_total,) + values_low.shape, jnp.bfloat16)

    def forward_hop(hop_step, loop_state):
        (
            send_keys,
            send_values,
            send_factor,
            kept_keys,
            kept_values,
            kept_rot,
            kept_factors,
            run_max,
            run_sum,
        ) = loop_state
        got_keys, got_values = passed_along((send_keys, send_values), "ctx", 1)
        got_factor = passed_along(send_factor.astype(jnp.bfloat16), "ctx", 1).astype(
            send_factor.dtype
        )
        query_rot, run_max, run_sum = rotate(hop_step, got_keys, got_factor, run_max, run_sum)
        kept_keys = lax.dynamic_update_index_in_dim(kept_keys, got_keys, hop_step, 0)
        kept_values = lax.dynamic_update_index_in_dim(kept_values, got_values, hop_step, 0)
        kept_rot = lax.dynamic_update_index_in_dim(kept_rot, query_rot, hop_step, 0)
        kept_factors = lax.dynamic_update_index_in_dim(kept_factors, got_factor, hop_step, 0)
        next_factor = jnp.einsum("shab,shbc->shac", factors, got_factor, precision=HIGHEST)
        return (
            got_keys,
            got_values,
            next_factor,
            kept_keys,
            kept_values,
            kept_rot,
            kept_factors,
            run_max,
            run_sum,
        )

    loop_state = lax.fori_loop(
        0,
        hop_total,
        forward_hop,
        (
            key_send,
            values_low,
            identity,
            stack_keys,
            stack_values,
            stack_rot,
            stack_factors,
            local_max,
            local_sum,
        ),
    )
    stack_keys, stack_values, stack_rot, stack_factors = (
        loop_state[3],
        loop_state[4],
        loop_state[5],
        loop_state[6],
    )
    run_max, run_sum = (loop_state[7], loop_state[8])

    def fetch(hop_step):
        return (
            lax.dynamic_index_in_dim(stack_keys, hop_step, 0, keepdims=False),
            lax.dynamic_index_in_dim(stack_values, hop_step, 0, keepdims=False),
        )

    log_total = run_max + jnp.log(run_sum)

    def recall(hop_step):
        hop_keys, hop_values = fetch(hop_step)
        hop_factor = lax.dynamic_index_in_dim(stack_factors, hop_step, 0, keepdims=False)
        query_rot = lax.dynamic_index_in_dim(stack_rot, hop_step, 0, keepdims=False)
        masked = jnp.where(
            hop_mask(hop_step + 1), cross_scores(query_rot, hop_keys, scaling), NEGATIVE
        )
        hop_probs = jnp.exp(masked - log_total[..., None])
        return (hop_keys, hop_values, hop_factor, query_rot, hop_probs)

    probs_local = jnp.exp(masked_local - log_total[..., None])
    probs_local_low = probs_local.astype(jnp.bfloat16)
    attn_acc = weighted_values(probs_local_low, values_low)
    attn_rest = weighted_values(
        (probs_local - probs_local_low.astype(jnp.float32)).astype(jnp.bfloat16), values_low
    )

    def value_hop(hop_step, running):
        total_low, total_rest = running
        hop_keys, hop_values, hop_factor, query_rot, hop_probs = recall(hop_step)
        hop_low = hop_probs.astype(jnp.bfloat16)
        total_low = total_low + weighted_values(hop_low, hop_values)
        total_rest = total_rest + weighted_values(
            (hop_probs - hop_low.astype(jnp.float32)).astype(jnp.bfloat16), hop_values
        )
        return (total_low, total_rest)

    attn_acc, attn_rest = lax.fori_loop(0, hop_total, value_hop, (attn_acc, attn_rest))
    attn_low = join_heads(attn_acc.astype(jnp.bfloat16))
    branch = lax.psum(project_back(attn_low, out_full), "tp")
    middle = residual + branch
    normed_two, factor_two = norm_rows(middle)
    h_two = (normed_two * gain_two_f).astype(jnp.bfloat16)
    gate_proj = project(h_two, gate_full)
    up_proj = project(h_two, up_full)
    gate_sigmoid = jax.nn.sigmoid(gate_proj)
    silu_gate = gate_proj * gate_sigmoid
    hidden_low = (silu_gate * up_proj).astype(jnp.bfloat16)
    mlp_out = lax.psum(project_back(hidden_low, down_full).astype(jnp.bfloat16), "tp").astype(
        jnp.float32
    )
    block_out = (middle + mlp_out).astype(jnp.bfloat16)
    down_grad = weight_grad(output_grad, hidden_low)
    d_hidden = project(output_grad, down_full)
    d_gate = (d_hidden * up_proj * gate_sigmoid * (1.0 + gate_proj * (1.0 - gate_sigmoid))).astype(
        jnp.bfloat16
    )
    d_up = (d_hidden * silu_gate).astype(jnp.bfloat16)
    gate_grad = weight_grad(h_two, d_gate)
    up_grad = weight_grad(h_two, d_up)
    d_two = lax.psum(project_back(d_gate, gate_full) + project_back(d_up, up_full), "tp")
    gain_two_grad = jnp.sum(d_two * normed_two, axis=(0, 1))
    d_middle = output_grad.astype(jnp.float32) + norm_back(
        d_two, normed_two, factor_two, gain_two_f
    )
    d_branch = d_middle.astype(jnp.bfloat16)
    out_grad = weight_grad(d_branch, attn_low)
    d_attn = split_heads(project(d_branch, out_full).astype(jnp.bfloat16), head_count)
    d_probs_local = jnp.einsum(
        "shqd,shkd->shqk", d_attn, values_low, preferred_element_type=jnp.float32
    )
    row_delta = jnp.sum(d_attn.astype(jnp.float32) * (attn_acc + attn_rest), axis=-1)
    zero_factor = jnp.zeros(factors.shape, jnp.float32)
    zero_bar = jnp.zeros(query_bar.shape, jnp.float32)

    def back_hop(back_step, loop_state):
        carry_keys, carry_values, carry_factor, d_bar, d_factors = loop_state
        hop_step = hop_total - 1 - back_step
        hop_keys, hop_values, hop_factor, query_rot, hop_probs = recall(hop_step)
        d_probs = jnp.einsum(
            "shqd,shkd->shqk", d_attn, hop_values, preferred_element_type=jnp.float32
        )
        d_cross = (hop_probs * (d_probs - row_delta[..., None])).astype(jnp.bfloat16)
        d_rot = (
            jnp.einsum("shqk,shkd->shqd", d_cross, hop_keys, preferred_element_type=jnp.float32)
            * scaling
        )
        d_bar = d_bar + jnp.einsum("shqb,shab->shqa", d_rot, hop_factor, precision=HIGHEST)
        factor_local = jnp.einsum("shqa,shqb->shab", query_bar, d_rot, precision=HIGHEST)
        keys_total = (
            carry_keys
            + jnp.einsum("shqk,shqd->shkd", d_cross, query_rot, preferred_element_type=jnp.float32)
            * scaling
        )
        values_total = carry_values + jnp.einsum(
            "shqk,shqd->shkd",
            hop_probs.astype(jnp.bfloat16),
            d_attn,
            preferred_element_type=jnp.float32,
        )
        factor_total = factor_local + jnp.einsum(
            "shba,shbc->shac", factors, carry_factor, precision=HIGHEST
        )
        d_factors = d_factors + jnp.einsum(
            "shac,shbc->shab", carry_factor, hop_factor, precision=HIGHEST
        )
        carry_keys, carry_values, carry_factor = (
            passed_along(keys_total.astype(jnp.bfloat16), "ctx", -1).astype(keys_total.dtype),
            passed_along(values_total.astype(jnp.bfloat16), "ctx", -1).astype(values_total.dtype),
            passed_along(factor_total.astype(jnp.bfloat16), "ctx", -1).astype(factor_total.dtype),
        )
        return (carry_keys, carry_values, carry_factor, d_bar, d_factors)

    zero_rows = jnp.zeros(key_send.shape, jnp.float32)
    loop_state = lax.fori_loop(
        0, hop_total, back_hop, (zero_rows, zero_rows, zero_factor, zero_bar, zero_factor)
    )
    carry_keys, carry_values, d_bar, d_factors = (
        loop_state[0],
        loop_state[1],
        loop_state[3],
        loop_state[4],
    )
    d_local = probs_local * (d_probs_local - row_delta[..., None])
    values_sum = carry_values + jnp.einsum(
        "shqk,shqd->shkd", probs_local_low, d_attn, preferred_element_type=jnp.float32
    )
    d_queries, d_keys, d_house, d_betas = local_back((d_local, d_bar, carry_keys, d_factors))
    query_low = join_heads(d_queries.astype(jnp.bfloat16))
    key_low = join_heads(d_keys.astype(jnp.bfloat16))
    value_low = join_heads(values_sum.astype(jnp.bfloat16))
    house_low = join_heads(d_house.astype(jnp.bfloat16))
    beta_low = d_betas.transpose(0, 2, 1).astype(jnp.bfloat16)
    query_grad = weight_grad(h_one, query_low)
    key_grad = weight_grad(h_one, key_low)
    value_grad = weight_grad(h_one, value_low)
    house_grad = weight_grad(h_one, house_low)
    beta_grad = weight_grad(h_one, beta_low)
    partial_one = (
        project_back(query_low, query_full)
        + project_back(key_low, key_full)
        + project_back(value_low, value_full)
    )
    partial_one = (
        partial_one + project_back(house_low, house_full) + project_back(beta_low, beta_full)
    )
    d_one = lax.psum(partial_one.astype(jnp.bfloat16), "tp").astype(jnp.float32)
    gain_one_grad = jnp.sum(d_one * normed_one, axis=(0, 1))
    input_grad = (d_middle + norm_back(d_one, normed_one, factor_one, gain_one_f)).astype(
        jnp.bfloat16
    )

    def scattered(partial):
        first = lax.psum_scatter(partial, "fsdp", scatter_dimension=0, tiled=True)
        return lax.psum_scatter(first, "ctx", scatter_dimension=0, tiled=True)

    results = tuple(
        (
            scattered(gain_one_grad.astype(jnp.bfloat16)).astype(jnp.float32),
            scattered(query_grad.astype(jnp.bfloat16)).astype(jnp.float32),
            scattered(key_grad.astype(jnp.bfloat16)).astype(jnp.float32),
            scattered(value_grad.astype(jnp.bfloat16)).astype(jnp.float32),
            scattered(house_grad.astype(jnp.bfloat16)).astype(jnp.float32),
            scattered(beta_grad.astype(jnp.bfloat16)).astype(jnp.float32),
            scattered(out_grad.astype(jnp.bfloat16)).astype(jnp.float32),
            scattered(gain_two_grad.astype(jnp.bfloat16)).astype(jnp.float32),
            scattered(gate_grad.astype(jnp.bfloat16)).astype(jnp.float32),
            scattered(up_grad.astype(jnp.bfloat16)).astype(jnp.float32),
            scattered(down_grad.astype(jnp.bfloat16)).astype(jnp.float32),
        )
    )
    return (block_out, input_grad) + results


def solution(mesh):
    in_specs = (
        P("fsdp", "ctx", None),
        P("fsdp", "ctx"),
        P("fsdp", "ctx"),
        P(("fsdp", "ctx")),
        P(("fsdp", "ctx"), "tp"),
        P(("fsdp", "ctx"), "tp"),
        P(("fsdp", "ctx"), "tp"),
        P(("fsdp", "ctx"), "tp"),
        P(("fsdp", "ctx"), "tp"),
        P(("fsdp", "ctx"), "tp"),
        P(("fsdp", "ctx")),
        P(("fsdp", "ctx"), "tp"),
        P(("fsdp", "ctx"), "tp"),
        P(("fsdp", "ctx"), "tp"),
        P("fsdp", "ctx", None),
    )
    out_specs = (
        P("fsdp", "ctx", None),
        P("fsdp", "ctx", None),
        P(("fsdp", "ctx")),
        P(("fsdp", "ctx"), "tp"),
        P(("fsdp", "ctx"), "tp"),
        P(("fsdp", "ctx"), "tp"),
        P(("fsdp", "ctx"), "tp"),
        P(("fsdp", "ctx"), "tp"),
        P(("fsdp", "ctx"), "tp"),
        P(("fsdp", "ctx")),
        P(("fsdp", "ctx"), "tp"),
        P(("fsdp", "ctx"), "tp"),
        P(("fsdp", "ctx"), "tp"),
    )
    return jax.shard_map(shards, mesh=mesh, in_specs=in_specs, out_specs=out_specs, check_vma=False)
```

```python
import functools
import math

import jax
import jax.numpy as jnp
from jax import lax
from jax.experimental import pallas as pl
from jax.experimental.pallas import tpu as pltpu
from jax.sharding import PartitionSpec as P

EPSILON = 1e-06
HIGHEST = lax.Precision.HIGHEST
NEGATIVE = -1e30


def passed_along(block, axis, distance):
    devices = range(lax.axis_size(axis))
    route = [(i - distance, i) for i in devices if i - distance in devices]
    return lax.ppermute(block, axis, route)


def group_algebra(queries, key_rows, house, betas):
    length = queries.shape[0]
    scaling = 1.0 / math.sqrt(queries.shape[1])
    row_index = lax.broadcasted_iota(jnp.int32, (length, length), 0)
    column_index = lax.broadcasted_iota(jnp.int32, (length, length), 1)
    strict_below = row_index > column_index
    house_gram = jnp.dot(house, house.T, precision=HIGHEST)
    system = jnp.where(strict_below, house_gram, 0.0) + jnp.diag(1.0 / betas)
    identity = jnp.eye(length, dtype=house.dtype)
    inverse = jax.scipy.linalg.solve_triangular(system, identity, lower=True)
    query_house = jnp.where(
        row_index >= column_index, jnp.dot(queries, house.T, precision=HIGHEST), 0.0
    )
    house_key = jnp.where(strict_below, jnp.dot(house, key_rows.T, precision=HIGHEST), 0.0)
    query_side = jnp.dot(query_house, inverse, precision=HIGHEST)
    key_side = jnp.dot(inverse, house_key, precision=HIGHEST)
    scores = (
        jnp.dot(queries, key_rows.T, precision=HIGHEST)
        - jnp.dot(query_side, house_key, precision=HIGHEST)
    ) * scaling
    query_bar = queries - jnp.dot(query_side, house, precision=HIGHEST)
    key_bar = key_rows - jnp.dot(key_side.T, house, precision=HIGHEST)
    inner = jnp.dot(inverse, house, precision=HIGHEST)
    factor = jnp.eye(house.shape[1], dtype=house.dtype) - jnp.dot(house.T, inner, precision=HIGHEST)
    return (scores, query_bar, key_bar, factor)


def local_map(queries, key_rows, house_raw, beta_logits):
    house = house_raw * lax.rsqrt(jnp.sum(house_raw * house_raw, axis=-1, keepdims=True) + EPSILON)
    betas = 2.0 * jax.nn.sigmoid(beta_logits)
    return jax.vmap(jax.vmap(group_algebra))(queries, key_rows, house, betas)


def doc_starts_local(segment_ids, group_first, first_position):
    length = segment_ids.shape[-1]
    previous = jnp.concatenate([segment_ids[..., :1], segment_ids[..., :-1]], axis=-1)
    offsets = lax.broadcasted_iota(jnp.int32, segment_ids.shape, segment_ids.ndim - 1)
    boundary = (offsets > 0) & (segment_ids != previous)
    marks = jnp.where(boundary, offsets + first_position, -1)
    row_index = lax.broadcasted_iota(jnp.int32, (length, length), 0)
    column_index = lax.broadcasted_iota(jnp.int32, (length, length), 1)
    seen = jnp.where(column_index <= row_index, marks[..., None, :], -1)
    return jnp.maximum(jnp.max(seen, axis=-1), group_first)


def norm_rows(values):
    factor = lax.rsqrt(jnp.mean(values * values, axis=-1, keepdims=True) + EPSILON)
    return (values * factor, factor)


def norm_back(gradient, normed, factor, norm_gain):
    scaled = gradient * norm_gain
    return factor * (scaled - normed * jnp.mean(scaled * normed, axis=-1, keepdims=True))


def split_heads(tensor, head_count):
    seq_count, length, total_width = tensor.shape
    return tensor.reshape(seq_count, length, head_count, total_width // head_count).transpose(
        0, 2, 1, 3
    )


def join_heads(tensor):
    seq_count, head_count, length, head_width = tensor.shape
    return tensor.transpose(0, 2, 1, 3).reshape(seq_count, length, head_count * head_width)


def project(inputs, weight):
    return jnp.einsum("scd,df->scf", inputs, weight, preferred_element_type=jnp.float32)


def project_back(gradient, weight):
    return jnp.einsum("scf,df->scd", gradient, weight, preferred_element_type=jnp.float32)


def weight_grad(inputs, gradient):
    return jnp.einsum("scd,scf->df", inputs, gradient, preferred_element_type=jnp.float32)


def cross_scores(query_rot, key_low, scaling):
    return (
        jnp.einsum("shqd,shkd->shqk", query_rot, key_low, preferred_element_type=jnp.float32)
        * scaling
    )


def weighted_values(weights, values_in):
    return jnp.einsum("shqk,shkd->shqd", weights, values_in, preferred_element_type=jnp.float32)


def ring_of_groups(
    hidden_in,
    segment_ids,
    doc_starts,
    norm1_gain,
    w_query,
    w_key,
    w_value,
    w_house,
    w_beta,
    w_out,
    norm2_gain,
    w_gate,
    w_up,
    w_down,
    output_grad,
):
    gathered = (
        lax.all_gather(norm1_gain, ("fsdp", "ctx"), axis=0, tiled=True),
        lax.all_gather(w_query, ("fsdp", "ctx"), axis=0, tiled=True),
        lax.all_gather(w_key, ("fsdp", "ctx"), axis=0, tiled=True),
        lax.all_gather(w_value, ("fsdp", "ctx"), axis=0, tiled=True),
        lax.all_gather(w_house, ("fsdp", "ctx"), axis=0, tiled=True),
        lax.all_gather(w_beta, ("fsdp", "ctx"), axis=0, tiled=True),
        lax.all_gather(w_out, ("fsdp", "ctx"), axis=0, tiled=True),
        lax.all_gather(norm2_gain, ("fsdp", "ctx"), axis=0, tiled=True),
        lax.all_gather(w_gate, ("fsdp", "ctx"), axis=0, tiled=True),
        lax.all_gather(w_up, ("fsdp", "ctx"), axis=0, tiled=True),
        lax.all_gather(w_down, ("fsdp", "ctx"), axis=0, tiled=True),
    )
    (
        gain_one,
        query_full,
        key_full,
        value_full,
        house_full,
        beta_full,
        out_full,
        gain_two,
        gate_full,
        up_full,
        down_full,
    ) = gathered
    gain_one_f = gain_one.astype(jnp.float32)
    gain_two_f = gain_two.astype(jnp.float32)
    head_count = beta_full.shape[1]
    length = hidden_in.shape[1]
    residual = hidden_in.astype(jnp.float32)
    normed_one, factor_one = norm_rows(residual)
    h_one = (normed_one * gain_one_f).astype(jnp.bfloat16)
    queries = split_heads(project(h_one, query_full), head_count)
    key_rows = split_heads(project(h_one, key_full), head_count)
    values_low = split_heads(project(h_one, value_full).astype(jnp.bfloat16), head_count)
    house_raw = split_heads(project(h_one, house_full), head_count)
    beta_logits = project(h_one, beta_full).transpose(0, 2, 1)
    (scores_local, query_bar, key_bar, factors), local_back = jax.vjp(
        local_map, queries, key_rows, house_raw, beta_logits
    )
    scaling = 1.0 / math.sqrt(queries.shape[-1])
    chain_index = lax.axis_index("ctx")
    hop_total = lax.axis_size("ctx") - 1
    first_position = chain_index * length
    starts = doc_starts_local(segment_ids, doc_starts, first_position)
    offsets = jnp.arange(length, dtype=jnp.int32)
    causal = (offsets[None, :] <= offsets[:, None])[None]
    local_mask = (causal & (offsets[None, None, :] + first_position >= starts[:, :, None]))[:, None]

    def hop_mask(distance):
        key_pos = (chain_index - distance) * length + offsets
        return (key_pos[None, None, :] >= starts[:, :, None])[:, None]

    masked_local = jnp.where(local_mask, scores_local, NEGATIVE)
    local_max = jnp.max(masked_local, axis=-1)
    local_sum = jnp.sum(jnp.exp(masked_local - local_max[..., None]), axis=-1)
    key_send = key_bar.astype(jnp.bfloat16)
    identity = jnp.broadcast_to(jnp.eye(factors.shape[-1], dtype=jnp.float32), factors.shape)
    stack_rot = jnp.zeros((hop_total,) + query_bar.shape, jnp.bfloat16)
    stack_factors = jnp.zeros((hop_total,) + factors.shape, jnp.float32)

    def rotate(hop_step, hop_keys, chain, run_max, run_sum):
        query_rot = jnp.einsum("shqa,shab->shqb", query_bar, chain, precision=HIGHEST).astype(
            jnp.bfloat16
        )
        masked = jnp.where(
            hop_mask(hop_step + 1), cross_scores(query_rot, hop_keys, scaling), NEGATIVE
        )
        new_max = jnp.maximum(run_max, jnp.max(masked, axis=-1))
        new_sum = run_sum * jnp.exp(run_max - new_max) + jnp.sum(
            jnp.exp(masked - new_max[..., None]), axis=-1
        )
        return (query_rot, new_max, new_sum)

    stack_keys = jnp.zeros((hop_total,) + key_send.shape, jnp.bfloat16)
    stack_values = jnp.zeros((hop_total,) + values_low.shape, jnp.bfloat16)

    def forward_hop(hop_step, loop_state):
        (
            send_keys,
            send_values,
            send_factor,
            kept_keys,
            kept_values,
            kept_rot,
            kept_factors,
            run_max,
            run_sum,
        ) = loop_state
        got_keys, got_values = passed_along((send_keys, send_values), "ctx", 1)
        got_factor = passed_along(send_factor.astype(jnp.bfloat16), "ctx", 1).astype(
            send_factor.dtype
        )
        query_rot, run_max, run_sum = rotate(hop_step, got_keys, got_factor, run_max, run_sum)
        kept_keys = lax.dynamic_update_index_in_dim(kept_keys, got_keys, hop_step, 0)
        kept_values = lax.dynamic_update_index_in_dim(kept_values, got_values, hop_step, 0)
        kept_rot = lax.dynamic_update_index_in_dim(kept_rot, query_rot, hop_step, 0)
        kept_factors = lax.dynamic_update_index_in_dim(kept_factors, got_factor, hop_step, 0)
        next_factor = jnp.einsum("shab,shbc->shac", factors, got_factor, precision=HIGHEST)
        return (
            got_keys,
            got_values,
            next_factor,
            kept_keys,
            kept_values,
            kept_rot,
            kept_factors,
            run_max,
            run_sum,
        )

    loop_state = lax.fori_loop(
        0,
        hop_total,
        forward_hop,
        (
            key_send,
            values_low,
            identity,
            stack_keys,
            stack_values,
            stack_rot,
            stack_factors,
            local_max,
            local_sum,
        ),
    )
    stack_keys, stack_values, stack_rot, stack_factors = (
        loop_state[3],
        loop_state[4],
        loop_state[5],
        loop_state[6],
    )
    run_max, run_sum = (loop_state[7], loop_state[8])

    def fetch(hop_step):
        return (
            lax.dynamic_index_in_dim(stack_keys, hop_step, 0, keepdims=False),
            lax.dynamic_index_in_dim(stack_values, hop_step, 0, keepdims=False),
        )

    log_total = run_max + jnp.log(run_sum)

    def recall(hop_step):
        hop_keys, hop_values = fetch(hop_step)
        hop_factor = lax.dynamic_index_in_dim(stack_factors, hop_step, 0, keepdims=False)
        query_rot = lax.dynamic_index_in_dim(stack_rot, hop_step, 0, keepdims=False)
        masked = jnp.where(
            hop_mask(hop_step + 1), cross_scores(query_rot, hop_keys, scaling), NEGATIVE
        )
        hop_probs = jnp.exp(masked - log_total[..., None])
        return (hop_keys, hop_values, hop_factor, query_rot, hop_probs)

    probs_local = jnp.exp(masked_local - log_total[..., None])
    probs_local_low = probs_local.astype(jnp.bfloat16)
    attn_acc = weighted_values(probs_local_low, values_low)
    attn_rest = weighted_values(
        (probs_local - probs_local_low.astype(jnp.float32)).astype(jnp.bfloat16), values_low
    )

    def value_hop(hop_step, running):
        total_low, total_rest = running
        hop_keys, hop_values, hop_factor, query_rot, hop_probs = recall(hop_step)
        hop_low = hop_probs.astype(jnp.bfloat16)
        total_low = total_low + weighted_values(hop_low, hop_values)
        total_rest = total_rest + weighted_values(
            (hop_probs - hop_low.astype(jnp.float32)).astype(jnp.bfloat16), hop_values
        )
        return (total_low, total_rest)

    attn_acc, attn_rest = lax.fori_loop(0, hop_total, value_hop, (attn_acc, attn_rest))
    attn_low = join_heads(attn_acc.astype(jnp.bfloat16))
    branch = lax.psum(project_back(attn_low, out_full), "tp")
    middle = residual + branch
    normed_two, factor_two = norm_rows(middle)
    h_two = (normed_two * gain_two_f).astype(jnp.bfloat16)
    gate_proj = project(h_two, gate_full)
    up_proj = project(h_two, up_full)
    gate_sigmoid = jax.nn.sigmoid(gate_proj)
    silu_gate = gate_proj * gate_sigmoid
    hidden_low = (silu_gate * up_proj).astype(jnp.bfloat16)
    mlp_out = lax.psum(project_back(hidden_low, down_full).astype(jnp.bfloat16), "tp").astype(
        jnp.float32
    )
    block_out = (middle + mlp_out).astype(jnp.bfloat16)
    down_grad = weight_grad(output_grad, hidden_low)
    d_hidden = project(output_grad, down_full)
    d_gate = (d_hidden * up_proj * gate_sigmoid * (1.0 + gate_proj * (1.0 - gate_sigmoid))).astype(
        jnp.bfloat16
    )
    d_up = (d_hidden * silu_gate).astype(jnp.bfloat16)
    gate_grad = weight_grad(h_two, d_gate)
    up_grad = weight_grad(h_two, d_up)
    d_two = lax.psum(project_back(d_gate, gate_full) + project_back(d_up, up_full), "tp")
    gain_two_grad = jnp.sum(d_two * normed_two, axis=(0, 1))
    d_middle = output_grad.astype(jnp.float32) + norm_back(
        d_two, normed_two, factor_two, gain_two_f
    )
    d_branch = d_middle.astype(jnp.bfloat16)
    out_grad = weight_grad(d_branch, attn_low)
    d_attn = split_heads(project(d_branch, out_full).astype(jnp.bfloat16), head_count)
    d_probs_local = jnp.einsum(
        "shqd,shkd->shqk", d_attn, values_low, preferred_element_type=jnp.float32
    )
    row_delta = jnp.sum(d_attn.astype(jnp.float32) * (attn_acc + attn_rest), axis=-1)
    zero_factor = jnp.zeros(factors.shape, jnp.float32)
    zero_bar = jnp.zeros(query_bar.shape, jnp.float32)

    def back_hop(back_step, loop_state):
        carry_keys, carry_values, carry_factor, d_bar, d_factors = loop_state
        hop_step = hop_total - 1 - back_step
        hop_keys, hop_values, hop_factor, query_rot, hop_probs = recall(hop_step)
        d_probs = jnp.einsum(
            "shqd,shkd->shqk", d_attn, hop_values, preferred_element_type=jnp.float32
        )
        d_cross = (hop_probs * (d_probs - row_delta[..., None])).astype(jnp.bfloat16)
        d_rot = (
            jnp.einsum("shqk,shkd->shqd", d_cross, hop_keys, preferred_element_type=jnp.float32)
            * scaling
        )
        d_bar = d_bar + jnp.einsum("shqb,shab->shqa", d_rot, hop_factor, precision=HIGHEST)
        factor_local = jnp.einsum("shqa,shqb->shab", query_bar, d_rot, precision=HIGHEST)
        keys_total = (
            carry_keys
            + jnp.einsum("shqk,shqd->shkd", d_cross, query_rot, preferred_element_type=jnp.float32)
            * scaling
        )
        values_total = carry_values + jnp.einsum(
            "shqk,shqd->shkd",
            hop_probs.astype(jnp.bfloat16),
            d_attn,
            preferred_element_type=jnp.float32,
        )
        factor_total = factor_local + jnp.einsum(
            "shba,shbc->shac", factors, carry_factor, precision=HIGHEST
        )
        d_factors = d_factors + jnp.einsum(
            "shac,shbc->shab", carry_factor, hop_factor, precision=HIGHEST
        )
        carry_keys, carry_values, carry_factor = (
            passed_along(keys_total.astype(jnp.bfloat16), "ctx", -1).astype(keys_total.dtype),
            passed_along(values_total.astype(jnp.bfloat16), "ctx", -1).astype(values_total.dtype),
            passed_along(factor_total.astype(jnp.bfloat16), "ctx", -1).astype(factor_total.dtype),
        )
        return (carry_keys, carry_values, carry_factor, d_bar, d_factors)

    zero_rows = jnp.zeros(key_send.shape, jnp.float32)
    loop_state = lax.fori_loop(
        0, hop_total, back_hop, (zero_rows, zero_rows, zero_factor, zero_bar, zero_factor)
    )
    carry_keys, carry_values, d_bar, d_factors = (
        loop_state[0],
        loop_state[1],
        loop_state[3],
        loop_state[4],
    )
    d_local = probs_local * (d_probs_local - row_delta[..., None])
    values_sum = carry_values + jnp.einsum(
        "shqk,shqd->shkd", probs_local_low, d_attn, preferred_element_type=jnp.float32
    )
    d_queries, d_keys, d_house, d_betas = local_back((d_local, d_bar, carry_keys, d_factors))
    query_low = join_heads(d_queries.astype(jnp.bfloat16))
    key_low = join_heads(d_keys.astype(jnp.bfloat16))
    value_low = join_heads(values_sum.astype(jnp.bfloat16))
    house_low = join_heads(d_house.astype(jnp.bfloat16))
    beta_low = d_betas.transpose(0, 2, 1).astype(jnp.bfloat16)
    query_grad = weight_grad(h_one, query_low)
    key_grad = weight_grad(h_one, key_low)
    value_grad = weight_grad(h_one, value_low)
    house_grad = weight_grad(h_one, house_low)
    beta_grad = weight_grad(h_one, beta_low)
    partial_one = (
        project_back(query_low, query_full)
        + project_back(key_low, key_full)
        + project_back(value_low, value_full)
    )
    partial_one = (
        partial_one + project_back(house_low, house_full) + project_back(beta_low, beta_full)
    )
    d_one = lax.psum(partial_one.astype(jnp.bfloat16), "tp").astype(jnp.float32)
    gain_one_grad = jnp.sum(d_one * normed_one, axis=(0, 1))
    input_grad = (d_middle + norm_back(d_one, normed_one, factor_one, gain_one_f)).astype(
        jnp.bfloat16
    )

    def scattered(partial):
        first = lax.psum_scatter(partial, "fsdp", scatter_dimension=0, tiled=True)
        return lax.psum_scatter(first, "ctx", scatter_dimension=0, tiled=True)

    results = tuple(
        (
            scattered(gain_one_grad.astype(jnp.bfloat16)).astype(jnp.float32),
            scattered(query_grad.astype(jnp.bfloat16)).astype(jnp.float32),
            scattered(key_grad.astype(jnp.bfloat16)).astype(jnp.float32),
            scattered(value_grad.astype(jnp.bfloat16)).astype(jnp.float32),
            scattered(house_grad.astype(jnp.bfloat16)).astype(jnp.float32),
            scattered(beta_grad.astype(jnp.bfloat16)).astype(jnp.float32),
            scattered(out_grad.astype(jnp.bfloat16)).astype(jnp.float32),
            scattered(gain_two_grad.astype(jnp.bfloat16)).astype(jnp.float32),
            scattered(gate_grad.astype(jnp.bfloat16)).astype(jnp.float32),
            scattered(up_grad.astype(jnp.bfloat16)).astype(jnp.float32),
            scattered(down_grad.astype(jnp.bfloat16)).astype(jnp.float32),
        )
    )
    return (block_out, input_grad) + results


def halves(value):
    high = value.astype(jnp.bfloat16)
    return high, (value - high.astype(jnp.float32)).astype(jnp.bfloat16)


AB = (((1,), (0,)), ((), ()))
ABT = (((1,), (1,)), ((), ()))
ATB = (((0,), (0,)), ((), ()))


def mm(a, b, dims=AB):
    return lax.dot_general(a, b, dims, preferred_element_type=jnp.float32)


def mm3(a, b, dims=AB):
    return mm(a[0], b[0], dims) + (mm(a[1], b[0], dims) + mm(a[0], b[1], dims))


def unit_lower_inverse(strict, row, col):
    size = strict.shape[0]
    inverse = jnp.where(row == col, 1.0, 0.0) - jnp.where(
        (row >> 1) == (col >> 1), strict, 0.0
    )
    level = 1
    while (1 << level) < size:
        joined = ((row >> (level + 1)) == (col >> (level + 1))) & ((row >> level) != (col >> level))
        parts = halves(inverse)
        step = mm3(halves(jnp.where(joined, strict, 0.0)), parts)
        inverse = inverse - mm3(parts, halves(step))
        level += 1
    return inverse


def head_forward(queries, keys, house_raw, values, betas, allowed, row, col, scaling):
    house = house_raw * lax.rsqrt(jnp.sum(house_raw * house_raw, axis=1, keepdims=True) + EPSILON)
    scaled = halves(betas * house)
    q, k, w = halves(queries), halves(keys), halves(house)
    strict = jnp.where(row > col, mm3(scaled, w, ABT), 0.0)
    inverse = halves(unit_lower_inverse(strict, row, col))
    house_key = jnp.where(row > col, mm3(scaled, k, ABT), 0.0)
    query_house = halves(jnp.where(row >= col, mm3(q, w, ABT), 0.0))
    key_side = mm3(inverse, halves(house_key))
    query_side = mm3(query_house, inverse)
    scores = (mm3(q, k, ABT) - mm3(query_house, halves(key_side))) * scaling
    masked = jnp.where(allowed, scores, NEGATIVE)
    weights = jnp.exp(masked - jnp.max(masked, axis=1, keepdims=True))
    probs = weights / jnp.sum(weights, axis=1, keepdims=True)
    attn = mm(probs.astype(jnp.bfloat16), values)
    return attn, probs, key_side, query_side


def head_backward(queries, keys, house_raw, values, betas, probs, key_side, query_side, d_attn, row, col, scaling):
    norm = lax.rsqrt(jnp.sum(house_raw * house_raw, axis=1, keepdims=True) + EPSILON)
    house = house_raw * norm
    d_values = mm(probs.astype(jnp.bfloat16), d_attn, ATB)
    d_probs = mm(d_attn, values, ABT)
    row_delta = jnp.sum(probs * d_probs, axis=1, keepdims=True)
    d_scores = halves(probs * (d_probs - row_delta) * scaling)
    q, k, w, scaled = halves(queries), halves(keys), halves(house), halves(betas * house)
    side = halves(query_side)
    d_side = -mm3(d_scores, halves(key_side), ABT)
    d_query_house = halves(jnp.where(row >= col, d_side, 0.0))
    d_strict = halves(jnp.where(row > col, -mm3(side, halves(d_side), ATB), 0.0))
    d_house_key = halves(jnp.where(row > col, -mm3(side, d_scores, ATB), 0.0))
    d_queries = mm3(d_scores, k) + mm3(d_query_house, w)
    d_keys = mm3(d_scores, q, ATB) + mm3(d_house_key, scaled, ATB)
    d_scaled = mm3(d_strict, w) + mm3(d_house_key, k)
    d_house = mm3(d_strict, scaled, ATB) + mm3(d_query_house, q, ATB)
    d_betas = jnp.sum(d_scaled * house, axis=1, keepdims=True)
    d_house = d_house + betas * d_scaled
    d_house_raw = norm * (d_house - house * jnp.sum(d_house * house, axis=1, keepdims=True))
    d_logits = d_betas * betas * (1.0 - 0.5 * betas)
    return d_queries, d_keys, d_house_raw, d_values, d_logits


def started(pairs, sems):
    copies = [
        pltpu.make_async_copy(source, target, sems.at[n]) for n, (source, target) in enumerate(pairs)
    ]
    for copy in copies:
        copy.start()
    return copies


def attention_forward_kernel(
    heads, places, *refs
):
    weights, xs, (gain, id_row, id_col) = refs[0:8], refs[8:12], refs[12:15]
    h_mine, h_other, proj, attn, probs, key_side, query_side = refs[15:22]
    w_all, x_all, weight_sems, x_sems = refs[22:26]
    depth, rows, width = weights[0].shape[0], x_all.shape[0] // 4, attn.shape[1]
    head, used = width // heads, proj.shape[1]
    x_copies = started(
        [
            (xs[n].at[pl.ds(0, rows)], x_all.at[pl.ds(pl.multiple_of(places[8 + n], 64), rows)])
            for n in range(4)
        ],
        x_sems,
    )
    w_copies = started(
        [
            (
                weights[n].at[:, pl.ds(0, used)],
                w_all.at[pl.ds(pl.multiple_of(places[n], 64), depth)],
            )
            for n in range(8)
        ],
        weight_sems,
    )
    for copy in x_copies:
        copy.wait()
    half = h_mine.shape[1]
    x = x_all[...].astype(jnp.float32)
    factor = lax.rsqrt(jnp.mean(x * x, axis=1, keepdims=True) + EPSILON)
    x_all[...] = (x * factor * gain[...]).astype(jnp.bfloat16)
    h_mine[...] = x_all[:, pl.ds(pl.multiple_of(places[12], 128), half)]
    h_other[...] = x_all[:, pl.ds(pl.multiple_of(places[13], 128), half)]
    for copy in w_copies:
        copy.wait()
    proj[...] = mm(x_all[...], w_all[...])
    length = x_all.shape[0]
    row = lax.broadcasted_iota(jnp.int32, (length, length), 0)
    col = lax.broadcasted_iota(jnp.int32, (length, length), 1)
    allowed = (col <= row) & (id_row[...] == id_col[...])
    betas = 2.0 * jax.nn.sigmoid(proj[:, 4 * width :])
    scaling = 1.0 / math.sqrt(head)
    for n in range(heads):
        at = [slice(p * width + n * head, p * width + (n + 1) * head) for p in range(4)]
        out, prob, key, query = head_forward(
            proj[:, at[2]],
            proj[:, at[1]],
            proj[:, at[0]],
            proj[:, at[3]].astype(jnp.bfloat16),
            betas[:, n : n + 1],
            allowed,
            row,
            col,
            scaling,
        )
        attn[:, n * head : (n + 1) * head] = out.astype(jnp.bfloat16)
        probs[n], key_side[n], query_side[n] = prob, key, query


def branch_kernel(places, *refs):
    weights, attn, parts = refs[0:8], refs[8], refs[9:13]
    w_all, total, sems = refs[13:16]
    depth, width, skip = weights[0].shape[0], attn.shape[1], weights[0].shape[1] - attn.shape[1]
    copies = started(
        [
            (
                weights[n].at[:, pl.ds(skip, width)],
                w_all.at[pl.ds(pl.multiple_of(places[n], 64), depth)],
            )
            for n in range(8)
        ],
        sems,
    )
    for copy in copies:
        copy.wait()
    total[...] = mm(attn[...], w_all[...], ABT).astype(jnp.bfloat16)
    for n in range(4):
        parts[n][...] = total[pl.ds(pl.multiple_of(places[8 + n], 64), parts[n].shape[0])]


def feed_forward_kernel(places, *refs):
    weights, ins, grads = refs[0:8], refs[8:16], refs[16:24]
    two_parts, out_parts = refs[24:28], refs[28:32]
    in_mine, in_other, grad_mine, grad_other, hidden, d_both = refs[32:38]
    w_all, in_all, grad_all, weight_sems, in_sems, grad_sems = refs[38:44]
    depth, rows, units = weights[0].shape[0], ins[0].shape[0], hidden.shape[1]
    w_copies = started(
        [
            (weights[n], w_all.at[pl.ds(pl.multiple_of(places[n], 64), depth)])
            for n in range(8)
        ],
        weight_sems,
    )
    grad_copies = started([(grads[n], grad_all.at[pl.ds(n * rows, rows)]) for n in range(8)], grad_sems)
    in_copies = started([(ins[n], in_all.at[pl.ds(n * rows, rows)]) for n in range(8)], in_sems)
    for copy in w_copies + grad_copies + in_copies:
        copy.wait()
    both = mm(in_all[...], w_all[:, : 2 * units])
    d_hidden = mm(grad_all[...], w_all[:, 2 * units :])
    gate, up = both[:, :units], both[:, units:]
    sigmoid = jax.nn.sigmoid(gate)
    silu = gate * sigmoid
    hidden[...] = (silu * up).astype(jnp.bfloat16)
    d_both[:, :units] = (d_hidden * up * sigmoid * (1.0 + gate * (1.0 - sigmoid))).astype(jnp.bfloat16)
    d_both[:, units:] = (d_hidden * silu).astype(jnp.bfloat16)
    d_two = mm(d_both[...], w_all[:, : 2 * units], ABT).astype(jnp.bfloat16)
    for n in range(4):
        for s in range(2):
            two_parts[n][s] = d_two[(s * 4 + n) * rows : (s * 4 + n + 1) * rows]
    out = mm(hidden[...], w_all[:, 2 * units :], ABT).astype(jnp.bfloat16)
    for n in range(4):
        for s in range(2):
            out_parts[n][s] = out[(s * 4 + n) * rows : (s * 4 + n + 1) * rows]
    half = in_mine.shape[1]
    mine = pl.ds(pl.multiple_of(places[12], 128), half)
    other = pl.ds(pl.multiple_of(places[13], 128), half)
    in_mine[...], in_other[...] = in_all[:, mine], in_all[:, other]
    grad_mine[...], grad_other[...] = grad_all[:, mine], grad_all[:, other]


def attention_backward_kernel(heads, places, *refs):
    weights, ds, (proj, probs, key_side, query_side) = refs[0:8], refs[8:12], refs[12:16]
    d_proj, d_mine, d_other, parts = refs[16], refs[17], refs[18], refs[19:23]
    w_all, d_all, d_attn, total, weight_sems, d_sems = refs[23:29]
    depth, rows, used = weights[0].shape[0], ds[0].shape[0], proj.shape[1]
    width = w_all.shape[1] - used
    head = width // heads
    w_copies = started(
        [
            (weights[n], w_all.at[pl.ds(pl.multiple_of(places[n], 64), depth)])
            for n in range(8)
        ],
        weight_sems,
    )
    d_copies = started(
        [(ds[n], d_all.at[pl.ds(pl.multiple_of(places[8 + n], 64), rows)]) for n in range(4)], d_sems
    )
    for copy in d_copies + w_copies:
        copy.wait()
    half = d_mine.shape[1]
    d_mine[...] = d_all[:, pl.ds(pl.multiple_of(places[12], 128), half)]
    d_other[...] = d_all[:, pl.ds(pl.multiple_of(places[13], 128), half)]
    d_attn[...] = mm(d_all[...], w_all[:, used:]).astype(jnp.bfloat16)
    length = d_all.shape[0]
    row = lax.broadcasted_iota(jnp.int32, (length, length), 0)
    col = lax.broadcasted_iota(jnp.int32, (length, length), 1)
    betas = 2.0 * jax.nn.sigmoid(proj[:, 4 * width :])
    lane = lax.broadcasted_iota(jnp.int32, betas.shape, 1)
    logits = jnp.zeros(betas.shape, jnp.float32)
    for n in range(heads):
        at = [slice(p * width + n * head, p * width + (n + 1) * head) for p in range(4)]
        d_queries, d_keys, d_house, d_values, d_logit = head_backward(
            proj[:, at[2]],
            proj[:, at[1]],
            proj[:, at[0]],
            proj[:, at[3]].astype(jnp.bfloat16),
            betas[:, n : n + 1],
            probs[n],
            key_side[n],
            query_side[n],
            d_attn[:, n * head : (n + 1) * head],
            row,
            col,
            1.0 / math.sqrt(head),
        )
        for p, value in enumerate((d_house, d_keys, d_queries, d_values)):
            d_proj[:, at[p]] = value.astype(jnp.bfloat16)
        logits = jnp.where(lane == n, d_logit, logits)
    d_proj[:, 4 * width :] = logits.astype(jnp.bfloat16)
    total[...] = mm(d_proj[...], w_all[:, :used], ABT).astype(jnp.bfloat16)
    for n in range(4):
        parts[n][...] = total[pl.ds(pl.multiple_of(places[8 + n], 64), rows)]


def weight_grad_kernel(count, places, *refs):
    pairs = [refs[4 * n : 4 * n + 4] for n in range(count)]
    near, far, total = refs[4 * count], refs[4 * count + 1], refs[4 * count + 2]
    at = 0
    for left, right, left_other, right_other in pairs:
        width = right.shape[1]
        total[:, at : at + width] = (
            mm(left[...], right[...], ATB) + mm(left_other[...], right_other[...], ATB)
        ).astype(jnp.bfloat16)
        at += width
    depth = near.shape[1]
    for n, target in enumerate((near.at[0], far.at[0], near.at[1], far.at[1])):
        target[...] = total[pl.ds(pl.multiple_of(places[14 + n], 64), depth)]


VMEM_BYTES = 56 * 1024 * 1024


def call(kernel, outs, scratch, places, operands, spaces):
    vmem = pl.BlockSpec(memory_space=pltpu.VMEM)
    kinds = {"v": vmem, "a": pl.BlockSpec(memory_space=pl.ANY)}
    return pl.pallas_call(
        kernel,
        out_shape=[jax.ShapeDtypeStruct(shape, kind) for shape, kind in outs],
        in_specs=[pl.BlockSpec(memory_space=pltpu.SMEM)] + [kinds[s] for s in spaces],
        out_specs=[vmem] * len(outs),
        scratch_shapes=scratch,
        compiler_params=pltpu.CompilerParams(vmem_limit_bytes=VMEM_BYTES),
    )(places, *operands)


def swap(block, axis, distance):
    size = lax.axis_size(axis)
    return lax.ppermute(block, axis, [(i, i ^ distance) for i in range(size)])


def turned(block):
    size = lax.axis_size("tp")
    route = [(c * size + t, t * size + c) for c in range(size) for t in range(size)]
    return lax.ppermute(block, ("ctx", "tp"), route)


def all_tp(block):
    return [block] + [swap(block, "tp", n) for n in (1, 2, 3)]


def sum_tp(parts):
    received = [swap(parts[n], "tp", n) for n in (1, 2, 3)]
    return [parts[0]] + received


def all_rows(first, second):
    own = [second, None, swap(first, "ctx", 2), None]
    own[1] = swap(own[0], "ctx", 1)
    own[3] = swap(own[2], "ctx", 1)
    return own + [swap(piece, "fsdp", 1) for piece in own]


def add_up(blocks):
    total = blocks[0].astype(jnp.float32)
    for block in blocks[1:]:
        total = total + block.astype(jnp.float32)
    return total


def whole_sequences(
    hidden_in,
    segment_ids,
    doc_starts,
    norm1_gain,
    w_query,
    w_key,
    w_value,
    w_house,
    w_beta,
    w_out,
    norm2_gain,
    w_gate,
    w_up,
    w_down,
    output_grad,
):
    low, wide = jnp.bfloat16, jnp.float32
    core, chain, column = lax.axis_index("fsdp"), lax.axis_index("ctx"), lax.axis_index("tp")
    rows, features = hidden_in.shape[1], hidden_in.shape[2]
    depth, width, heads = w_query.shape[0], w_query.shape[1], w_beta.shape[1]
    length, half = 4 * rows, features // 2
    near = jnp.arange(4, dtype=jnp.int32)
    places = jnp.concatenate(
        [
            (core * 4 + (chain ^ near)) * depth,
            ((1 - core) * 4 + (chain ^ near)) * depth,
            (column ^ near) * rows,
            jnp.stack([core, 1 - core]) * half,
            (chain ^ near) * depth,
        ]
    ).astype(jnp.int32)

    extra = jnp.zeros((16, features), low)
    own_ids = lax.dynamic_index_in_dim(segment_ids, column, 0, keepdims=False)
    extra = extra.at[0, :rows].set(own_ids.astype(low))
    extra = extra.at[1, : 2 * depth].set(jnp.concatenate([norm1_gain, norm2_gain]))
    own_x = lax.dynamic_index_in_dim(hidden_in, column, 0, keepdims=False)
    x_block = turned(jnp.concatenate([own_x, extra]))
    x_pieces = all_tp(x_block)

    beta_wide = jnp.pad(w_beta, ((0, 0), (0, 128 - heads)))
    first = jnp.concatenate([w_house, w_key, w_query, w_value, beta_wide, w_out], axis=1)
    used = first.shape[1] - width
    attn_weights = all_rows(first, first)

    own_grad = turned(lax.dynamic_index_in_dim(output_grad, column, 0, keepdims=False))
    grad_pieces = all_tp(own_grad) + all_tp(swap(own_grad, "ctx", 2))

    units = w_gate.shape[1] // 2
    upper = chain >= 2

    def part_of(take_upper):
        return jnp.concatenate(
            [jnp.where(take_upper, w[:, units:], w[:, :units]) for w in (w_gate, w_up, w_down)], axis=1
        )

    ffn_weights = all_rows(part_of(~upper), part_of(upper))

    info = jnp.stack([piece[rows : rows + 2] for piece in x_pieces])
    chosen = near[:, None] == (near[None, :] ^ column)
    info = jnp.sum(jnp.where(chosen[:, :, None, None], info[None].astype(wide), 0.0), axis=1)
    ids = info[:, 0, :rows].reshape(length)
    gains = info[:, 1, : 2 * depth].astype(low)
    gains_other = swap(gains, "fsdp", 1)
    gains = jnp.where(core == 0, jnp.stack([gains, gains_other]), jnp.stack([gains_other, gains]))
    gain_one = gains[:, :, :depth].reshape(1, features).astype(wide)
    gain_two = gains[:, :, depth:].reshape(1, features).astype(wide)

    square = (heads, length, length)
    h_mine, h_other, proj, attn, probs, key_side, query_side = call(
        functools.partial(attention_forward_kernel, heads),
        [
            ((length, half), low),
            ((length, half), low),
            ((length, used), wide),
            ((length, width), low),
            (square, wide),
            (square, wide),
            (square, wide),
        ],
        [
            pltpu.VMEM((features, used), low),
            pltpu.VMEM((length, features), low),
            pltpu.SemaphoreType.DMA((8,)),
            pltpu.SemaphoreType.DMA((4,)),
        ],
        places,
        [*attn_weights, *x_pieces, gain_one, ids[None, :], ids[:, None]],
        "a" * 12 + "v" * 3,
    )
    branch_parts = call(
        branch_kernel,
        [((rows, features), low)] * 4,
        [
            pltpu.VMEM((features, width), low),
            pltpu.VMEM((length, features), low),
            pltpu.SemaphoreType.DMA((8,)),
        ],
        places,
        [*attn_weights, attn],
        "a" * 8 + "v",
    )
    residual = x_block[:rows].astype(wide)
    normed_one, factor_one = norm_rows(residual)
    middle = residual + add_up(sum_tp(branch_parts))
    normed_two, factor_two = norm_rows(middle)
    h_two = (normed_two * gain_two).astype(low)
    in_pieces = all_tp(h_two) + all_tp(swap(h_two, "ctx", 2))

    tokens = 2 * length
    pair = ((2, rows, features), low)
    outs = call(
        feed_forward_kernel,
        [pair] * 8 + [((tokens, half), low)] * 4 + [((tokens, units), low), ((tokens, 2 * units), low)],
        [
            pltpu.VMEM((features, 3 * units), low),
            pltpu.VMEM((tokens, features), low),
            pltpu.VMEM((tokens, features), low),
            pltpu.SemaphoreType.DMA((8,)),
            pltpu.SemaphoreType.DMA((8,)),
            pltpu.SemaphoreType.DMA((8,)),
        ],
        places,
        [*ffn_weights, *in_pieces, *grad_pieces],
        "a" * 24,
    )
    two_parts, out_parts = outs[:4], outs[4:8]
    in_mine, in_other, grad_mine, grad_other, hidden, d_both = outs[8:]

    two_sum = add_up(sum_tp(two_parts))
    d_two = two_sum[0] + swap(two_sum[1].astype(low), "ctx", 2).astype(wide)
    gain_two_grad = jnp.sum(d_two * normed_two, axis=0)
    d_middle = own_grad.astype(wide) + norm_back(d_two, normed_two, factor_two, gain_two)
    d_pieces = all_tp(d_middle.astype(low))

    def exchanged(left_mine, left_other, right):
        return [left_mine, right, swap(left_other, "fsdp", 1), swap(right, "fsdp", 1)]

    def grads_of(groups):
        total = sum(group[1].shape[1] for group in groups)
        return call(
            functools.partial(weight_grad_kernel, len(groups)),
            [((2, depth, total), low)] * 2,
            [pltpu.VMEM((half, total), low)],
            places,
            [operand for group in groups for operand in group],
            "v" * (4 * len(groups)),
        )

    def over_ctx(stay, leave):
        return add_up([stay, swap(leave, "ctx", 1)])

    ffn_sum = over_ctx(
        *grads_of([exchanged(in_mine, in_other, d_both), exchanged(grad_mine, grad_other, hidden)])
    )
    ffn_other = swap(ffn_sum[1].astype(low), "ctx", 2).astype(wide)

    def ffn_result(n):
        kept = ffn_sum[0, :, n * units : (n + 1) * units]
        came = ffn_other[:, n * units : (n + 1) * units]
        return jnp.concatenate([jnp.where(upper, came, kept), jnp.where(upper, kept, came)], axis=1)

    back = call(
        functools.partial(attention_backward_kernel, heads),
        [((length, used), low), ((length, half), low), ((length, half), low)]
        + [((rows, features), low)] * 4,
        [
            pltpu.VMEM((features, used + width), low),
            pltpu.VMEM((length, features), low),
            pltpu.VMEM((length, width), low),
            pltpu.VMEM((length, features), low),
            pltpu.SemaphoreType.DMA((8,)),
            pltpu.SemaphoreType.DMA((4,)),
        ],
        places,
        [*attn_weights, *d_pieces, proj, probs, key_side, query_side],
        "a" * 12 + "v" * 4,
    )
    d_proj, d_mine, d_other = back[:3]
    d_one = add_up(sum_tp(back[3:]))
    gain_one_grad = jnp.sum(d_one * normed_one, axis=0)
    in_grad = (d_middle + norm_back(d_one, normed_one, factor_one, gain_one)).astype(low)

    attn_sum = over_ctx(
        *grads_of([exchanged(h_mine, h_other, d_proj), exchanged(d_mine, d_other, attn)])
    )
    attn_grads = attn_sum[0] + swap(attn_sum[1].astype(low), "ctx", 2).astype(wide)

    out_sum = add_up(sum_tp(out_parts))
    mlp_out = out_sum[0] + swap(out_sum[1].astype(low), "ctx", 2).astype(wide)
    block_out = lax.all_gather(turned((middle + mlp_out).astype(low)), "tp", axis=0)
    input_grad = lax.all_gather(turned(in_grad), "tp", axis=0)

    gain_grads = lax.psum(jnp.stack([gain_one_grad, gain_two_grad]), ("fsdp", "ctx", "tp"))
    gain_grads = lax.dynamic_slice_in_dim(gain_grads, (core * 4 + chain) * depth, depth, axis=1)
    house_grad, key_grad, query_grad, value_grad = (
        attn_grads[:, n * width : (n + 1) * width] for n in range(4)
    )
    beta_grad = attn_grads[:, 4 * width : 4 * width + heads]
    return (
        block_out,
        input_grad,
        gain_grads[0],
        query_grad,
        key_grad,
        value_grad,
        house_grad,
        beta_grad,
        attn_grads[:, used:],
        gain_grads[1],
        ffn_result(0),
        ffn_result(1),
        ffn_result(2),
    )


def shards(*args):
    sizes = [lax.axis_size(axis) for axis in ("fsdp", "ctx", "tp")]
    if sizes == [2, 4, 4] and args[0].shape[0] == 4:
        return whole_sequences(*args)
    return ring_of_groups(*args)


def solution(mesh):
    in_specs = (
        P("fsdp", "ctx", None),
        P("fsdp", "ctx"),
        P("fsdp", "ctx"),
        P(("fsdp", "ctx")),
        P(("fsdp", "ctx"), "tp"),
        P(("fsdp", "ctx"), "tp"),
        P(("fsdp", "ctx"), "tp"),
        P(("fsdp", "ctx"), "tp"),
        P(("fsdp", "ctx"), "tp"),
        P(("fsdp", "ctx"), "tp"),
        P(("fsdp", "ctx")),
        P(("fsdp", "ctx"), "tp"),
        P(("fsdp", "ctx"), "tp"),
        P(("fsdp", "ctx"), "tp"),
        P("fsdp", "ctx", None),
    )
    out_specs = (
        P("fsdp", "ctx", None),
        P("fsdp", "ctx", None),
        P(("fsdp", "ctx")),
        P(("fsdp", "ctx"), "tp"),
        P(("fsdp", "ctx"), "tp"),
        P(("fsdp", "ctx"), "tp"),
        P(("fsdp", "ctx"), "tp"),
        P(("fsdp", "ctx"), "tp"),
        P(("fsdp", "ctx"), "tp"),
        P(("fsdp", "ctx")),
        P(("fsdp", "ctx"), "tp"),
        P(("fsdp", "ctx"), "tp"),
        P(("fsdp", "ctx"), "tp"),
    )
    return jax.shard_map(shards, mesh=mesh, in_specs=in_specs, out_specs=out_specs, check_vma=False)
```

```python
import functools
import math

import jax
import jax.numpy as jnp
from jax import lax
from jax.experimental import pallas as pl
from jax.experimental.pallas import tpu as pltpu
from jax.sharding import PartitionSpec as P

EPSILON = 1e-06
HIGHEST = lax.Precision.HIGHEST
NEGATIVE = -1e30


def passed_along(block, axis, distance):
    devices = range(lax.axis_size(axis))
    route = [(i - distance, i) for i in devices if i - distance in devices]
    return lax.ppermute(block, axis, route)


def group_algebra(queries, key_rows, house, betas):
    length = queries.shape[0]
    scaling = 1.0 / math.sqrt(queries.shape[1])
    row_index = lax.broadcasted_iota(jnp.int32, (length, length), 0)
    column_index = lax.broadcasted_iota(jnp.int32, (length, length), 1)
    strict_below = row_index > column_index
    house_gram = jnp.dot(house, house.T, precision=HIGHEST)
    system = jnp.where(strict_below, house_gram, 0.0) + jnp.diag(1.0 / betas)
    identity = jnp.eye(length, dtype=house.dtype)
    inverse = jax.scipy.linalg.solve_triangular(system, identity, lower=True)
    query_house = jnp.where(
        row_index >= column_index, jnp.dot(queries, house.T, precision=HIGHEST), 0.0
    )
    house_key = jnp.where(strict_below, jnp.dot(house, key_rows.T, precision=HIGHEST), 0.0)
    query_side = jnp.dot(query_house, inverse, precision=HIGHEST)
    key_side = jnp.dot(inverse, house_key, precision=HIGHEST)
    scores = (
        jnp.dot(queries, key_rows.T, precision=HIGHEST)
        - jnp.dot(query_side, house_key, precision=HIGHEST)
    ) * scaling
    query_bar = queries - jnp.dot(query_side, house, precision=HIGHEST)
    key_bar = key_rows - jnp.dot(key_side.T, house, precision=HIGHEST)
    inner = jnp.dot(inverse, house, precision=HIGHEST)
    factor = jnp.eye(house.shape[1], dtype=house.dtype) - jnp.dot(house.T, inner, precision=HIGHEST)
    return (scores, query_bar, key_bar, factor)


def local_map(queries, key_rows, house_raw, beta_logits):
    house = house_raw * lax.rsqrt(jnp.sum(house_raw * house_raw, axis=-1, keepdims=True) + EPSILON)
    betas = 2.0 * jax.nn.sigmoid(beta_logits)
    return jax.vmap(jax.vmap(group_algebra))(queries, key_rows, house, betas)


def doc_starts_local(segment_ids, group_first, first_position):
    length = segment_ids.shape[-1]
    previous = jnp.concatenate([segment_ids[..., :1], segment_ids[..., :-1]], axis=-1)
    offsets = lax.broadcasted_iota(jnp.int32, segment_ids.shape, segment_ids.ndim - 1)
    boundary = (offsets > 0) & (segment_ids != previous)
    marks = jnp.where(boundary, offsets + first_position, -1)
    row_index = lax.broadcasted_iota(jnp.int32, (length, length), 0)
    column_index = lax.broadcasted_iota(jnp.int32, (length, length), 1)
    seen = jnp.where(column_index <= row_index, marks[..., None, :], -1)
    return jnp.maximum(jnp.max(seen, axis=-1), group_first)


def norm_rows(values):
    factor = lax.rsqrt(jnp.mean(values * values, axis=-1, keepdims=True) + EPSILON)
    return (values * factor, factor)


def norm_back(gradient, normed, factor, norm_gain):
    scaled = gradient * norm_gain
    return factor * (scaled - normed * jnp.mean(scaled * normed, axis=-1, keepdims=True))


def split_heads(tensor, head_count):
    seq_count, length, total_width = tensor.shape
    return tensor.reshape(seq_count, length, head_count, total_width // head_count).transpose(
        0, 2, 1, 3
    )


def join_heads(tensor):
    seq_count, head_count, length, head_width = tensor.shape
    return tensor.transpose(0, 2, 1, 3).reshape(seq_count, length, head_count * head_width)


def project(inputs, weight):
    return jnp.einsum("scd,df->scf", inputs, weight, preferred_element_type=jnp.float32)


def project_back(gradient, weight):
    return jnp.einsum("scf,df->scd", gradient, weight, preferred_element_type=jnp.float32)


def weight_grad(inputs, gradient):
    return jnp.einsum("scd,scf->df", inputs, gradient, preferred_element_type=jnp.float32)


def cross_scores(query_rot, key_low, scaling):
    return (
        jnp.einsum("shqd,shkd->shqk", query_rot, key_low, preferred_element_type=jnp.float32)
        * scaling
    )


def weighted_values(weights, values_in):
    return jnp.einsum("shqk,shkd->shqd", weights, values_in, preferred_element_type=jnp.float32)


def ring_of_groups(
    hidden_in,
    segment_ids,
    doc_starts,
    norm1_gain,
    w_query,
    w_key,
    w_value,
    w_house,
    w_beta,
    w_out,
    norm2_gain,
    w_gate,
    w_up,
    w_down,
    output_grad,
):
    gathered = (
        lax.all_gather(norm1_gain, ("fsdp", "ctx"), axis=0, tiled=True),
        lax.all_gather(w_query, ("fsdp", "ctx"), axis=0, tiled=True),
        lax.all_gather(w_key, ("fsdp", "ctx"), axis=0, tiled=True),
        lax.all_gather(w_value, ("fsdp", "ctx"), axis=0, tiled=True),
        lax.all_gather(w_house, ("fsdp", "ctx"), axis=0, tiled=True),
        lax.all_gather(w_beta, ("fsdp", "ctx"), axis=0, tiled=True),
        lax.all_gather(w_out, ("fsdp", "ctx"), axis=0, tiled=True),
        lax.all_gather(norm2_gain, ("fsdp", "ctx"), axis=0, tiled=True),
        lax.all_gather(w_gate, ("fsdp", "ctx"), axis=0, tiled=True),
        lax.all_gather(w_up, ("fsdp", "ctx"), axis=0, tiled=True),
        lax.all_gather(w_down, ("fsdp", "ctx"), axis=0, tiled=True),
    )
    (
        gain_one,
        query_full,
        key_full,
        value_full,
        house_full,
        beta_full,
        out_full,
        gain_two,
        gate_full,
        up_full,
        down_full,
    ) = gathered
    gain_one_f = gain_one.astype(jnp.float32)
    gain_two_f = gain_two.astype(jnp.float32)
    head_count = beta_full.shape[1]
    length = hidden_in.shape[1]
    residual = hidden_in.astype(jnp.float32)
    normed_one, factor_one = norm_rows(residual)
    h_one = (normed_one * gain_one_f).astype(jnp.bfloat16)
    queries = split_heads(project(h_one, query_full), head_count)
    key_rows = split_heads(project(h_one, key_full), head_count)
    values_low = split_heads(project(h_one, value_full).astype(jnp.bfloat16), head_count)
    house_raw = split_heads(project(h_one, house_full), head_count)
    beta_logits = project(h_one, beta_full).transpose(0, 2, 1)
    (scores_local, query_bar, key_bar, factors), local_back = jax.vjp(
        local_map, queries, key_rows, house_raw, beta_logits
    )
    scaling = 1.0 / math.sqrt(queries.shape[-1])
    chain_index = lax.axis_index("ctx")
    hop_total = lax.axis_size("ctx") - 1
    first_position = chain_index * length
    starts = doc_starts_local(segment_ids, doc_starts, first_position)
    offsets = jnp.arange(length, dtype=jnp.int32)
    causal = (offsets[None, :] <= offsets[:, None])[None]
    local_mask = (causal & (offsets[None, None, :] + first_position >= starts[:, :, None]))[:, None]

    def hop_mask(distance):
        key_pos = (chain_index - distance) * length + offsets
        return (key_pos[None, None, :] >= starts[:, :, None])[:, None]

    masked_local = jnp.where(local_mask, scores_local, NEGATIVE)
    local_max = jnp.max(masked_local, axis=-1)
    local_sum = jnp.sum(jnp.exp(masked_local - local_max[..., None]), axis=-1)
    key_send = key_bar.astype(jnp.bfloat16)
    identity = jnp.broadcast_to(jnp.eye(factors.shape[-1], dtype=jnp.float32), factors.shape)
    stack_rot = jnp.zeros((hop_total,) + query_bar.shape, jnp.bfloat16)
    stack_factors = jnp.zeros((hop_total,) + factors.shape, jnp.float32)

    def rotate(hop_step, hop_keys, chain, run_max, run_sum):
        query_rot = jnp.einsum("shqa,shab->shqb", query_bar, chain, precision=HIGHEST).astype(
            jnp.bfloat16
        )
        masked = jnp.where(
            hop_mask(hop_step + 1), cross_scores(query_rot, hop_keys, scaling), NEGATIVE
        )
        new_max = jnp.maximum(run_max, jnp.max(masked, axis=-1))
        new_sum = run_sum * jnp.exp(run_max - new_max) + jnp.sum(
            jnp.exp(masked - new_max[..., None]), axis=-1
        )
        return (query_rot, new_max, new_sum)

    stack_keys = jnp.zeros((hop_total,) + key_send.shape, jnp.bfloat16)
    stack_values = jnp.zeros((hop_total,) + values_low.shape, jnp.bfloat16)

    def forward_hop(hop_step, loop_state):
        (
            send_keys,
            send_values,
            send_factor,
            kept_keys,
            kept_values,
            kept_rot,
            kept_factors,
            run_max,
            run_sum,
        ) = loop_state
        got_keys, got_values = passed_along((send_keys, send_values), "ctx", 1)
        got_factor = passed_along(send_factor.astype(jnp.bfloat16), "ctx", 1).astype(
            send_factor.dtype
        )
        query_rot, run_max, run_sum = rotate(hop_step, got_keys, got_factor, run_max, run_sum)
        kept_keys = lax.dynamic_update_index_in_dim(kept_keys, got_keys, hop_step, 0)
        kept_values = lax.dynamic_update_index_in_dim(kept_values, got_values, hop_step, 0)
        kept_rot = lax.dynamic_update_index_in_dim(kept_rot, query_rot, hop_step, 0)
        kept_factors = lax.dynamic_update_index_in_dim(kept_factors, got_factor, hop_step, 0)
        next_factor = jnp.einsum("shab,shbc->shac", factors, got_factor, precision=HIGHEST)
        return (
            got_keys,
            got_values,
            next_factor,
            kept_keys,
            kept_values,
            kept_rot,
            kept_factors,
            run_max,
            run_sum,
        )

    loop_state = lax.fori_loop(
        0,
        hop_total,
        forward_hop,
        (
            key_send,
            values_low,
            identity,
            stack_keys,
            stack_values,
            stack_rot,
            stack_factors,
            local_max,
            local_sum,
        ),
    )
    stack_keys, stack_values, stack_rot, stack_factors = (
        loop_state[3],
        loop_state[4],
        loop_state[5],
        loop_state[6],
    )
    run_max, run_sum = (loop_state[7], loop_state[8])

    def fetch(hop_step):
        return (
            lax.dynamic_index_in_dim(stack_keys, hop_step, 0, keepdims=False),
            lax.dynamic_index_in_dim(stack_values, hop_step, 0, keepdims=False),
        )

    log_total = run_max + jnp.log(run_sum)

    def recall(hop_step):
        hop_keys, hop_values = fetch(hop_step)
        hop_factor = lax.dynamic_index_in_dim(stack_factors, hop_step, 0, keepdims=False)
        query_rot = lax.dynamic_index_in_dim(stack_rot, hop_step, 0, keepdims=False)
        masked = jnp.where(
            hop_mask(hop_step + 1), cross_scores(query_rot, hop_keys, scaling), NEGATIVE
        )
        hop_probs = jnp.exp(masked - log_total[..., None])
        return (hop_keys, hop_values, hop_factor, query_rot, hop_probs)

    probs_local = jnp.exp(masked_local - log_total[..., None])
    probs_local_low = probs_local.astype(jnp.bfloat16)
    attn_acc = weighted_values(probs_local_low, values_low)
    attn_rest = weighted_values(
        (probs_local - probs_local_low.astype(jnp.float32)).astype(jnp.bfloat16), values_low
    )

    def value_hop(hop_step, running):
        total_low, total_rest = running
        hop_keys, hop_values, hop_factor, query_rot, hop_probs = recall(hop_step)
        hop_low = hop_probs.astype(jnp.bfloat16)
        total_low = total_low + weighted_values(hop_low, hop_values)
        total_rest = total_rest + weighted_values(
            (hop_probs - hop_low.astype(jnp.float32)).astype(jnp.bfloat16), hop_values
        )
        return (total_low, total_rest)

    attn_acc, attn_rest = lax.fori_loop(0, hop_total, value_hop, (attn_acc, attn_rest))
    attn_low = join_heads(attn_acc.astype(jnp.bfloat16))
    branch = lax.psum(project_back(attn_low, out_full), "tp")
    middle = residual + branch
    normed_two, factor_two = norm_rows(middle)
    h_two = (normed_two * gain_two_f).astype(jnp.bfloat16)
    gate_proj = project(h_two, gate_full)
    up_proj = project(h_two, up_full)
    gate_sigmoid = jax.nn.sigmoid(gate_proj)
    silu_gate = gate_proj * gate_sigmoid
    hidden_low = (silu_gate * up_proj).astype(jnp.bfloat16)
    mlp_out = lax.psum(project_back(hidden_low, down_full).astype(jnp.bfloat16), "tp").astype(
        jnp.float32
    )
    block_out = (middle + mlp_out).astype(jnp.bfloat16)
    down_grad = weight_grad(output_grad, hidden_low)
    d_hidden = project(output_grad, down_full)
    d_gate = (d_hidden * up_proj * gate_sigmoid * (1.0 + gate_proj * (1.0 - gate_sigmoid))).astype(
        jnp.bfloat16
    )
    d_up = (d_hidden * silu_gate).astype(jnp.bfloat16)
    gate_grad = weight_grad(h_two, d_gate)
    up_grad = weight_grad(h_two, d_up)
    d_two = lax.psum(project_back(d_gate, gate_full) + project_back(d_up, up_full), "tp")
    gain_two_grad = jnp.sum(d_two * normed_two, axis=(0, 1))
    d_middle = output_grad.astype(jnp.float32) + norm_back(
        d_two, normed_two, factor_two, gain_two_f
    )
    d_branch = d_middle.astype(jnp.bfloat16)
    out_grad = weight_grad(d_branch, attn_low)
    d_attn = split_heads(project(d_branch, out_full).astype(jnp.bfloat16), head_count)
    d_probs_local = jnp.einsum(
        "shqd,shkd->shqk", d_attn, values_low, preferred_element_type=jnp.float32
    )
    row_delta = jnp.sum(d_attn.astype(jnp.float32) * (attn_acc + attn_rest), axis=-1)
    zero_factor = jnp.zeros(factors.shape, jnp.float32)
    zero_bar = jnp.zeros(query_bar.shape, jnp.float32)

    def back_hop(back_step, loop_state):
        carry_keys, carry_values, carry_factor, d_bar, d_factors = loop_state
        hop_step = hop_total - 1 - back_step
        hop_keys, hop_values, hop_factor, query_rot, hop_probs = recall(hop_step)
        d_probs = jnp.einsum(
            "shqd,shkd->shqk", d_attn, hop_values, preferred_element_type=jnp.float32
        )
        d_cross = (hop_probs * (d_probs - row_delta[..., None])).astype(jnp.bfloat16)
        d_rot = (
            jnp.einsum("shqk,shkd->shqd", d_cross, hop_keys, preferred_element_type=jnp.float32)
            * scaling
        )
        d_bar = d_bar + jnp.einsum("shqb,shab->shqa", d_rot, hop_factor, precision=HIGHEST)
        factor_local = jnp.einsum("shqa,shqb->shab", query_bar, d_rot, precision=HIGHEST)
        keys_total = (
            carry_keys
            + jnp.einsum("shqk,shqd->shkd", d_cross, query_rot, preferred_element_type=jnp.float32)
            * scaling
        )
        values_total = carry_values + jnp.einsum(
            "shqk,shqd->shkd",
            hop_probs.astype(jnp.bfloat16),
            d_attn,
            preferred_element_type=jnp.float32,
        )
        factor_total = factor_local + jnp.einsum(
            "shba,shbc->shac", factors, carry_factor, precision=HIGHEST
        )
        d_factors = d_factors + jnp.einsum(
            "shac,shbc->shab", carry_factor, hop_factor, precision=HIGHEST
        )
        carry_keys, carry_values, carry_factor = (
            passed_along(keys_total.astype(jnp.bfloat16), "ctx", -1).astype(keys_total.dtype),
            passed_along(values_total.astype(jnp.bfloat16), "ctx", -1).astype(values_total.dtype),
            passed_along(factor_total.astype(jnp.bfloat16), "ctx", -1).astype(factor_total.dtype),
        )
        return (carry_keys, carry_values, carry_factor, d_bar, d_factors)

    zero_rows = jnp.zeros(key_send.shape, jnp.float32)
    loop_state = lax.fori_loop(
        0, hop_total, back_hop, (zero_rows, zero_rows, zero_factor, zero_bar, zero_factor)
    )
    carry_keys, carry_values, d_bar, d_factors = (
        loop_state[0],
        loop_state[1],
        loop_state[3],
        loop_state[4],
    )
    d_local = probs_local * (d_probs_local - row_delta[..., None])
    values_sum = carry_values + jnp.einsum(
        "shqk,shqd->shkd", probs_local_low, d_attn, preferred_element_type=jnp.float32
    )
    d_queries, d_keys, d_house, d_betas = local_back((d_local, d_bar, carry_keys, d_factors))
    query_low = join_heads(d_queries.astype(jnp.bfloat16))
    key_low = join_heads(d_keys.astype(jnp.bfloat16))
    value_low = join_heads(values_sum.astype(jnp.bfloat16))
    house_low = join_heads(d_house.astype(jnp.bfloat16))
    beta_low = d_betas.transpose(0, 2, 1).astype(jnp.bfloat16)
    query_grad = weight_grad(h_one, query_low)
    key_grad = weight_grad(h_one, key_low)
    value_grad = weight_grad(h_one, value_low)
    house_grad = weight_grad(h_one, house_low)
    beta_grad = weight_grad(h_one, beta_low)
    partial_one = (
        project_back(query_low, query_full)
        + project_back(key_low, key_full)
        + project_back(value_low, value_full)
    )
    partial_one = (
        partial_one + project_back(house_low, house_full) + project_back(beta_low, beta_full)
    )
    d_one = lax.psum(partial_one.astype(jnp.bfloat16), "tp").astype(jnp.float32)
    gain_one_grad = jnp.sum(d_one * normed_one, axis=(0, 1))
    input_grad = (d_middle + norm_back(d_one, normed_one, factor_one, gain_one_f)).astype(
        jnp.bfloat16
    )

    def scattered(partial):
        first = lax.psum_scatter(partial, "fsdp", scatter_dimension=0, tiled=True)
        return lax.psum_scatter(first, "ctx", scatter_dimension=0, tiled=True)

    results = tuple(
        (
            scattered(gain_one_grad.astype(jnp.bfloat16)).astype(jnp.float32),
            scattered(query_grad.astype(jnp.bfloat16)).astype(jnp.float32),
            scattered(key_grad.astype(jnp.bfloat16)).astype(jnp.float32),
            scattered(value_grad.astype(jnp.bfloat16)).astype(jnp.float32),
            scattered(house_grad.astype(jnp.bfloat16)).astype(jnp.float32),
            scattered(beta_grad.astype(jnp.bfloat16)).astype(jnp.float32),
            scattered(out_grad.astype(jnp.bfloat16)).astype(jnp.float32),
            scattered(gain_two_grad.astype(jnp.bfloat16)).astype(jnp.float32),
            scattered(gate_grad.astype(jnp.bfloat16)).astype(jnp.float32),
            scattered(up_grad.astype(jnp.bfloat16)).astype(jnp.float32),
            scattered(down_grad.astype(jnp.bfloat16)).astype(jnp.float32),
        )
    )
    return (block_out, input_grad) + results


def halves(value):
    high = value.astype(jnp.bfloat16)
    return high, (value - high.astype(jnp.float32)).astype(jnp.bfloat16)


AB = (((1,), (0,)), ((), ()))
ABT = (((1,), (1,)), ((), ()))
ATB = (((0,), (0,)), ((), ()))


def mm(a, b, dims=AB):
    return lax.dot_general(a, b, dims, preferred_element_type=jnp.float32)


def mm3(a, b, dims=AB):
    return mm(a[0], b[0], dims) + (mm(a[1], b[0], dims) + mm(a[0], b[1], dims))


def unit_lower_inverse(strict, row, col):
    size = strict.shape[0]
    inverse = jnp.where(row == col, 1.0, 0.0) - jnp.where(
        (row >> 1) == (col >> 1), strict, 0.0
    )
    level = 1
    while (1 << level) < size:
        joined = ((row >> (level + 1)) == (col >> (level + 1))) & ((row >> level) != (col >> level))
        parts = halves(inverse)
        step = mm3(halves(jnp.where(joined, strict, 0.0)), parts)
        inverse = inverse - mm3(parts, halves(step))
        level += 1
    return inverse


def unit_rows(raw):
    norm = lax.rsqrt(jnp.sum(raw * raw, axis=1, keepdims=True) + EPSILON)
    return raw * norm, norm


def key_half(house_raw, keys, betas, row, col):
    house, _ = unit_rows(house_raw)
    scaled, w, k = halves(betas * house), halves(house), halves(keys)
    strict = jnp.where(row > col, mm3(scaled, w, ABT), 0.0)
    house_key = jnp.where(row > col, mm3(scaled, k, ABT), 0.0)
    inverse = unit_lower_inverse(strict, row, col)
    return inverse, mm3(halves(inverse), halves(house_key))


def query_half(queries, values, house_raw, keys, inverse, key_side, allowed, row, col):
    house, _ = unit_rows(house_raw)
    q, k, w = halves(queries), halves(keys), halves(house)
    query_house = halves(jnp.where(row >= col, mm3(q, w, ABT), 0.0))
    scores = mm3(q, k, ABT) - mm3(query_house, halves(key_side))
    masked = jnp.where(allowed, scores * (1.0 / math.sqrt(queries.shape[1])), NEGATIVE)
    weights = jnp.exp(masked - jnp.max(masked, axis=1, keepdims=True))
    probs = weights / jnp.sum(weights, axis=1, keepdims=True)
    attn = mm(probs.astype(jnp.bfloat16), values)
    return attn, probs, mm3(query_house, halves(inverse))


def head_backward(
    queries, keys, house_raw, values, betas, probs, key_side, query_side, d_attn, row, col
):
    house, norm = unit_rows(house_raw)
    scaling = 1.0 / math.sqrt(queries.shape[1])
    d_values = mm(probs.astype(jnp.bfloat16), d_attn, ATB)
    d_probs = mm(d_attn, values, ABT)
    row_delta = jnp.sum(probs * d_probs, axis=1, keepdims=True)
    d_scores = halves(probs * (d_probs - row_delta) * scaling)
    q, k, w, scaled = halves(queries), halves(keys), halves(house), halves(betas * house)
    side = halves(query_side)
    d_side = -mm3(d_scores, halves(key_side), ABT)
    d_query_house = halves(jnp.where(row >= col, d_side, 0.0))
    d_strict = halves(jnp.where(row > col, -mm3(side, halves(d_side), ATB), 0.0))
    d_house_key = halves(jnp.where(row > col, -mm3(side, d_scores, ATB), 0.0))
    d_queries = mm3(d_scores, k) + mm3(d_query_house, w)
    d_keys = mm3(d_scores, q, ATB) + mm3(d_house_key, scaled, ATB)
    d_scaled = mm3(d_strict, w) + mm3(d_house_key, k)
    d_house = mm3(d_strict, scaled, ATB) + mm3(d_query_house, q, ATB)
    d_betas = jnp.sum(d_scaled * house, axis=1, keepdims=True)
    d_house = d_house + betas * d_scaled
    d_house_raw = norm * (d_house - house * jnp.sum(d_house * house, axis=1, keepdims=True))
    d_logits = d_betas * betas * (1.0 - 0.5 * betas)
    return d_queries, d_keys, d_house_raw, d_values, d_logits


def started(pairs, sems):
    copies = [
        pltpu.make_async_copy(source, target, sems.at[n]) for n, (source, target) in enumerate(pairs)
    ]
    for copy in copies:
        copy.start()
    return copies


def token_rows(places, n, k, quarter):
    return pl.ds(pl.multiple_of(places[8 + n] + places[18 + k], 16), quarter)


def placed(gathered, whole, places):
    quarter = gathered.shape[1] // 4
    return [
        (
            gathered.at[n, pl.ds(k * quarter, quarter)],
            whole.at[pl.ds(pl.multiple_of(places[18 + k] + n * quarter, 16), quarter)],
        )
        for n in range(4)
        for k in range(4)
    ]


def split_tokens(whole, parts, places):
    quarter = parts[0].shape[0] // 4
    for n in range(4):
        for k in range(4):
            parts[n][pl.ds(k * quarter, quarter)] = whole[token_rows(places, n, k, quarter)]


def wide_row(row, rows):
    return jnp.broadcast_to(row, (rows, row.shape[1])).astype(jnp.bfloat16)


def own_blocks(places, source, target, sequence=26, at=0):
    quarter = target.shape[-2]
    rows = pl.ds(pl.multiple_of(places[22], 16), quarter)
    return [(source.at[places[sequence + k], rows], target.at[k + at]) for k in range(4)]


def message_kernel(places, hidden_in, ids, gain_one, gain_two, *refs):
    messages, blocks, sems = refs[0:4], refs[4], refs[5]
    quarter, features = blocks.shape[1], blocks.shape[2]
    rows, depth = ids.shape[1], gain_one.shape[0]
    copies = started(own_blocks(places, hidden_in, blocks), sems)
    for k in range(4):
        messages[k][:, features:] = jnp.zeros((quarter, 640), jnp.bfloat16)
        own_ids = ids[pl.ds(places[26 + k], 1)].astype(jnp.float32)
        messages[k][:, features : features + rows] = wide_row(own_ids, quarter)
        at = features + 128
        messages[k][:, at : at + depth] = wide_row(gain_one[...].astype(jnp.float32)[None], quarter)
        at += 256
        messages[k][:, at : at + depth] = wide_row(gain_two[...].astype(jnp.float32)[None], quarter)
    for copy in copies:
        copy.wait()
    for k in range(4):
        messages[k][:, :features] = blocks[k]


def attention_pack_kernel(places, house, key, beta, query, value, out, first, second):
    for target, sources in ((first, (house, key, beta)), (second, (query, value, out))):
        at = 0
        for source in sources:
            width = source.shape[1]
            if width < 128:
                target[:, at : at + 128] = jnp.zeros((target.shape[0], 128), jnp.bfloat16)
            target[:, at : at + width] = source[...]
            at += width


def feed_forward_pack_kernel(places, output_grad, gate, up, down, *refs):
    messages, give, keep, blocks, sems = refs[0:4], refs[4], refs[5], refs[6], refs[7]
    copies = started(
        own_blocks(places, output_grad, blocks) + own_blocks(places, output_grad, blocks, 30, 4), sems
    )
    units = gate.shape[1] // 2
    for pack, start in ((keep, places[23]), (give, places[24])):
        for n, source in enumerate((gate, up, down)):
            pack[:, n * units : (n + 1) * units] = source[:, pl.ds(pl.multiple_of(start, 128), units)]
    for copy in copies:
        copy.wait()
    for k in range(4):
        messages[k][0] = blocks[k]
        messages[k][1] = blocks[4 + k]


def result_kernel(places, d_parts, *refs):
    out_parts, (middle, d_middle, x, factor, gain, gain_two_grad) = refs[0:4], refs[4:10]
    messages = refs[10:14]
    quarter, features = x.shape[0] // 4, x.shape[1]
    d_one = sum(d_parts[n].astype(jnp.float32) for n in range(4))
    normed = x[...] * factor[...]
    scaled = d_one * gain[...]
    mean = jnp.mean(scaled * normed, axis=1, keepdims=True)
    in_grad = (d_middle[...] + factor[...] * (scaled - normed * mean)).astype(jnp.bfloat16)
    gain_one_grad = jnp.sum(d_one * normed, axis=0, keepdims=True)
    out = sum(part[...].astype(jnp.float32) for part in out_parts)
    out_own, out_pair = (middle[...] + out[0]).astype(jnp.bfloat16), out[1].astype(jnp.bfloat16)
    row = lax.broadcasted_iota(jnp.int32, (3 * quarter, 128), 0)
    gains, count = jnp.zeros((3 * quarter, 128), jnp.float32), features // 128
    for n in range(count):
        lanes = slice(n * 128, (n + 1) * 128)
        gains = jnp.where(row == n, gain_one_grad[:, lanes], gains)
        gains = jnp.where(row == count + n, gain_two_grad[:, lanes], gains)
    gains = gains.astype(jnp.bfloat16)
    for k in range(4):
        own, pair = slice(k * quarter, (k + 1) * quarter), (k ^ 2) * quarter
        messages[k][:quarter, :features] = in_grad[own]
        messages[k][quarter : 2 * quarter, :features] = out_own[own]
        messages[k][2 * quarter :, :features] = out_pair[pair : pair + quarter]
        messages[k][:, features:] = gains


def owner_kernel(places, *refs):
    messages, owned = refs[0:4], refs[4]
    quarter, features = messages[0].shape[0] // 3, messages[0].shape[1] - 128
    for k in range(4):
        owned[k * quarter : (k + 1) * quarter, :features] = messages[k][:quarter, :features]
        out = messages[k][quarter : 2 * quarter, :features].astype(jnp.float32)
        out = out + messages[k ^ 2][2 * quarter :, :features].astype(jnp.float32)
        owned[(4 + k) * quarter : (5 + k) * quarter, :features] = out.astype(jnp.bfloat16)
    gains = sum(message[:, features:].astype(jnp.float32) for message in messages)
    owned[: 3 * quarter, features:] = gains.astype(jnp.bfloat16)
    owned[3 * quarter :, features:] = jnp.zeros((5 * quarter, 128), jnp.bfloat16)


def spread_kernel(places, *refs):
    pieces, out, grad, gains = refs[0:4], refs[4], refs[5], refs[6]
    quarter, features = out.shape[1] // 4, out.shape[2]
    for n in range(4):
        rows = pl.ds(pl.multiple_of(places[8 + n], 16), quarter)
        for k in range(4):
            at = pl.ds(places[26 + k], 1)
            grad[at, rows] = pieces[n][k * quarter : (k + 1) * quarter, :features][None]
            out[at, rows] = pieces[n][(4 + k) * quarter : (5 + k) * quarter, :features][None]
    gains[...] = sum(piece[: 3 * quarter, features:].astype(jnp.float32) for piece in pieces)


def weights_in_place(pieces, whole, places, first=0, count=None):
    depth = pieces[0].shape[0]
    width = count or pieces[0].shape[1]
    return [
        (
            pieces[n].at[:, pl.ds(first, width)],
            whole.at[pl.ds(pl.multiple_of(places[n], 64), depth), pl.ds(0, width)],
        )
        for n in range(8)
    ]


def keys_kernel(heads, places, *refs):
    weights, xs, gain = refs[0:8], refs[8], refs[9]
    h_all, proj, inverses, key_side = refs[10:14]
    w_all, weight_sems, x_sems, x_all = refs[14:18]
    x_copies = started(placed(xs, x_all, places), x_sems)
    w_copies = started(weights_in_place(weights, w_all, places), weight_sems)
    for copy in x_copies:
        copy.wait()
    width = (proj.shape[1] - 128) // 2
    head = width // heads
    x = x_all[...].astype(jnp.float32)
    factor = lax.rsqrt(jnp.mean(x * x, axis=1, keepdims=True) + EPSILON)
    h_all[...] = (x * factor * gain[...]).astype(jnp.bfloat16)
    for copy in w_copies:
        copy.wait()
    proj[...] = mm(h_all[...], w_all[...])
    length = h_all.shape[0]
    row = lax.broadcasted_iota(jnp.int32, (length, length), 0)
    col = lax.broadcasted_iota(jnp.int32, (length, length), 1)
    betas = 2.0 * jax.nn.sigmoid(proj[:, 2 * width :])
    for n in range(heads):
        inverses[n], key_side[n] = key_half(
            proj[:, n * head : (n + 1) * head],
            proj[:, width + n * head : width + (n + 1) * head],
            betas[:, n : n + 1],
            row,
            col,
        )


def queries_kernel(heads, places, *refs):
    weights, (h_all, proj_keys, inverses, key_side, id_row, id_col) = refs[0:8], refs[8:14]
    proj, attn, probs, query_side, parts = refs[14], refs[15], refs[16], refs[17], refs[18:22]
    w_all, total, sems = refs[22:25]
    for copy in started(weights_in_place(weights, w_all, places), sems):
        copy.wait()
    width = attn.shape[1]
    head = width // heads
    proj[...] = mm(h_all[...], w_all[:, : 2 * width])
    length = h_all.shape[0]
    row = lax.broadcasted_iota(jnp.int32, (length, length), 0)
    col = lax.broadcasted_iota(jnp.int32, (length, length), 1)
    allowed = (col <= row) & (id_row[...] == id_col[...])
    for n in range(heads):
        out, probs[n], query_side[n] = query_half(
            proj[:, n * head : (n + 1) * head],
            proj[:, width + n * head : width + (n + 1) * head].astype(jnp.bfloat16),
            proj_keys[:, n * head : (n + 1) * head],
            proj_keys[:, width + n * head : width + (n + 1) * head],
            inverses[n],
            key_side[n],
            allowed,
            row,
            col,
        )
        attn[:, n * head : (n + 1) * head] = out.astype(jnp.bfloat16)
    total[...] = mm(attn[...], w_all[:, 2 * width :], ABT).astype(jnp.bfloat16)
    split_tokens(total, parts, places)


def feed_forward_kernel(places, *refs):
    weights, ins, grads = refs[0:8], refs[8:10], refs[10:14]
    two_parts, out_parts, keeps, sends = refs[14:22], refs[22:26], refs[26], refs[27]
    w_all, in_all, grad_all, total, weight_sems, in_sems, grad_sems = refs[28:35]
    rows, units, half = two_parts[0].shape[0], w_all.shape[1] // 3, w_all.shape[0] // 2

    def block(s, n):
        return pl.ds(pl.multiple_of(places[8 + n] * 4 + s * 4 * rows, 64), rows)

    w_copies = started(weights_in_place(weights, w_all, places), weight_sems)
    grad_copies = started(
        [
            (grads[n].at[s], grad_all.at[block(s, n)])
            for n in range(4)
            for s in range(2)
        ],
        grad_sems,
    )
    in_copies = started(
        [(ins[s].at[n], in_all.at[pl.ds((s * 4 + n) * rows, rows)]) for s in range(2) for n in range(4)],
        in_sems,
    )
    for copy in w_copies + grad_copies + in_copies:
        copy.wait()
    both = mm(in_all[...], w_all[:, : 2 * units])
    d_hidden = mm(grad_all[...], w_all[:, 2 * units :])
    gate, up = both[:, :units], both[:, units:]
    sigmoid = jax.nn.sigmoid(gate)
    silu = gate * sigmoid
    hidden = (silu * up).astype(jnp.bfloat16)
    d_gate = (d_hidden * up * sigmoid * (1.0 + gate * (1.0 - sigmoid))).astype(jnp.bfloat16)
    d_up = (d_hidden * silu).astype(jnp.bfloat16)
    for target in (keeps, sends):
        at = 2 * half
        for value in (d_gate, d_up, hidden):
            target[:, at : at + units] = value
            at += units
    d_both = keeps[:, 2 * half : 2 * half + 2 * units]
    total[...] = mm(d_both, w_all[:, : 2 * units], ABT).astype(jnp.bfloat16)
    for s in range(2):
        for n in range(4):
            two_parts[s * 4 + n][...] = total[block(s, n)]
    total[...] = mm(hidden, w_all[:, 2 * units :], ABT).astype(jnp.bfloat16)
    for s in range(2):
        for n in range(4):
            out_parts[n][s] = total[block(s, n)]
    for target, place in ((keeps, 12), (sends, 13)):
        lanes = pl.ds(pl.multiple_of(places[place], 128), half)
        target[:, :half] = in_all[:, lanes]
        target[:, half : 2 * half] = grad_all[:, lanes]


def attention_backward_kernel(heads, places, *refs):
    first, second, ds = refs[0:8], refs[8:16], refs[16]
    proj_keys, proj, probs, key_side, query_side, h_all, attn = refs[17:24]
    keeps, sends, parts = refs[24:27]
    w_first, w_second, d_all, d_attn, total, first_sems, second_sems, d_sems = refs[27:35]
    half, width = d_all.shape[1] // 2, d_attn.shape[1]
    d_keys_all = keeps.at[:, pl.ds(2 * half, 2 * width + 128)]
    d_queries_all = keeps.at[:, pl.ds(2 * half + 2 * width + 128, 2 * width)]
    second_copies = started(weights_in_place(second, w_second, places), second_sems)
    d_copies = started(placed(ds, d_all, places), d_sems)
    first_copies = started(weights_in_place(first, w_first, places), first_sems)
    for copy in d_copies + second_copies:
        copy.wait()
    head = width // heads
    d_attn[...] = mm(d_all[...], w_second[:, 2 * width :]).astype(jnp.bfloat16)
    length = d_all.shape[0]
    row = lax.broadcasted_iota(jnp.int32, (length, length), 0)
    col = lax.broadcasted_iota(jnp.int32, (length, length), 1)
    betas = 2.0 * jax.nn.sigmoid(proj_keys[:, 2 * width :])
    lane = lax.broadcasted_iota(jnp.int32, betas.shape, 1)
    logits = jnp.zeros(betas.shape, jnp.float32)
    for n in range(heads):
        low_at, high_at = slice(n * head, (n + 1) * head), slice(width + n * head, width + (n + 1) * head)
        d_queries, d_keys, d_house, d_values, d_logit = head_backward(
            proj[:, low_at],
            proj_keys[:, high_at],
            proj_keys[:, low_at],
            proj[:, high_at].astype(jnp.bfloat16),
            betas[:, n : n + 1],
            probs[n],
            key_side[n],
            query_side[n],
            d_attn[:, low_at],
            row,
            col,
        )
        d_keys_all[:, low_at] = d_house.astype(jnp.bfloat16)
        d_keys_all[:, high_at] = d_keys.astype(jnp.bfloat16)
        d_queries_all[:, low_at] = d_queries.astype(jnp.bfloat16)
        d_queries_all[:, high_at] = d_values.astype(jnp.bfloat16)
        logits = jnp.where(lane == n, d_logit, logits)
    d_keys_all[:, 2 * width :] = logits.astype(jnp.bfloat16)
    for copy in first_copies:
        copy.wait()
    keeps[:, keeps.shape[1] - width :] = attn[...]
    sends[:, 2 * half :] = keeps[:, 2 * half :]
    for target, place in ((keeps, 12), (sends, 13)):
        lanes = pl.ds(pl.multiple_of(places[place], 128), half)
        target[:, :half] = h_all[:, lanes]
        target[:, half : 2 * half] = d_all[:, lanes]
    total[...] = (
        mm(d_keys_all[...], w_first[...], ABT) + mm(d_queries_all[...], w_second[:, : 2 * width], ABT)
    ).astype(jnp.bfloat16)
    quarter = parts.shape[1] // 4
    for n in range(4):
        for k in range(4):
            rows = pl.ds(pl.multiple_of(places[18 + k] + n * quarter, 16), quarter)
            parts[n, k * quarter : (k + 1) * quarter] = total[rows]


def weight_grad_kernel(groups, places, mine, came, near, far, total):
    half, at = total.shape[0], 0
    for left, start, width in groups:
        lefts, rights = slice(left * half, (left + 1) * half), slice(start, start + width)
        total[:, at : at + width] = (
            mm(mine[:, lefts], mine[:, rights], ATB) + mm(came[:, lefts], came[:, rights], ATB)
        ).astype(jnp.bfloat16)
        at += width
    depth = near.shape[1]
    for n, target in enumerate((near.at[0], far.at[0], near.at[1], far.at[1])):
        target[...] = total[pl.ds(pl.multiple_of(places[14 + n], 64), depth)]


VMEM_BYTES = 56 * 1024 * 1024


def call(kernel, outs, scratch, places, operands, spaces, micros, out_spaces=None):
    vmem = pl.BlockSpec(memory_space=pltpu.VMEM)
    kinds = {"v": vmem, "a": pl.BlockSpec(memory_space=pl.ANY)}
    return pl.pallas_call(
        kernel,
        out_shape=[jax.ShapeDtypeStruct(shape, kind) for shape, kind in outs],
        in_specs=[pl.BlockSpec(memory_space=pltpu.SMEM)] + [kinds[s] for s in spaces],
        out_specs=[kinds[s] for s in out_spaces or "v" * len(outs)],
        scratch_shapes=scratch,
        compiler_params=pltpu.CompilerParams(vmem_limit_bytes=VMEM_BYTES),
        cost_estimate=pl.CostEstimate(
            flops=int(micros * 1.1e9), transcendentals=0, bytes_accessed=int(micros * 3.6e6)
        ),
    )(places, *operands)


def swap(block, axis, distance):
    size = lax.axis_size(axis)
    return lax.ppermute(block, axis, [(i, i ^ distance) for i in range(size)])


def gathered_tp(block):
    return lax.all_gather(block, "tp", axis=0)


def all_tp(block):
    return [block] + [swap(block, "tp", n) for n in (1, 2, 3)]


def to_owners(messages):
    return [messages[0]] + [swap(messages[n], "ctx", n) for n in (1, 2, 3)]


def sum_tp(parts):
    return [parts[0]] + [swap(parts[n], "tp", n) for n in (1, 2, 3)]


def add_up(blocks):
    total = blocks[0].astype(jnp.float32)
    for block in blocks[1:]:
        total = total + block.astype(jnp.float32)
    return total


def other_core(block):
    return swap(block, "fsdp", 1)


def whole_sequences(
    hidden_in,
    segment_ids,
    doc_starts,
    norm1_gain,
    w_query,
    w_key,
    w_value,
    w_house,
    w_beta,
    w_out,
    norm2_gain,
    w_gate,
    w_up,
    w_down,
    output_grad,
):
    low, wide = jnp.bfloat16, jnp.float32
    core, chain, column = lax.axis_index("fsdp"), lax.axis_index("ctx"), lax.axis_index("tp")
    rows, features = hidden_in.shape[1], hidden_in.shape[2]
    depth, width, heads = w_query.shape[0], w_query.shape[1], w_beta.shape[1]
    length, half, quarter = 4 * rows, features // 2, rows // 4
    units, used = w_gate.shape[1] // 2, 4 * width + 128
    near = jnp.arange(4, dtype=jnp.int32)
    upper = (chain // 2).astype(jnp.int32)
    places = jnp.concatenate(
        [
            (core * 4 + (chain ^ near)) * depth,
            ((1 - core) * 4 + (chain ^ near)) * depth,
            (column ^ near) * quarter,
            jnp.stack([core, 1 - core]) * half,
            (chain ^ near) * depth,
            (chain ^ near) * rows,
            jnp.stack([column * quarter, upper * units, (1 - upper) * units, upper]),
            chain ^ near,
            chain ^ near ^ 2,
        ]
    ).astype(jnp.int32)
    step = lax.optimization_barrier
    block = pltpu.VMEM((4, quarter, features), low)
    token_messages = call(
        message_kernel,
        [((quarter, features + 640), low)] * 4,
        [block, pltpu.SemaphoreType.DMA((4,))],
        places,
        [hidden_in, segment_ids, norm1_gain, norm2_gain],
        "avvv",
        2,
    )
    first, second = call(
        attention_pack_kernel,
        [((depth, 2 * width + 128), low), ((depth, 3 * width), low)],
        [],
        places,
        [w_house, w_key, w_beta, w_query, w_value, w_out],
        "v" * 6,
        2,
    )
    packed = call(
        feed_forward_pack_kernel,
        [((2, quarter, features), low)] * 4 + [((depth, 3 * units), low)] * 2,
        [pltpu.VMEM((8, quarter, features), low), pltpu.SemaphoreType.DMA((8,))],
        places,
        [output_grad, w_gate, w_up, w_down],
        "avvv",
        3,
    )
    grad_messages, give, keep = packed[:4], packed[4], packed[5]
    x_messages, first, second, grad_messages, give, keep = step(
        (to_owners(token_messages), first, second, grad_messages, give, keep)
    )

    first_two, first_one = swap(first, "ctx", 2), swap(first, "ctx", 1)
    x_block = jnp.concatenate([message[:, :features] for message in x_messages])
    x_pieces = gathered_tp(x_block)
    info = jnp.stack([message[0, features:] for message in x_messages])
    chosen = near[:, None] == (near[None, :] ^ chain)
    info = jnp.sum(jnp.where(chosen[:, :, None], info[None].astype(wide), 0.0), axis=1)
    ids = info[:, :rows].reshape(length)
    gains = jnp.concatenate(
        [info[:, 128 : 128 + depth], info[:, 384 : 384 + depth]], axis=1
    ).astype(low)
    first_two, first_one, x_pieces, first, gains, grad_messages = step(
        (first_two, first_one, x_pieces, first, gains, grad_messages)
    )

    first_three = swap(first_two, "ctx", 1)
    grad_messages = to_owners(grad_messages)
    first_others = [other_core(piece) for piece in (first, first_one, first_two)]
    gains_other = other_core(gains)
    gains = jnp.where(core == 0, jnp.stack([gains, gains_other]), jnp.stack([gains_other, gains]))
    gain_one = gains[:, :, :depth].reshape(1, features).astype(wide)
    gain_two = gains[:, :, depth:].reshape(1, features).astype(wide)
    first_three, first_others, grad_messages, gain_one, second = step(
        (first_three, first_others, grad_messages, gain_one, second)
    )
    key_weights = [first, first_one, first_two, first_three, *first_others, other_core(first_three)]
    grads = jnp.stack(
        [
            jnp.concatenate([message[0] for message in grad_messages]),
            jnp.concatenate([grad_messages[n ^ 2][1] for n in range(4)]),
        ]
    )
    own_grad = grads[0]

    second_two, second_one = swap(second, "ctx", 2), swap(second, "ctx", 1)
    grad_pieces = all_tp(grads)
    square = ((heads, length, length), wide)
    h_all, proj_keys, inverses, key_side = call(
        functools.partial(keys_kernel, heads),
        [((length, features), low), ((length, 2 * width + 128), wide), square, square],
        [
            pltpu.VMEM((features, 2 * width + 128), low),
            pltpu.SemaphoreType.DMA((8,)),
            pltpu.SemaphoreType.DMA((16,)),
            pltpu.VMEM((length, features), low),
        ],
        places,
        [*key_weights, x_pieces, gain_one],
        "a" * 9 + "v",
        20,
    )
    second_two, second_one, grad_pieces, proj_keys, second = step(
        (second_two, second_one, grad_pieces, proj_keys, second)
    )
    second_three = swap(second_two, "ctx", 1)
    second_others = [other_core(piece) for piece in (second, second_one, second_two)]
    second_three, second_others, proj_keys, give, keep = step(
        (second_three, second_others, proj_keys, give, keep)
    )
    query_weights = [
        second, second_one, second_two, second_three, *second_others, other_core(second_three)
    ]

    give_two, keep_one = swap(give, "ctx", 2), swap(keep, "ctx", 1)
    outs = call(
        functools.partial(queries_kernel, heads),
        [((length, 2 * width), wide), ((length, width), low), square, square]
        + [((rows, features), low)] * 4,
        [
            pltpu.VMEM((features, 3 * width), low),
            pltpu.VMEM((length, features), low),
            pltpu.SemaphoreType.DMA((8,)),
        ],
        places,
        [*query_weights, h_all, proj_keys, inverses, key_side, ids[None, :], ids[:, None]],
        "a" * 8 + "v" * 6,
        9,
    )
    proj, attn, probs, query_side = outs[:4]
    residual = x_block.astype(wide)
    normed_one, factor_one = norm_rows(residual)
    middle = residual + add_up(sum_tp(outs[4:]))
    normed_two, factor_two = norm_rows(middle)
    h_two = (normed_two * gain_two).astype(low)
    give_two, keep_one, keep, h_two = step((give_two, keep_one, keep, h_two))

    h_pair, keep_three = swap(h_two, "ctx", 2), swap(give_two, "ctx", 1)
    h_own = gathered_tp(h_two)
    h_pair, keep_three, h_own, keep, keep_one, give_two = step(
        (h_pair, keep_three, h_own, keep, keep_one, give_two)
    )
    ffn_weights = [keep, keep_one, give_two, keep_three]
    ffn_weights = ffn_weights + [other_core(piece) for piece in ffn_weights]
    h_pair = gathered_tp(h_pair)

    tokens = 2 * length
    pair = ((2, rows, features), low)
    outs = call(
        feed_forward_kernel,
        [((rows, features), low)] * 8 + [pair] * 4 + [((tokens, features + 3 * units), low)] * 2,
        [
            pltpu.VMEM((features, 3 * units), low),
            pltpu.VMEM((tokens, features), low),
            pltpu.VMEM((tokens, features), low),
            pltpu.VMEM((tokens, features), low),
            pltpu.SemaphoreType.DMA((8,)),
            pltpu.SemaphoreType.DMA((8,)),
            pltpu.SemaphoreType.DMA((8,)),
        ],
        places,
        [*ffn_weights, h_own, h_pair, *grad_pieces],
        "a" * 14,
        12,
    )
    own_parts, pair_parts, out_parts, keeps, sends = outs[:4], outs[4:8], outs[8:12], outs[12], outs[13]

    def grads_of(mine, came, groups):
        total = sum(group[2] for group in groups)
        return call(
            functools.partial(weight_grad_kernel, groups),
            [((2, depth, total), low)] * 2,
            [pltpu.VMEM((half, total), low)],
            places,
            [mine, came],
            "vv",
            total / 400.0,
        )

    pair_sum = add_up(sum_tp(pair_parts)).astype(low)
    came, pair_sum, own_parts = step((other_core(sends), pair_sum, own_parts))

    two_other = swap(pair_sum, "ctx", 2)
    own_sum = add_up(sum_tp(own_parts))
    ffn_near, ffn_far = grads_of(
        keeps, came, ((0, features, 2 * units), (1, features + 2 * units, units))
    )
    d_two = own_sum + two_other.astype(wide)
    gain_two_grad = jnp.sum(d_two * normed_two, axis=0)
    d_middle = own_grad.astype(wide) + norm_back(d_two, normed_two, factor_two, gain_two)
    d_low, ffn_near, ffn_far = step((d_middle.astype(low), ffn_near, ffn_far))

    ffn_came = swap(ffn_far, "ctx", 1)
    d_pieces = gathered_tp(d_low)
    d_pieces, out_parts = step((d_pieces, out_parts))
    out_received = sum_tp(out_parts)
    back = call(
        functools.partial(attention_backward_kernel, heads),
        [((length, features + used + width), low)] * 2 + [((4, rows, features), low)],
        [
            pltpu.VMEM((features, 2 * width + 128), low),
            pltpu.VMEM((features, 3 * width), low),
            pltpu.VMEM((length, features), low),
            pltpu.VMEM((length, width), low),
            pltpu.VMEM((length, features), low),
            pltpu.SemaphoreType.DMA((8,)),
            pltpu.SemaphoreType.DMA((8,)),
            pltpu.SemaphoreType.DMA((16,)),
        ],
        places,
        [*key_weights, *query_weights, d_pieces, proj_keys, proj, probs, key_side, query_side, h_all, attn],
        "a" * 17 + "v" * 7,
        14,
    )
    ffn_sum = add_up([ffn_near, ffn_came])
    ffn_leave, out_received, (keeps, sends, d_parts) = step(
        (ffn_sum[1].astype(low), out_received, tuple(back))
    )

    ffn_other = swap(ffn_leave, "ctx", 2)
    came = other_core(sends)
    query_start = features + 2 * width + 128
    near_two, far_two = grads_of(
        keeps, came, ((0, query_start, 2 * width), (1, query_start + 2 * width, width))
    )
    two_came = swap(far_two, "ctx", 1)
    near_one, far_one = grads_of(keeps, came, ((0, features, 2 * width + 128),))
    d_received = lax.all_to_all(d_parts, "tp", 0, 0)
    messages = call(
        result_kernel,
        [((3 * quarter, features + 128), low)] * 4,
        [],
        places,
        [
            d_received,
            *out_received,
            middle,
            d_middle,
            residual,
            factor_one,
            gain_one,
            gain_two_grad[None],
        ],
        "v" * 11,
        3,
    )
    two_sum = add_up([near_two, two_came])
    ffn_other, two_leave, near_one, far_one, messages = step(
        (ffn_other, two_sum[1].astype(low), near_one, far_one, messages)
    )

    messages = to_owners(messages)
    one_came = swap(far_one, "ctx", 1)
    query_other = swap(two_leave, "ctx", 2)
    owned = call(
        owner_kernel, [((2 * rows, features + 128), low)], [], places, messages, "v" * 4, 2
    )[0]
    one_sum = add_up([near_one, one_came])
    one_leave, owned, query_other = step((one_sum[1].astype(low), owned, query_other))

    key_other = swap(one_leave, "ctx", 2)
    block_out, input_grad, gain_total = call(
        spread_kernel,
        [((4, rows, features), low)] * 2 + [((3 * quarter, 128), wide)],
        [],
        places,
        all_tp(owned),
        "v" * 4,
        3,
    )
    gain_total = (gain_total + other_core(gain_total))[: features // 64].reshape(2, features)
    gain_total = lax.dynamic_slice_in_dim(gain_total, (core * 4 + chain) * depth, depth, axis=1)
    query_grads = two_sum[0] + query_other.astype(wide)
    key_grads = one_sum[0] + key_other.astype(wide)

    def ffn_result(n):
        kept = ffn_sum[0, :, n * units : (n + 1) * units]
        came = ffn_other[:, n * units : (n + 1) * units].astype(wide)
        return jnp.concatenate(
            [jnp.where(upper == 1, came, kept), jnp.where(upper == 1, kept, came)], axis=1
        )

    return (
        block_out,
        input_grad,
        gain_total[0],
        query_grads[:, :width],
        key_grads[:, width : 2 * width],
        query_grads[:, width : 2 * width],
        key_grads[:, :width],
        key_grads[:, 2 * width : 2 * width + heads],
        query_grads[:, 2 * width :],
        gain_total[1],
        ffn_result(0),
        ffn_result(1),
        ffn_result(2),
    )


def shards(*args):
    sizes = [lax.axis_size(axis) for axis in ("fsdp", "ctx", "tp")]
    if sizes == [2, 4, 4] and args[0].shape[:2] == (4, 64):
        return whole_sequences(*args)
    return ring_of_groups(*args)


def solution(mesh):
    in_specs = (
        P("fsdp", "ctx", None),
        P("fsdp", "ctx"),
        P("fsdp", "ctx"),
        P(("fsdp", "ctx")),
        P(("fsdp", "ctx"), "tp"),
        P(("fsdp", "ctx"), "tp"),
        P(("fsdp", "ctx"), "tp"),
        P(("fsdp", "ctx"), "tp"),
        P(("fsdp", "ctx"), "tp"),
        P(("fsdp", "ctx"), "tp"),
        P(("fsdp", "ctx")),
        P(("fsdp", "ctx"), "tp"),
        P(("fsdp", "ctx"), "tp"),
        P(("fsdp", "ctx"), "tp"),
        P("fsdp", "ctx", None),
    )
    out_specs = (
        P("fsdp", "ctx", None),
        P("fsdp", "ctx", None),
        P(("fsdp", "ctx")),
        P(("fsdp", "ctx"), "tp"),
        P(("fsdp", "ctx"), "tp"),
        P(("fsdp", "ctx"), "tp"),
        P(("fsdp", "ctx"), "tp"),
        P(("fsdp", "ctx"), "tp"),
        P(("fsdp", "ctx"), "tp"),
        P(("fsdp", "ctx")),
        P(("fsdp", "ctx"), "tp"),
        P(("fsdp", "ctx"), "tp"),
        P(("fsdp", "ctx"), "tp"),
    )
    return jax.shard_map(shards, mesh=mesh, in_specs=in_specs, out_specs=out_specs, check_vma=False)
```

```python
import functools
import math

import jax
import jax.numpy as jnp
from jax import lax
from jax.experimental import pallas as pl
from jax.experimental.pallas import tpu as pltpu
from jax.sharding import PartitionSpec as P

EPSILON = 1e-06
HIGHEST = lax.Precision.HIGHEST
NEGATIVE = -1e30


def passed_along(block, axis, distance):
    devices = range(lax.axis_size(axis))
    route = [(i - distance, i) for i in devices if i - distance in devices]
    return lax.ppermute(block, axis, route)


def group_algebra(queries, key_rows, house, betas):
    length = queries.shape[0]
    scaling = 1.0 / math.sqrt(queries.shape[1])
    row_index = lax.broadcasted_iota(jnp.int32, (length, length), 0)
    column_index = lax.broadcasted_iota(jnp.int32, (length, length), 1)
    strict_below = row_index > column_index
    house_gram = jnp.dot(house, house.T, precision=HIGHEST)
    system = jnp.where(strict_below, house_gram, 0.0) + jnp.diag(1.0 / betas)
    identity = jnp.eye(length, dtype=house.dtype)
    inverse = jax.scipy.linalg.solve_triangular(system, identity, lower=True)
    query_house = jnp.where(
        row_index >= column_index, jnp.dot(queries, house.T, precision=HIGHEST), 0.0
    )
    house_key = jnp.where(strict_below, jnp.dot(house, key_rows.T, precision=HIGHEST), 0.0)
    query_side = jnp.dot(query_house, inverse, precision=HIGHEST)
    key_side = jnp.dot(inverse, house_key, precision=HIGHEST)
    scores = (
        jnp.dot(queries, key_rows.T, precision=HIGHEST)
        - jnp.dot(query_side, house_key, precision=HIGHEST)
    ) * scaling
    query_bar = queries - jnp.dot(query_side, house, precision=HIGHEST)
    key_bar = key_rows - jnp.dot(key_side.T, house, precision=HIGHEST)
    inner = jnp.dot(inverse, house, precision=HIGHEST)
    factor = jnp.eye(house.shape[1], dtype=house.dtype) - jnp.dot(house.T, inner, precision=HIGHEST)
    return (scores, query_bar, key_bar, factor)


def local_map(queries, key_rows, house_raw, beta_logits):
    house = house_raw * lax.rsqrt(jnp.sum(house_raw * house_raw, axis=-1, keepdims=True) + EPSILON)
    betas = 2.0 * jax.nn.sigmoid(beta_logits)
    return jax.vmap(jax.vmap(group_algebra))(queries, key_rows, house, betas)


def doc_starts_local(segment_ids, group_first, first_position):
    length = segment_ids.shape[-1]
    previous = jnp.concatenate([segment_ids[..., :1], segment_ids[..., :-1]], axis=-1)
    offsets = lax.broadcasted_iota(jnp.int32, segment_ids.shape, segment_ids.ndim - 1)
    boundary = (offsets > 0) & (segment_ids != previous)
    marks = jnp.where(boundary, offsets + first_position, -1)
    row_index = lax.broadcasted_iota(jnp.int32, (length, length), 0)
    column_index = lax.broadcasted_iota(jnp.int32, (length, length), 1)
    seen = jnp.where(column_index <= row_index, marks[..., None, :], -1)
    return jnp.maximum(jnp.max(seen, axis=-1), group_first)


def norm_rows(values):
    factor = lax.rsqrt(jnp.mean(values * values, axis=-1, keepdims=True) + EPSILON)
    return (values * factor, factor)


def norm_back(gradient, normed, factor, norm_gain):
    scaled = gradient * norm_gain
    return factor * (scaled - normed * jnp.mean(scaled * normed, axis=-1, keepdims=True))


def split_heads(tensor, head_count):
    seq_count, length, total_width = tensor.shape
    return tensor.reshape(seq_count, length, head_count, total_width // head_count).transpose(
        0, 2, 1, 3
    )


def join_heads(tensor):
    seq_count, head_count, length, head_width = tensor.shape
    return tensor.transpose(0, 2, 1, 3).reshape(seq_count, length, head_count * head_width)


def project(inputs, weight):
    return jnp.einsum("scd,df->scf", inputs, weight, preferred_element_type=jnp.float32)


def project_back(gradient, weight):
    return jnp.einsum("scf,df->scd", gradient, weight, preferred_element_type=jnp.float32)


def weight_grad(inputs, gradient):
    return jnp.einsum("scd,scf->df", inputs, gradient, preferred_element_type=jnp.float32)


def cross_scores(query_rot, key_low, scaling):
    return (
        jnp.einsum("shqd,shkd->shqk", query_rot, key_low, preferred_element_type=jnp.float32)
        * scaling
    )


def weighted_values(weights, values_in):
    return jnp.einsum("shqk,shkd->shqd", weights, values_in, preferred_element_type=jnp.float32)


def ring_of_groups(
    hidden_in,
    segment_ids,
    doc_starts,
    norm1_gain,
    w_query,
    w_key,
    w_value,
    w_house,
    w_beta,
    w_out,
    norm2_gain,
    w_gate,
    w_up,
    w_down,
    output_grad,
):
    gathered = (
        lax.all_gather(norm1_gain, ("fsdp", "ctx"), axis=0, tiled=True),
        lax.all_gather(w_query, ("fsdp", "ctx"), axis=0, tiled=True),
        lax.all_gather(w_key, ("fsdp", "ctx"), axis=0, tiled=True),
        lax.all_gather(w_value, ("fsdp", "ctx"), axis=0, tiled=True),
        lax.all_gather(w_house, ("fsdp", "ctx"), axis=0, tiled=True),
        lax.all_gather(w_beta, ("fsdp", "ctx"), axis=0, tiled=True),
        lax.all_gather(w_out, ("fsdp", "ctx"), axis=0, tiled=True),
        lax.all_gather(norm2_gain, ("fsdp", "ctx"), axis=0, tiled=True),
        lax.all_gather(w_gate, ("fsdp", "ctx"), axis=0, tiled=True),
        lax.all_gather(w_up, ("fsdp", "ctx"), axis=0, tiled=True),
        lax.all_gather(w_down, ("fsdp", "ctx"), axis=0, tiled=True),
    )
    (
        gain_one,
        query_full,
        key_full,
        value_full,
        house_full,
        beta_full,
        out_full,
        gain_two,
        gate_full,
        up_full,
        down_full,
    ) = gathered
    gain_one_f = gain_one.astype(jnp.float32)
    gain_two_f = gain_two.astype(jnp.float32)
    head_count = beta_full.shape[1]
    length = hidden_in.shape[1]
    residual = hidden_in.astype(jnp.float32)
    normed_one, factor_one = norm_rows(residual)
    h_one = (normed_one * gain_one_f).astype(jnp.bfloat16)
    queries = split_heads(project(h_one, query_full), head_count)
    key_rows = split_heads(project(h_one, key_full), head_count)
    values_low = split_heads(project(h_one, value_full).astype(jnp.bfloat16), head_count)
    house_raw = split_heads(project(h_one, house_full), head_count)
    beta_logits = project(h_one, beta_full).transpose(0, 2, 1)
    (scores_local, query_bar, key_bar, factors), local_back = jax.vjp(
        local_map, queries, key_rows, house_raw, beta_logits
    )
    scaling = 1.0 / math.sqrt(queries.shape[-1])
    chain_index = lax.axis_index("ctx")
    hop_total = lax.axis_size("ctx") - 1
    first_position = chain_index * length
    starts = doc_starts_local(segment_ids, doc_starts, first_position)
    offsets = jnp.arange(length, dtype=jnp.int32)
    causal = (offsets[None, :] <= offsets[:, None])[None]
    local_mask = (causal & (offsets[None, None, :] + first_position >= starts[:, :, None]))[:, None]

    def hop_mask(distance):
        key_pos = (chain_index - distance) * length + offsets
        return (key_pos[None, None, :] >= starts[:, :, None])[:, None]

    masked_local = jnp.where(local_mask, scores_local, NEGATIVE)
    local_max = jnp.max(masked_local, axis=-1)
    local_sum = jnp.sum(jnp.exp(masked_local - local_max[..., None]), axis=-1)
    key_send = key_bar.astype(jnp.bfloat16)
    identity = jnp.broadcast_to(jnp.eye(factors.shape[-1], dtype=jnp.float32), factors.shape)
    stack_rot = jnp.zeros((hop_total,) + query_bar.shape, jnp.bfloat16)
    stack_factors = jnp.zeros((hop_total,) + factors.shape, jnp.float32)

    def rotate(hop_step, hop_keys, chain, run_max, run_sum):
        query_rot = jnp.einsum("shqa,shab->shqb", query_bar, chain, precision=HIGHEST).astype(
            jnp.bfloat16
        )
        masked = jnp.where(
            hop_mask(hop_step + 1), cross_scores(query_rot, hop_keys, scaling), NEGATIVE
        )
        new_max = jnp.maximum(run_max, jnp.max(masked, axis=-1))
        new_sum = run_sum * jnp.exp(run_max - new_max) + jnp.sum(
            jnp.exp(masked - new_max[..., None]), axis=-1
        )
        return (query_rot, new_max, new_sum)

    stack_keys = jnp.zeros((hop_total,) + key_send.shape, jnp.bfloat16)
    stack_values = jnp.zeros((hop_total,) + values_low.shape, jnp.bfloat16)

    def forward_hop(hop_step, loop_state):
        (
            send_keys,
            send_values,
            send_factor,
            kept_keys,
            kept_values,
            kept_rot,
            kept_factors,
            run_max,
            run_sum,
        ) = loop_state
        got_keys, got_values = passed_along((send_keys, send_values), "ctx", 1)
        got_factor = passed_along(send_factor.astype(jnp.bfloat16), "ctx", 1).astype(
            send_factor.dtype
        )
        query_rot, run_max, run_sum = rotate(hop_step, got_keys, got_factor, run_max, run_sum)
        kept_keys = lax.dynamic_update_index_in_dim(kept_keys, got_keys, hop_step, 0)
        kept_values = lax.dynamic_update_index_in_dim(kept_values, got_values, hop_step, 0)
        kept_rot = lax.dynamic_update_index_in_dim(kept_rot, query_rot, hop_step, 0)
        kept_factors = lax.dynamic_update_index_in_dim(kept_factors, got_factor, hop_step, 0)
        next_factor = jnp.einsum("shab,shbc->shac", factors, got_factor, precision=HIGHEST)
        return (
            got_keys,
            got_values,
            next_factor,
            kept_keys,
            kept_values,
            kept_rot,
            kept_factors,
            run_max,
            run_sum,
        )

    loop_state = lax.fori_loop(
        0,
        hop_total,
        forward_hop,
        (
            key_send,
            values_low,
            identity,
            stack_keys,
            stack_values,
            stack_rot,
            stack_factors,
            local_max,
            local_sum,
        ),
    )
    stack_keys, stack_values, stack_rot, stack_factors = (
        loop_state[3],
        loop_state[4],
        loop_state[5],
        loop_state[6],
    )
    run_max, run_sum = (loop_state[7], loop_state[8])

    def fetch(hop_step):
        return (
            lax.dynamic_index_in_dim(stack_keys, hop_step, 0, keepdims=False),
            lax.dynamic_index_in_dim(stack_values, hop_step, 0, keepdims=False),
        )

    log_total = run_max + jnp.log(run_sum)

    def recall(hop_step):
        hop_keys, hop_values = fetch(hop_step)
        hop_factor = lax.dynamic_index_in_dim(stack_factors, hop_step, 0, keepdims=False)
        query_rot = lax.dynamic_index_in_dim(stack_rot, hop_step, 0, keepdims=False)
        masked = jnp.where(
            hop_mask(hop_step + 1), cross_scores(query_rot, hop_keys, scaling), NEGATIVE
        )
        hop_probs = jnp.exp(masked - log_total[..., None])
        return (hop_keys, hop_values, hop_factor, query_rot, hop_probs)

    probs_local = jnp.exp(masked_local - log_total[..., None])
    probs_local_low = probs_local.astype(jnp.bfloat16)
    attn_acc = weighted_values(probs_local_low, values_low)
    attn_rest = weighted_values(
        (probs_local - probs_local_low.astype(jnp.float32)).astype(jnp.bfloat16), values_low
    )

    def value_hop(hop_step, running):
        total_low, total_rest = running
        hop_keys, hop_values, hop_factor, query_rot, hop_probs = recall(hop_step)
        hop_low = hop_probs.astype(jnp.bfloat16)
        total_low = total_low + weighted_values(hop_low, hop_values)
        total_rest = total_rest + weighted_values(
            (hop_probs - hop_low.astype(jnp.float32)).astype(jnp.bfloat16), hop_values
        )
        return (total_low, total_rest)

    attn_acc, attn_rest = lax.fori_loop(0, hop_total, value_hop, (attn_acc, attn_rest))
    attn_low = join_heads(attn_acc.astype(jnp.bfloat16))
    branch = lax.psum(project_back(attn_low, out_full), "tp")
    middle = residual + branch
    normed_two, factor_two = norm_rows(middle)
    h_two = (normed_two * gain_two_f).astype(jnp.bfloat16)
    gate_proj = project(h_two, gate_full)
    up_proj = project(h_two, up_full)
    gate_sigmoid = jax.nn.sigmoid(gate_proj)
    silu_gate = gate_proj * gate_sigmoid
    hidden_low = (silu_gate * up_proj).astype(jnp.bfloat16)
    mlp_out = lax.psum(project_back(hidden_low, down_full).astype(jnp.bfloat16), "tp").astype(
        jnp.float32
    )
    block_out = (middle + mlp_out).astype(jnp.bfloat16)
    down_grad = weight_grad(output_grad, hidden_low)
    d_hidden = project(output_grad, down_full)
    d_gate = (d_hidden * up_proj * gate_sigmoid * (1.0 + gate_proj * (1.0 - gate_sigmoid))).astype(
        jnp.bfloat16
    )
    d_up = (d_hidden * silu_gate).astype(jnp.bfloat16)
    gate_grad = weight_grad(h_two, d_gate)
    up_grad = weight_grad(h_two, d_up)
    d_two = lax.psum(project_back(d_gate, gate_full) + project_back(d_up, up_full), "tp")
    gain_two_grad = jnp.sum(d_two * normed_two, axis=(0, 1))
    d_middle = output_grad.astype(jnp.float32) + norm_back(
        d_two, normed_two, factor_two, gain_two_f
    )
    d_branch = d_middle.astype(jnp.bfloat16)
    out_grad = weight_grad(d_branch, attn_low)
    d_attn = split_heads(project(d_branch, out_full).astype(jnp.bfloat16), head_count)
    d_probs_local = jnp.einsum(
        "shqd,shkd->shqk", d_attn, values_low, preferred_element_type=jnp.float32
    )
    row_delta = jnp.sum(d_attn.astype(jnp.float32) * (attn_acc + attn_rest), axis=-1)
    zero_factor = jnp.zeros(factors.shape, jnp.float32)
    zero_bar = jnp.zeros(query_bar.shape, jnp.float32)

    def back_hop(back_step, loop_state):
        carry_keys, carry_values, carry_factor, d_bar, d_factors = loop_state
        hop_step = hop_total - 1 - back_step
        hop_keys, hop_values, hop_factor, query_rot, hop_probs = recall(hop_step)
        d_probs = jnp.einsum(
            "shqd,shkd->shqk", d_attn, hop_values, preferred_element_type=jnp.float32
        )
        d_cross = (hop_probs * (d_probs - row_delta[..., None])).astype(jnp.bfloat16)
        d_rot = (
            jnp.einsum("shqk,shkd->shqd", d_cross, hop_keys, preferred_element_type=jnp.float32)
            * scaling
        )
        d_bar = d_bar + jnp.einsum("shqb,shab->shqa", d_rot, hop_factor, precision=HIGHEST)
        factor_local = jnp.einsum("shqa,shqb->shab", query_bar, d_rot, precision=HIGHEST)
        keys_total = (
            carry_keys
            + jnp.einsum("shqk,shqd->shkd", d_cross, query_rot, preferred_element_type=jnp.float32)
            * scaling
        )
        values_total = carry_values + jnp.einsum(
            "shqk,shqd->shkd",
            hop_probs.astype(jnp.bfloat16),
            d_attn,
            preferred_element_type=jnp.float32,
        )
        factor_total = factor_local + jnp.einsum(
            "shba,shbc->shac", factors, carry_factor, precision=HIGHEST
        )
        d_factors = d_factors + jnp.einsum(
            "shac,shbc->shab", carry_factor, hop_factor, precision=HIGHEST
        )
        carry_keys, carry_values, carry_factor = (
            passed_along(keys_total.astype(jnp.bfloat16), "ctx", -1).astype(keys_total.dtype),
            passed_along(values_total.astype(jnp.bfloat16), "ctx", -1).astype(values_total.dtype),
            passed_along(factor_total.astype(jnp.bfloat16), "ctx", -1).astype(factor_total.dtype),
        )
        return (carry_keys, carry_values, carry_factor, d_bar, d_factors)

    zero_rows = jnp.zeros(key_send.shape, jnp.float32)
    loop_state = lax.fori_loop(
        0, hop_total, back_hop, (zero_rows, zero_rows, zero_factor, zero_bar, zero_factor)
    )
    carry_keys, carry_values, d_bar, d_factors = (
        loop_state[0],
        loop_state[1],
        loop_state[3],
        loop_state[4],
    )
    d_local = probs_local * (d_probs_local - row_delta[..., None])
    values_sum = carry_values + jnp.einsum(
        "shqk,shqd->shkd", probs_local_low, d_attn, preferred_element_type=jnp.float32
    )
    d_queries, d_keys, d_house, d_betas = local_back((d_local, d_bar, carry_keys, d_factors))
    query_low = join_heads(d_queries.astype(jnp.bfloat16))
    key_low = join_heads(d_keys.astype(jnp.bfloat16))
    value_low = join_heads(values_sum.astype(jnp.bfloat16))
    house_low = join_heads(d_house.astype(jnp.bfloat16))
    beta_low = d_betas.transpose(0, 2, 1).astype(jnp.bfloat16)
    query_grad = weight_grad(h_one, query_low)
    key_grad = weight_grad(h_one, key_low)
    value_grad = weight_grad(h_one, value_low)
    house_grad = weight_grad(h_one, house_low)
    beta_grad = weight_grad(h_one, beta_low)
    partial_one = (
        project_back(query_low, query_full)
        + project_back(key_low, key_full)
        + project_back(value_low, value_full)
    )
    partial_one = (
        partial_one + project_back(house_low, house_full) + project_back(beta_low, beta_full)
    )
    d_one = lax.psum(partial_one.astype(jnp.bfloat16), "tp").astype(jnp.float32)
    gain_one_grad = jnp.sum(d_one * normed_one, axis=(0, 1))
    input_grad = (d_middle + norm_back(d_one, normed_one, factor_one, gain_one_f)).astype(
        jnp.bfloat16
    )

    def scattered(partial):
        first = lax.psum_scatter(partial, "fsdp", scatter_dimension=0, tiled=True)
        return lax.psum_scatter(first, "ctx", scatter_dimension=0, tiled=True)

    results = tuple(
        (
            scattered(gain_one_grad.astype(jnp.bfloat16)).astype(jnp.float32),
            scattered(query_grad.astype(jnp.bfloat16)).astype(jnp.float32),
            scattered(key_grad.astype(jnp.bfloat16)).astype(jnp.float32),
            scattered(value_grad.astype(jnp.bfloat16)).astype(jnp.float32),
            scattered(house_grad.astype(jnp.bfloat16)).astype(jnp.float32),
            scattered(beta_grad.astype(jnp.bfloat16)).astype(jnp.float32),
            scattered(out_grad.astype(jnp.bfloat16)).astype(jnp.float32),
            scattered(gain_two_grad.astype(jnp.bfloat16)).astype(jnp.float32),
            scattered(gate_grad.astype(jnp.bfloat16)).astype(jnp.float32),
            scattered(up_grad.astype(jnp.bfloat16)).astype(jnp.float32),
            scattered(down_grad.astype(jnp.bfloat16)).astype(jnp.float32),
        )
    )
    return (block_out, input_grad) + results


def halves(value):
    high = value.astype(jnp.bfloat16)
    return high, (value - high.astype(jnp.float32)).astype(jnp.bfloat16)


AB = (((1,), (0,)), ((), ()))
ABT = (((1,), (1,)), ((), ()))
ATB = (((0,), (0,)), ((), ()))


def mm(a, b, dims=AB):
    return lax.dot_general(a, b, dims, preferred_element_type=jnp.float32)


def mm3(a, b, dims=AB):
    left, right = dims[0][0][0], dims[0][1][0]
    return mm(
        jnp.concatenate([a[0], a[1], a[0]], axis=left),
        jnp.concatenate([b[0], b[0], b[1]], axis=right),
        dims,
    )


def each(function, *lists):
    return [function(*values) for values in zip(*lists)]


def square_index(size):
    row = lax.broadcasted_iota(jnp.int32, (size, size), 0)
    return row, lax.broadcasted_iota(jnp.int32, (size, size), 1)


def unit_lower_inverses(strict):
    size = strict[0].shape[0]
    part, half = size // 4, size // 2
    lane = lax.broadcasted_iota(jnp.int32, (part, size), 1)
    row = lax.broadcasted_iota(jnp.int32, (part, size), 0)
    block = lane // part
    col = lane - block * part
    own = [block == b for b in range(4)]
    zero = jnp.zeros((part, size), jnp.bfloat16)

    def side_by_side(matrix, below):
        packed = jnp.zeros((part, size), jnp.float32)
        for b in range(4 - below):
            packed = jnp.where(own[b], matrix[(b + below) * part : (b + below + 1) * part], packed)
        return packed

    def stacked(pair, order=(0, 1, 2, 3)):
        return tuple(
            jnp.concatenate(
                [zero if b is None else jnp.where(own[b], value, zero) for b in order], axis=0
            )
            for value in pair
        )

    diagonal = [side_by_side(matrix, 0) for matrix in strict]
    inverse = [
        jnp.where(row == col, 1.0, 0.0) - jnp.where((row >> 1) == (col >> 1), matrix, 0.0)
        for matrix in diagonal
    ]
    level = 1
    while (1 << level) < part:
        joined = ((row >> (level + 1)) == (col >> (level + 1))) & ((row >> level) != (col >> level))
        pairs = each(halves, inverse)
        steps = [
            mm3(halves(jnp.where(joined, matrix, 0.0)), stacked(pair))
            for matrix, pair in zip(diagonal, pairs)
        ]
        inverse = [
            value - mm3(pair, stacked(halves(step)))
            for value, pair, step in zip(inverse, pairs, steps)
        ]
        level += 1
    pairs = each(halves, inverse)
    even = own[0] | own[2]
    steps = [
        mm3(halves(jnp.where(even, side_by_side(matrix, 1), 0.0)), stacked(pair))
        for matrix, pair in zip(strict, pairs)
    ]
    corners = [
        -mm3(pair, stacked(halves(step), (None, 0, None, 2))) for pair, step in zip(pairs, steps)
    ]

    def joined_block(value, corner, n):
        lanes = slice(n * half, (n + 1) * half)
        upper = jnp.where(own[2 * n], value, 0.0)[:, lanes]
        return jnp.concatenate([upper, jnp.where(own[2 * n], corner, value)[:, lanes]], axis=0)

    first = [joined_block(value, corner, 0) for value, corner in zip(inverse, corners)]
    last = [joined_block(value, corner, 1) for value, corner in zip(inverse, corners)]
    steps = [mm3(halves(matrix[half:, :half]), halves(value)) for matrix, value in zip(strict, first)]
    lower = [-mm3(halves(value), halves(step)) for value, step in zip(last, steps)]
    blank = jnp.zeros((half, half), jnp.float32)
    return [
        jnp.concatenate(
            [
                jnp.concatenate([top, blank], axis=1),
                jnp.concatenate([left, right], axis=1),
            ],
            axis=0,
        )
        for top, left, right in zip(first, lower, last)
    ]


def unit_rows(raw):
    norm = lax.rsqrt(jnp.sum(raw * raw, axis=1, keepdims=True) + EPSILON)
    return raw * norm, norm


def below(matrix, row, col):
    return jnp.where(row > col, matrix, 0.0)


def key_halves(house_raw, keys, betas):
    row, col = square_index(keys[0].shape[0])
    house = [unit_rows(raw)[0] for raw in house_raw]
    scaled = [halves(beta * value) for beta, value in zip(betas, house)]
    strict = [below(mm3(a, halves(b), ABT), row, col) for a, b in zip(scaled, house)]
    house_key = [halves(below(mm3(a, halves(b), ABT), row, col)) for a, b in zip(scaled, keys)]
    inverses = unit_lower_inverses(strict)
    return inverses, [mm3(halves(a), b) for a, b in zip(inverses, house_key)]


def query_halves(queries, values, house_raw, keys, inverses, key_side, allowed):
    row, col = square_index(keys[0].shape[0])
    scaling = 1.0 / math.sqrt(queries[0].shape[1])
    q = each(halves, queries)
    query_house = [
        halves(jnp.where(row >= col, mm3(a, halves(unit_rows(raw)[0]), ABT), 0.0))
        for a, raw in zip(q, house_raw)
    ]
    scores = [mm3(a, halves(b), ABT) for a, b in zip(q, keys)]
    scores = [score - mm3(a, halves(b)) for score, a, b in zip(scores, query_house, key_side)]
    masked = [jnp.where(allowed, score * scaling, NEGATIVE) for score in scores]
    weights = [jnp.exp(value - jnp.max(value, axis=1, keepdims=True)) for value in masked]
    probs = [value / jnp.sum(value, axis=1, keepdims=True) for value in weights]
    attn = [mm(prob.astype(jnp.bfloat16), value) for prob, value in zip(probs, values)]
    return attn, probs, [mm3(a, halves(b)) for a, b in zip(query_house, inverses)]


def heads_backward(queries, keys, house_raw, values, betas, probs, key_side, query_side, d_attn):
    row, col = square_index(keys[0].shape[0])
    scaling = 1.0 / math.sqrt(queries[0].shape[1])
    house, norm = zip(*[unit_rows(raw) for raw in house_raw])
    d_values = [mm(prob.astype(jnp.bfloat16), d, ATB) for prob, d in zip(probs, d_attn)]
    d_probs = [mm(d, value, ABT) for d, value in zip(d_attn, values)]
    d_scores = [
        halves(prob * (d - jnp.sum(prob * d, axis=1, keepdims=True)) * scaling)
        for prob, d in zip(probs, d_probs)
    ]
    q, k, w = each(halves, queries), each(halves, keys), each(halves, house)
    scaled = [halves(beta * value) for beta, value in zip(betas, house)]
    side = each(halves, query_side)
    d_side = [-mm3(d, halves(value), ABT) for d, value in zip(d_scores, key_side)]
    d_query_house = [halves(jnp.where(row >= col, d, 0.0)) for d in d_side]
    d_strict = [halves(below(-mm3(a, halves(d), ATB), row, col)) for a, d in zip(side, d_side)]
    d_house_key = [halves(below(-mm3(a, d, ATB), row, col)) for a, d in zip(side, d_scores)]
    d_queries = [mm3(d, a) + mm3(e, b) for d, a, e, b in zip(d_scores, k, d_query_house, w)]
    d_keys = [
        mm3(d, a, ATB) + mm3(e, b, ATB) for d, a, e, b in zip(d_scores, q, d_house_key, scaled)
    ]
    d_scaled = [mm3(d, a) + mm3(e, b) for d, a, e, b in zip(d_strict, w, d_house_key, k)]
    d_house = [
        mm3(d, a, ATB) + mm3(e, b, ATB) for d, a, e, b in zip(d_strict, scaled, d_query_house, q)
    ]
    d_betas = [jnp.sum(d * value, axis=1, keepdims=True) for d, value in zip(d_scaled, house)]
    d_house = [d + beta * e for d, beta, e in zip(d_house, betas, d_scaled)]
    d_house_raw = [
        n * (d - value * jnp.sum(d * value, axis=1, keepdims=True))
        for n, d, value in zip(norm, d_house, house)
    ]
    d_logits = [d * beta * (1.0 - 0.5 * beta) for d, beta in zip(d_betas, betas)]
    return d_queries, d_keys, d_house_raw, d_values, d_logits


def head_slices(ref, first, heads, head):
    return [ref[:, first + n * head : first + (n + 1) * head] for n in range(heads)]


def started(pairs, sems):
    copies = [
        pltpu.make_async_copy(source, target, sems.at[n]) for n, (source, target) in enumerate(pairs)
    ]
    for copy in copies:
        copy.start()
    return copies


def token_rows(places, n, k, quarter):
    return pl.ds(pl.multiple_of(places[8 + n] + places[18 + k], 16), quarter)


def placed(gathered, whole, places):
    quarter = gathered.shape[1] // 4
    return [
        (
            gathered.at[n, pl.ds(k * quarter, quarter)],
            whole.at[pl.ds(pl.multiple_of(places[18 + k] + n * quarter, 16), quarter)],
        )
        for n in range(4)
        for k in range(4)
    ]


def split_tokens(whole, parts, places):
    quarter = parts[0].shape[0] // 4
    for n in range(4):
        for k in range(4):
            parts[n][pl.ds(k * quarter, quarter)] = whole[token_rows(places, n, k, quarter)]


def wide_row(row, rows):
    return jnp.broadcast_to(row, (rows, row.shape[1])).astype(jnp.bfloat16)


def own_blocks(places, source, target, sequence=26, at=0):
    quarter = target.shape[-2]
    rows = pl.ds(pl.multiple_of(places[22], 16), quarter)
    return [(source.at[places[sequence + k], rows], target.at[k + at]) for k in range(4)]


def message_kernel(places, hidden_in, ids, gain_one, gain_two, *refs):
    messages, blocks, sems = refs[0:4], refs[4], refs[5]
    quarter, features = blocks.shape[1], blocks.shape[2]
    rows, depth = ids.shape[1], gain_one.shape[0]
    copies = started(own_blocks(places, hidden_in, blocks), sems)
    for k in range(4):
        messages[k][:, features:] = jnp.zeros((quarter, 640), jnp.bfloat16)
        own_ids = ids[pl.ds(places[26 + k], 1)].astype(jnp.float32)
        messages[k][:, features : features + rows] = wide_row(own_ids, quarter)
        at = features + 128
        messages[k][:, at : at + depth] = wide_row(gain_one[...].astype(jnp.float32)[None], quarter)
        at += 256
        messages[k][:, at : at + depth] = wide_row(gain_two[...].astype(jnp.float32)[None], quarter)
    for copy in copies:
        copy.wait()
    for k in range(4):
        messages[k][:, :features] = blocks[k]


def attention_pack_kernel(places, house, key, beta, query, value, out, first, second):
    for target, sources in ((first, (house, key, beta)), (second, (query, value, out))):
        at = 0
        for source in sources:
            width = source.shape[1]
            if width < 128:
                target[:, at : at + 128] = jnp.zeros((target.shape[0], 128), jnp.bfloat16)
            target[:, at : at + width] = source[...]
            at += width


def feed_forward_pack_kernel(places, output_grad, gate, up, down, *refs):
    messages, gives, keeps, blocks, sems = refs[0:4], refs[4:6], refs[6:8], refs[8], refs[9]
    copies = started(
        own_blocks(places, output_grad, blocks) + own_blocks(places, output_grad, blocks, 30, 4), sems
    )
    units = gate.shape[1] // 2
    part = units // 2
    for packs, start in ((keeps, places[23]), (gives, places[24])):
        for n in range(6):
            at = pl.ds(pl.multiple_of(start + n % 2 * part, 128), part)
            packs[n // 3][:, n % 3 * part : (n % 3 + 1) * part] = (gate, up, down)[n // 2][:, at]
    for copy in copies:
        copy.wait()
    for k in range(4):
        messages[k][0] = blocks[k]
        messages[k][1] = blocks[4 + k]


def out_message_kernel(places, *refs):
    out_parts, middle, messages = refs[0:4], refs[4], refs[5:9]
    quarter = middle.shape[0] // 4
    out = sum(part[...].astype(jnp.float32) for part in out_parts)
    own, pair = (middle[...] + out[0]).astype(jnp.bfloat16), out[1].astype(jnp.bfloat16)
    for k in range(4):
        messages[k][:quarter] = own[k * quarter : (k + 1) * quarter]
        messages[k][quarter:] = pair[(k ^ 2) * quarter : ((k ^ 2) + 1) * quarter]


def result_kernel(places, d_parts, d_middle, x, factor, gain, gain_two_grad, *messages):
    quarter, features = x.shape[0] // 4, x.shape[1]
    d_one = sum(d_parts[n].astype(jnp.float32) for n in range(4))
    normed = x[...] * factor[...]
    scaled = d_one * gain[...]
    mean = jnp.mean(scaled * normed, axis=1, keepdims=True)
    in_grad = (d_middle[...] + factor[...] * (scaled - normed * mean)).astype(jnp.bfloat16)
    gain_one_grad = jnp.sum(d_one * normed, axis=0, keepdims=True)
    row = lax.broadcasted_iota(jnp.int32, (quarter, 128), 0)
    for g, gains in enumerate((gain_one_grad, gain_two_grad[...])):
        packed = jnp.zeros((quarter, 128), jnp.float32)
        for n in range(features // 128):
            packed = jnp.where(row == n, gains[:, n * 128 : (n + 1) * 128], packed)
        at = features + g * 128
        for k in range(4):
            messages[k][:, at : at + 128] = packed.astype(jnp.bfloat16)
    for k in range(4):
        messages[k][:, :features] = in_grad[k * quarter : (k + 1) * quarter]


def spread_kernel(places, out_pieces, grad_pieces, out, grad, gains):
    quarter, features = out.shape[1] // 4, out.shape[2]
    for n in range(4):
        rows = slice(n * quarter, (n + 1) * quarter)
        for k in range(4):
            at = pl.ds(places[26 + k], 1)
            out[at, rows] = out_pieces[n, k * quarter : (k + 1) * quarter][None]
            grad[at, rows] = grad_pieces[n, k * quarter : (k + 1) * quarter, :features][None]
    gains[...] = sum(grad_pieces[n, :quarter, features:].astype(jnp.float32) for n in range(4))


def weights_in_place(pieces, whole, places, first=0, count=None):
    depth = pieces[0].shape[0]
    width = count or pieces[0].shape[1]
    return [
        (
            pieces[n].at[:, pl.ds(first, width)],
            whole.at[pl.ds(pl.multiple_of(places[n], 64), depth), pl.ds(0, width)],
        )
        for n in range(8)
    ]


def keys_kernel(heads, places, *refs):
    weights, xs, gain = refs[0:8], refs[8], refs[9]
    h_all, proj, inverses, key_side = refs[10:14]
    w_all, weight_sems, x_sems, x_all = refs[14:18]
    x_copies = started(placed(xs, x_all, places), x_sems)
    w_copies = started(weights_in_place(weights, w_all, places), weight_sems)
    for copy in x_copies:
        copy.wait()
    width = (proj.shape[1] - 128) // 2
    head = width // heads
    x = x_all[...].astype(jnp.float32)
    factor = lax.rsqrt(jnp.mean(x * x, axis=1, keepdims=True) + EPSILON)
    h_all[...] = (x * factor * gain[...]).astype(jnp.bfloat16)
    for copy in w_copies:
        copy.wait()
    proj[...] = mm(h_all[...], w_all[...])
    betas = 2.0 * jax.nn.sigmoid(proj[:, 2 * width :])
    results = key_halves(
        head_slices(proj, 0, heads, head),
        head_slices(proj, width, heads, head),
        [betas[:, n : n + 1] for n in range(heads)],
    )
    for n in range(heads):
        inverses[n], key_side[n] = results[0][n], results[1][n]


def queries_kernel(heads, places, *refs):
    weights, (h_all, proj_keys, inverses, key_side, id_row, id_col) = refs[0:8], refs[8:14]
    proj, attn, probs, query_side, parts = refs[14], refs[15], refs[16], refs[17], refs[18:22]
    w_all, total, sems = refs[22:25]
    for copy in started(weights_in_place(weights, w_all, places), sems):
        copy.wait()
    width = attn.shape[1]
    head = width // heads
    proj[...] = mm(h_all[...], w_all[:, : 2 * width])
    row, col = square_index(h_all.shape[0])
    results = query_halves(
        head_slices(proj, 0, heads, head),
        [value.astype(jnp.bfloat16) for value in head_slices(proj, width, heads, head)],
        head_slices(proj_keys, 0, heads, head),
        head_slices(proj_keys, width, heads, head),
        [inverses[n] for n in range(heads)],
        [key_side[n] for n in range(heads)],
        (col <= row) & (id_row[...] == id_col[...]),
    )
    for n in range(heads):
        attn[:, n * head : (n + 1) * head] = results[0][n].astype(jnp.bfloat16)
        probs[n], query_side[n] = results[1][n], results[2][n]
    total[...] = mm(attn[...], w_all[:, 2 * width :], ABT).astype(jnp.bfloat16)
    split_tokens(total, parts, places)


def feed_forward_kernel(places, *refs):
    weights, ins, grads = refs[0:16], refs[16:18], refs[18:22]
    two_parts, out_parts, keeps, sends = refs[22:30], refs[30:34], refs[34], refs[35]
    w_all, in_all, grad_all, total, weight_sems, in_sems, grad_sems = refs[36:43]
    rows, units, half = two_parts[0].shape[0], w_all.shape[1] // 3, w_all.shape[0] // 2

    def block(s, n):
        return pl.ds(pl.multiple_of(places[8 + n] * 4 + s * 4 * rows, 64), rows)

    depth, part = weights[0].shape[0], w_all.shape[1] // 2
    w_pairs = []
    for n in range(16):
        row = pl.ds(pl.multiple_of(places[n // 2], 64), depth)
        w_pairs.append((weights[n], w_all.at[row, pl.ds(n % 2 * part, part)]))
    w_copies = started(w_pairs, weight_sems)
    grad_copies = started(
        [
            (grads[n].at[s], grad_all.at[block(s, n)])
            for n in range(4)
            for s in range(2)
        ],
        grad_sems,
    )
    in_copies = started(
        [(ins[s].at[n], in_all.at[pl.ds((s * 4 + n) * rows, rows)]) for s in range(2) for n in range(4)],
        in_sems,
    )
    for copy in w_copies + grad_copies + in_copies:
        copy.wait()
    both = mm(in_all[...], w_all[:, : 2 * units])
    d_hidden = mm(grad_all[...], w_all[:, 2 * units :])
    gate, up = both[:, :units], both[:, units:]
    sigmoid = jax.nn.sigmoid(gate)
    silu = gate * sigmoid
    hidden = (silu * up).astype(jnp.bfloat16)
    d_gate = (d_hidden * up * sigmoid * (1.0 + gate * (1.0 - sigmoid))).astype(jnp.bfloat16)
    d_up = (d_hidden * silu).astype(jnp.bfloat16)
    for target in (keeps, sends):
        at = 2 * half
        for value in (d_gate, d_up, hidden):
            target[:, at : at + units] = value
            at += units
    d_both = keeps[:, 2 * half : 2 * half + 2 * units]
    total[...] = mm(d_both, w_all[:, : 2 * units], ABT).astype(jnp.bfloat16)
    for s in range(2):
        for n in range(4):
            two_parts[s * 4 + n][...] = total[block(s, n)]
    total[...] = mm(hidden, w_all[:, 2 * units :], ABT).astype(jnp.bfloat16)
    for s in range(2):
        for n in range(4):
            out_parts[n][s] = total[block(s, n)]
    for target, place in ((keeps, 12), (sends, 13)):
        lanes = pl.ds(pl.multiple_of(places[place], 128), half)
        target[:, :half] = in_all[:, lanes]
        target[:, half : 2 * half] = grad_all[:, lanes]


def attention_backward_kernel(heads, places, *refs):
    first, second, ds = refs[0:8], refs[8:16], refs[16]
    proj_keys, proj, probs, key_side, query_side, h_all, attn = refs[17:24]
    keeps, sends, parts = refs[24:27]
    w_first, w_second, d_all, d_attn, total, first_sems, second_sems, d_sems = refs[27:35]
    half, width = d_all.shape[1] // 2, d_attn.shape[1]
    d_keys_all = keeps.at[:, pl.ds(2 * half, 2 * width + 128)]
    d_queries_all = keeps.at[:, pl.ds(2 * half + 2 * width + 128, 2 * width)]
    second_copies = started(weights_in_place(second, w_second, places), second_sems)
    d_copies = started(placed(ds, d_all, places), d_sems)
    first_copies = started(weights_in_place(first, w_first, places), first_sems)
    for copy in d_copies + second_copies:
        copy.wait()
    head = width // heads
    d_attn[...] = mm(d_all[...], w_second[:, 2 * width :]).astype(jnp.bfloat16)
    betas = 2.0 * jax.nn.sigmoid(proj_keys[:, 2 * width :])
    lane = lax.broadcasted_iota(jnp.int32, betas.shape, 1)
    logits = jnp.zeros(betas.shape, jnp.float32)
    results = heads_backward(
        head_slices(proj, 0, heads, head),
        head_slices(proj_keys, width, heads, head),
        head_slices(proj_keys, 0, heads, head),
        [value.astype(jnp.bfloat16) for value in head_slices(proj, width, heads, head)],
        [betas[:, n : n + 1] for n in range(heads)],
        [probs[n] for n in range(heads)],
        [key_side[n] for n in range(heads)],
        [query_side[n] for n in range(heads)],
        head_slices(d_attn, 0, heads, head),
    )
    for n in range(heads):
        d_queries, d_keys, d_house, d_values, d_logit = [result[n] for result in results]
        low_at, high_at = slice(n * head, (n + 1) * head), slice(width + n * head, width + (n + 1) * head)
        d_keys_all[:, low_at] = d_house.astype(jnp.bfloat16)
        d_keys_all[:, high_at] = d_keys.astype(jnp.bfloat16)
        d_queries_all[:, low_at] = d_queries.astype(jnp.bfloat16)
        d_queries_all[:, high_at] = d_values.astype(jnp.bfloat16)
        logits = jnp.where(lane == n, d_logit, logits)
    d_keys_all[:, 2 * width :] = logits.astype(jnp.bfloat16)
    for copy in first_copies:
        copy.wait()
    keeps[:, keeps.shape[1] - width :] = attn[...]
    sends[:, 2 * half :] = keeps[:, 2 * half :]
    for target, place in ((keeps, 12), (sends, 13)):
        lanes = pl.ds(pl.multiple_of(places[place], 128), half)
        target[:, :half] = h_all[:, lanes]
        target[:, half : 2 * half] = d_all[:, lanes]
    total[...] = (
        mm(d_keys_all[...], w_first[...], ABT) + mm(d_queries_all[...], w_second[:, : 2 * width], ABT)
    ).astype(jnp.bfloat16)
    quarter = parts.shape[1] // 4
    for n in range(4):
        for k in range(4):
            rows = pl.ds(pl.multiple_of(places[18 + k] + n * quarter, 16), quarter)
            parts[n, k * quarter : (k + 1) * quarter] = total[rows]


def weight_grad_kernel(groups, places, mine, came, *refs):
    outs, total = refs[:-1], refs[-1]
    half, at = total.shape[0], 0
    for left, start, width in groups:
        lefts, rights = slice(left * half, (left + 1) * half), slice(start, start + width)
        total[:, at : at + width] = (
            mm(mine[:, lefts], mine[:, rights], ATB) + mm(came[:, lefts], came[:, rights], ATB)
        ).astype(jnp.bfloat16)
        at += width
    depth, at = outs[0].shape[1], 0
    for n in range(0, len(outs), 2):
        width = outs[n].shape[2]
        for k in range(4):
            rows = pl.ds(pl.multiple_of(places[14 + k], 64), depth)
            outs[n + k % 2][k // 2] = total[rows, at : at + width]
        at += width


VMEM_BYTES = 56 * 1024 * 1024


def call(kernel, outs, scratch, places, operands, spaces, micros, out_spaces=None):
    vmem = pl.BlockSpec(memory_space=pltpu.VMEM)
    kinds = {"v": vmem, "a": pl.BlockSpec(memory_space=pl.ANY)}
    return pl.pallas_call(
        kernel,
        out_shape=[jax.ShapeDtypeStruct(shape, kind) for shape, kind in outs],
        in_specs=[pl.BlockSpec(memory_space=pltpu.SMEM)] + [kinds[s] for s in spaces],
        out_specs=[kinds[s] for s in out_spaces or "v" * len(outs)],
        scratch_shapes=scratch,
        compiler_params=pltpu.CompilerParams(vmem_limit_bytes=VMEM_BYTES),
        cost_estimate=pl.CostEstimate(
            flops=int(micros * 1.1e9), transcendentals=0, bytes_accessed=int(micros * 3.6e6)
        ),
    )(places, *operands)


def swap(block, axis, distance):
    size = lax.axis_size(axis)
    return lax.ppermute(block, axis, [(i, i ^ distance) for i in range(size)])


def gathered_tp(block):
    return lax.all_gather(block, "tp", axis=0)


def all_tp(block):
    return [block] + [swap(block, "tp", n) for n in (1, 2, 3)]


def to_owners(messages):
    return [messages[0]] + [swap(messages[n], "ctx", n) for n in (1, 2, 3)]


def sum_tp(parts):
    return [parts[0]] + [swap(parts[n], "tp", n) for n in (1, 2, 3)]


def add_up(blocks):
    total = blocks[0].astype(jnp.float32)
    for block in blocks[1:]:
        total = total + block.astype(jnp.float32)
    return total


def other_core(block):
    return swap(block, "fsdp", 1)


def whole_sequences(
    hidden_in,
    segment_ids,
    doc_starts,
    norm1_gain,
    w_query,
    w_key,
    w_value,
    w_house,
    w_beta,
    w_out,
    norm2_gain,
    w_gate,
    w_up,
    w_down,
    output_grad,
):
    low, wide = jnp.bfloat16, jnp.float32
    core, chain, column = lax.axis_index("fsdp"), lax.axis_index("ctx"), lax.axis_index("tp")
    rows, features = hidden_in.shape[1], hidden_in.shape[2]
    depth, width, heads = w_query.shape[0], w_query.shape[1], w_beta.shape[1]
    length, half, quarter = 4 * rows, features // 2, rows // 4
    units, used = w_gate.shape[1] // 2, 4 * width + 128
    near = jnp.arange(4, dtype=jnp.int32)
    upper = (chain // 2).astype(jnp.int32)
    places = jnp.concatenate(
        [
            (core * 4 + (chain ^ near)) * depth,
            ((1 - core) * 4 + (chain ^ near)) * depth,
            (column ^ near) * quarter,
            jnp.stack([core, 1 - core]) * half,
            (chain ^ near) * depth,
            (chain ^ near) * rows,
            jnp.stack([column * quarter, upper * units, (1 - upper) * units, upper]),
            chain ^ near,
            chain ^ near ^ 2,
        ]
    ).astype(jnp.int32)
    step = lax.optimization_barrier
    block = pltpu.VMEM((4, quarter, features), low)
    token_messages = call(
        message_kernel,
        [((quarter, features + 640), low)] * 4,
        [block, pltpu.SemaphoreType.DMA((4,))],
        places,
        [hidden_in, segment_ids, norm1_gain, norm2_gain],
        "avvv",
        2,
    )
    first, second = call(
        attention_pack_kernel,
        [((depth, 2 * width + 128), low), ((depth, 3 * width), low)],
        [],
        places,
        [w_house, w_key, w_beta, w_query, w_value, w_out],
        "v" * 6,
        2,
    )
    packed = call(
        feed_forward_pack_kernel,
        [((2, quarter, features), low)] * 4
        + [((depth, 3 * units // 2), low)] * 4,
        [pltpu.VMEM((8, quarter, features), low), pltpu.SemaphoreType.DMA((8,))],
        places,
        [output_grad, w_gate, w_up, w_down],
        "avvv",
        3,
    )
    x_messages, first, second, grad_messages, gives, ffn_keeps = step(
        (to_owners(token_messages), first, second, packed[:4], packed[4:6], packed[6:8])
    )

    first_two, first_one = swap(first, "ctx", 2), swap(first, "ctx", 1)
    x_block = jnp.concatenate([message[:, :features] for message in x_messages])
    x_pieces = gathered_tp(x_block)
    info = jnp.stack([message[0, features:] for message in x_messages])
    chosen = near[:, None] == (near[None, :] ^ chain)
    info = jnp.sum(jnp.where(chosen[:, :, None], info[None].astype(wide), 0.0), axis=1)
    ids = info[:, :rows].reshape(length)
    gains = jnp.concatenate(
        [info[:, 128 : 128 + depth], info[:, 384 : 384 + depth]], axis=1
    ).astype(low)
    grad_messages = to_owners(grad_messages)
    first_two, first_one, x_pieces, first, gains, grad_messages, second = step(
        (first_two, first_one, x_pieces, first, gains, grad_messages, second)
    )

    first_three = swap(first_two, "ctx", 1)
    second_two = swap(second, "ctx", 2)
    grads = jnp.stack(
        [
            jnp.concatenate([message[0] for message in grad_messages]),
            jnp.concatenate([grad_messages[n ^ 2][1] for n in range(4)]),
        ]
    )
    own_grad = grads[0]
    grad_pieces = all_tp(grads)
    first_three, first_two, first_one, second_two, gains, second, grad_pieces, gives = step(
        (first_three, first_two, first_one, second_two, gains, second, grad_pieces, gives)
    )

    key_weights = [first, first_one, first_two, first_three]
    key_weights = key_weights + [other_core(piece) for piece in key_weights]
    gains_other = other_core(gains)
    gains = jnp.where(core == 0, jnp.stack([gains, gains_other]), jnp.stack([gains_other, gains]))
    gain_one = gains[:, :, :depth].reshape(1, features).astype(wide)
    gain_two = gains[:, :, depth:].reshape(1, features).astype(wide)
    second_one = swap(second, "ctx", 1)
    give_two = [swap(gives[0], "ctx", 2)]
    square = ((heads, length, length), wide)
    h_all, proj_keys, inverses, key_side = call(
        functools.partial(keys_kernel, heads),
        [((length, features), low), ((length, 2 * width + 128), wide), square, square],
        [
            pltpu.VMEM((features, 2 * width + 128), low),
            pltpu.SemaphoreType.DMA((8,)),
            pltpu.SemaphoreType.DMA((16,)),
            pltpu.VMEM((length, features), low),
        ],
        places,
        [*key_weights, x_pieces, gain_one],
        "a" * 9 + "v",
        20,
    )
    second_two, second_one, give_two, give_last, proj_keys, second = step(
        (second_two, second_one, give_two, gives[1], proj_keys, second)
    )
    second_three = swap(second_two, "ctx", 1)
    second_others = [other_core(piece) for piece in (second, second_one, second_two)]
    give_two = give_two + [swap(give_last, "ctx", 2)]
    second_three, second_others, proj_keys, give_two, ffn_keeps = step(
        (second_three, second_others, proj_keys, give_two, ffn_keeps)
    )
    query_weights = [
        second, second_one, second_two, second_three, *second_others, other_core(second_three)
    ]

    keep_one, give_three = [swap(ffn_keeps[0], "ctx", 1)], [swap(give_two[0], "ctx", 1)]
    outs = call(
        functools.partial(queries_kernel, heads),
        [((length, 2 * width), wide), ((length, width), low), square, square]
        + [((rows, features), low)] * 4,
        [
            pltpu.VMEM((features, 3 * width), low),
            pltpu.VMEM((length, features), low),
            pltpu.SemaphoreType.DMA((8,)),
        ],
        places,
        [*query_weights, h_all, proj_keys, inverses, key_side, ids[None, :], ids[:, None]],
        "a" * 8 + "v" * 6,
        9,
    )
    proj, attn, probs, query_side = outs[:4]
    give_two, branch_parts, keep_one, give_three, ffn_keeps = step(
        (give_two, outs[4:], keep_one, give_three, ffn_keeps)
    )
    keep_one = keep_one + [swap(ffn_keeps[1], "ctx", 1)]
    give_three = give_three + [swap(give_two[1], "ctx", 1)]
    residual = x_block.astype(wide)
    normed_one, factor_one = norm_rows(residual)
    middle = residual + add_up(sum_tp(branch_parts))
    normed_two, factor_two = norm_rows(middle)
    h_two = (normed_two * gain_two).astype(low)
    give_two, give_three, keep_one, h_two = step((give_two, give_three, keep_one, h_two))

    h_pair = swap(h_two, "ctx", 2)
    h_own = gathered_tp(h_two)
    h_pair, give_three, h_own, keep_one, give_two = step(
        (h_pair, give_three, h_own, keep_one, give_two)
    )
    ffn_weights = [*ffn_keeps, *keep_one, *give_two, *give_three]
    ffn_weights = ffn_weights + [other_core(piece) for piece in ffn_weights]
    h_pair = gathered_tp(h_pair)

    tokens = 2 * length
    pair = ((2, rows, features), low)
    outs = call(
        feed_forward_kernel,
        [((rows, features), low)] * 8 + [pair] * 4 + [((tokens, features + 3 * units), low)] * 2,
        [
            pltpu.VMEM((features, 3 * units), low),
            pltpu.VMEM((tokens, features), low),
            pltpu.VMEM((tokens, features), low),
            pltpu.VMEM((tokens, features), low),
            pltpu.SemaphoreType.DMA((16,)),
            pltpu.SemaphoreType.DMA((8,)),
            pltpu.SemaphoreType.DMA((8,)),
        ],
        places,
        [*ffn_weights, h_own, h_pair, *grad_pieces],
        "a" * 22,
        12,
    )
    own_parts, pair_parts, out_parts, keeps, sends = outs[:4], outs[4:8], outs[8:12], outs[12], outs[13]

    def grads_of(mine, came, groups, pieces=1):
        total = sum(group[2] for group in groups)
        return call(
            functools.partial(weight_grad_kernel, groups),
            [((2, depth, total // pieces), low)] * (2 * pieces),
            [pltpu.VMEM((half, total), low)],
            places,
            [mine, came],
            "vv",
            total / 400.0,
        )

    pair_sum = add_up(sum_tp(pair_parts)).astype(low)
    came, pair_sum, own_parts = step((other_core(sends), pair_sum, own_parts))

    two_other = swap(pair_sum, "ctx", 2)
    own_sum = add_up(sum_tp(own_parts))
    ffn_grads = grads_of(
        keeps, came, ((0, features, 2 * units), (1, features + 2 * units, units)), 2
    )
    d_two = own_sum + two_other.astype(wide)
    gain_two_grad = jnp.sum(d_two * normed_two, axis=0)
    d_middle = own_grad.astype(wide) + norm_back(d_two, normed_two, factor_two, gain_two)
    d_low, ffn_grads = step((d_middle.astype(low), tuple(ffn_grads)))

    ffn_came = [swap(ffn_grads[1], "ctx", 1)]
    d_pieces = gathered_tp(d_low)
    ffn_sums = [add_up([ffn_grads[0], ffn_came[0]])]
    ffn_leave = ffn_sums[0][1].astype(low)
    d_pieces, out_parts, ffn_leave, ffn_far = step((d_pieces, out_parts, ffn_leave, ffn_grads[3]))

    ffn_other = [swap(ffn_leave, "ctx", 2)]
    ffn_came = ffn_came + [swap(ffn_far, "ctx", 1)]
    out_received = sum_tp(out_parts)
    back = call(
        functools.partial(attention_backward_kernel, heads),
        [((length, features + used + width), low)] * 2 + [((4, rows, features), low)],
        [
            pltpu.VMEM((features, 2 * width + 128), low),
            pltpu.VMEM((features, 3 * width), low),
            pltpu.VMEM((length, features), low),
            pltpu.VMEM((length, width), low),
            pltpu.VMEM((length, features), low),
            pltpu.SemaphoreType.DMA((8,)),
            pltpu.SemaphoreType.DMA((8,)),
            pltpu.SemaphoreType.DMA((16,)),
        ],
        places,
        [*key_weights, *query_weights, d_pieces, proj_keys, proj, probs, key_side, query_side, h_all, attn],
        "a" * 17 + "v" * 7,
        14,
    )
    ffn_sums = ffn_sums + [add_up([ffn_grads[2], ffn_came[1]])]
    ffn_leave, ffn_other, out_received, (keeps, sends, d_parts) = step(
        (ffn_sums[1][1].astype(low), ffn_other, out_received, tuple(back))
    )

    came, keeps, d_parts = step((other_core(sends), keeps, d_parts))

    query_start = features + 2 * width + 128
    near_two, far_two = grads_of(
        keeps, came, ((0, query_start, 2 * width), (1, query_start + 2 * width, width))
    )
    two_came = swap(far_two, "ctx", 1)
    ffn_other = ffn_other + [swap(ffn_leave, "ctx", 2)]
    near_one, far_one = grads_of(keeps, came, ((0, features, 2 * width + 128),))
    out_messages = call(
        out_message_kernel,
        [((2 * quarter, features), low)] * 4,
        [],
        places,
        [*out_received, middle],
        "v" * 5,
        2,
    )
    out_messages = to_owners(out_messages)
    d_received = lax.all_to_all(d_parts, "tp", 0, 0)
    messages = call(
        result_kernel,
        [((quarter, features + 256), low)] * 4,
        [],
        places,
        [d_received, d_middle, residual, factor_one, gain_one, gain_two_grad[None]],
        "v" * 6,
        3,
    )
    two_sum = add_up([near_two, two_came])
    ffn_other, two_leave, near_one, far_one, messages, out_messages = step(
        (ffn_other, two_sum[1].astype(low), near_one, far_one, tuple(messages), out_messages)
    )

    one_came = swap(far_one, "ctx", 1)
    query_other = swap(two_leave, "ctx", 2)
    messages, out_messages = step((to_owners(messages), out_messages))
    out_block = jnp.concatenate(
        [add_up([out_messages[n][:quarter], out_messages[n ^ 2][quarter:]]) for n in range(4)]
    ).astype(low)
    out_pieces = gathered_tp(out_block)
    owned = jnp.concatenate(
        [message[:, :features] for message in messages]
    )
    gain_sum = add_up([message[:, features:] for message in messages]).astype(low)
    owned = jnp.concatenate([owned, jnp.pad(gain_sum, ((0, 3 * quarter), (0, 0)))], axis=1)
    one_sum = add_up([near_one, one_came])
    one_leave, owned, query_other, out_pieces = step(
        (one_sum[1].astype(low), owned, query_other, out_pieces)
    )

    key_other = swap(one_leave, "ctx", 2)
    block_out, input_grad, gain_total = call(
        spread_kernel,
        [((4, rows, features), low)] * 2 + [((quarter, 256), wide)],
        [],
        places,
        [out_pieces, gathered_tp(owned)],
        "vv",
        3,
    )
    gain_total = gain_total + other_core(gain_total)
    gain_total = jnp.concatenate(
        [gain_total[: features // 128, :128], gain_total[: features // 128, 128:]]
    ).reshape(2, features)
    gain_total = lax.dynamic_slice_in_dim(gain_total, (core * 4 + chain) * depth, depth, axis=1)
    query_grads = two_sum[0] + query_other.astype(wide)
    key_grads = one_sum[0] + key_other.astype(wide)

    ffn_kept = jnp.concatenate([total[0] for total in ffn_sums], axis=1)
    ffn_other = jnp.concatenate(ffn_other, axis=1).astype(wide)

    def ffn_result(n):
        kept = ffn_kept[:, n * units : (n + 1) * units]
        came = ffn_other[:, n * units : (n + 1) * units]
        return jnp.concatenate(
            [jnp.where(upper == 1, came, kept), jnp.where(upper == 1, kept, came)], axis=1
        )

    return (
        block_out,
        input_grad,
        gain_total[0],
        query_grads[:, :width],
        key_grads[:, width : 2 * width],
        query_grads[:, width : 2 * width],
        key_grads[:, :width],
        key_grads[:, 2 * width : 2 * width + heads],
        query_grads[:, 2 * width :],
        gain_total[1],
        ffn_result(0),
        ffn_result(1),
        ffn_result(2),
    )


def shards(*args):
    sizes = [lax.axis_size(axis) for axis in ("fsdp", "ctx", "tp")]
    if sizes == [2, 4, 4] and args[0].shape[:2] == (4, 64):
        return whole_sequences(*args)
    return ring_of_groups(*args)


def solution(mesh):
    in_specs = (
        P("fsdp", "ctx", None),
        P("fsdp", "ctx"),
        P("fsdp", "ctx"),
        P(("fsdp", "ctx")),
        P(("fsdp", "ctx"), "tp"),
        P(("fsdp", "ctx"), "tp"),
        P(("fsdp", "ctx"), "tp"),
        P(("fsdp", "ctx"), "tp"),
        P(("fsdp", "ctx"), "tp"),
        P(("fsdp", "ctx"), "tp"),
        P(("fsdp", "ctx")),
        P(("fsdp", "ctx"), "tp"),
        P(("fsdp", "ctx"), "tp"),
        P(("fsdp", "ctx"), "tp"),
        P("fsdp", "ctx", None),
    )
    out_specs = (
        P("fsdp", "ctx", None),
        P("fsdp", "ctx", None),
        P(("fsdp", "ctx")),
        P(("fsdp", "ctx"), "tp"),
        P(("fsdp", "ctx"), "tp"),
        P(("fsdp", "ctx"), "tp"),
        P(("fsdp", "ctx"), "tp"),
        P(("fsdp", "ctx"), "tp"),
        P(("fsdp", "ctx"), "tp"),
        P(("fsdp", "ctx")),
        P(("fsdp", "ctx"), "tp"),
        P(("fsdp", "ctx"), "tp"),
        P(("fsdp", "ctx"), "tp"),
    )
    return jax.shard_map(shards, mesh=mesh, in_specs=in_specs, out_specs=out_specs, check_vma=False)
```

```python
import functools
import math

import jax
import jax.numpy as jnp
from jax import lax
from jax.experimental import pallas as pl
from jax.experimental.pallas import tpu as pltpu
from jax.sharding import PartitionSpec as P

EPSILON = 1e-06
HIGHEST = lax.Precision.HIGHEST
NEGATIVE = -1e30


def passed_along(block, axis, distance):
    devices = range(lax.axis_size(axis))
    route = [(i - distance, i) for i in devices if i - distance in devices]
    return lax.ppermute(block, axis, route)


def group_algebra(queries, key_rows, house, betas):
    length = queries.shape[0]
    scaling = 1.0 / math.sqrt(queries.shape[1])
    row_index = lax.broadcasted_iota(jnp.int32, (length, length), 0)
    column_index = lax.broadcasted_iota(jnp.int32, (length, length), 1)
    strict_below = row_index > column_index
    house_gram = jnp.dot(house, house.T, precision=HIGHEST)
    system = jnp.where(strict_below, house_gram, 0.0) + jnp.diag(1.0 / betas)
    identity = jnp.eye(length, dtype=house.dtype)
    inverse = jax.scipy.linalg.solve_triangular(system, identity, lower=True)
    query_house = jnp.where(
        row_index >= column_index, jnp.dot(queries, house.T, precision=HIGHEST), 0.0
    )
    house_key = jnp.where(strict_below, jnp.dot(house, key_rows.T, precision=HIGHEST), 0.0)
    query_side = jnp.dot(query_house, inverse, precision=HIGHEST)
    key_side = jnp.dot(inverse, house_key, precision=HIGHEST)
    scores = (
        jnp.dot(queries, key_rows.T, precision=HIGHEST)
        - jnp.dot(query_side, house_key, precision=HIGHEST)
    ) * scaling
    query_bar = queries - jnp.dot(query_side, house, precision=HIGHEST)
    key_bar = key_rows - jnp.dot(key_side.T, house, precision=HIGHEST)
    inner = jnp.dot(inverse, house, precision=HIGHEST)
    factor = jnp.eye(house.shape[1], dtype=house.dtype) - jnp.dot(house.T, inner, precision=HIGHEST)
    return (scores, query_bar, key_bar, factor)


def local_map(queries, key_rows, house_raw, beta_logits):
    house = house_raw * lax.rsqrt(jnp.sum(house_raw * house_raw, axis=-1, keepdims=True) + EPSILON)
    betas = 2.0 * jax.nn.sigmoid(beta_logits)
    return jax.vmap(jax.vmap(group_algebra))(queries, key_rows, house, betas)


def doc_starts_local(segment_ids, group_first, first_position):
    length = segment_ids.shape[-1]
    previous = jnp.concatenate([segment_ids[..., :1], segment_ids[..., :-1]], axis=-1)
    offsets = lax.broadcasted_iota(jnp.int32, segment_ids.shape, segment_ids.ndim - 1)
    boundary = (offsets > 0) & (segment_ids != previous)
    marks = jnp.where(boundary, offsets + first_position, -1)
    row_index = lax.broadcasted_iota(jnp.int32, (length, length), 0)
    column_index = lax.broadcasted_iota(jnp.int32, (length, length), 1)
    seen = jnp.where(column_index <= row_index, marks[..., None, :], -1)
    return jnp.maximum(jnp.max(seen, axis=-1), group_first)


def norm_rows(values):
    factor = lax.rsqrt(jnp.mean(values * values, axis=-1, keepdims=True) + EPSILON)
    return (values * factor, factor)


def norm_back(gradient, normed, factor, norm_gain):
    scaled = gradient * norm_gain
    return factor * (scaled - normed * jnp.mean(scaled * normed, axis=-1, keepdims=True))


def split_heads(tensor, head_count):
    seq_count, length, total_width = tensor.shape
    return tensor.reshape(seq_count, length, head_count, total_width // head_count).transpose(
        0, 2, 1, 3
    )


def join_heads(tensor):
    seq_count, head_count, length, head_width = tensor.shape
    return tensor.transpose(0, 2, 1, 3).reshape(seq_count, length, head_count * head_width)


def project(inputs, weight):
    return jnp.einsum("scd,df->scf", inputs, weight, preferred_element_type=jnp.float32)


def project_back(gradient, weight):
    return jnp.einsum("scf,df->scd", gradient, weight, preferred_element_type=jnp.float32)


def weight_grad(inputs, gradient):
    return jnp.einsum("scd,scf->df", inputs, gradient, preferred_element_type=jnp.float32)


def cross_scores(query_rot, key_low, scaling):
    return (
        jnp.einsum("shqd,shkd->shqk", query_rot, key_low, preferred_element_type=jnp.float32)
        * scaling
    )


def weighted_values(weights, values_in):
    return jnp.einsum("shqk,shkd->shqd", weights, values_in, preferred_element_type=jnp.float32)


def ring_of_groups(
    hidden_in,
    segment_ids,
    doc_starts,
    norm1_gain,
    w_query,
    w_key,
    w_value,
    w_house,
    w_beta,
    w_out,
    norm2_gain,
    w_gate,
    w_up,
    w_down,
    output_grad,
):
    gathered = (
        lax.all_gather(norm1_gain, ("fsdp", "ctx"), axis=0, tiled=True),
        lax.all_gather(w_query, ("fsdp", "ctx"), axis=0, tiled=True),
        lax.all_gather(w_key, ("fsdp", "ctx"), axis=0, tiled=True),
        lax.all_gather(w_value, ("fsdp", "ctx"), axis=0, tiled=True),
        lax.all_gather(w_house, ("fsdp", "ctx"), axis=0, tiled=True),
        lax.all_gather(w_beta, ("fsdp", "ctx"), axis=0, tiled=True),
        lax.all_gather(w_out, ("fsdp", "ctx"), axis=0, tiled=True),
        lax.all_gather(norm2_gain, ("fsdp", "ctx"), axis=0, tiled=True),
        lax.all_gather(w_gate, ("fsdp", "ctx"), axis=0, tiled=True),
        lax.all_gather(w_up, ("fsdp", "ctx"), axis=0, tiled=True),
        lax.all_gather(w_down, ("fsdp", "ctx"), axis=0, tiled=True),
    )
    (
        gain_one,
        query_full,
        key_full,
        value_full,
        house_full,
        beta_full,
        out_full,
        gain_two,
        gate_full,
        up_full,
        down_full,
    ) = gathered
    gain_one_f = gain_one.astype(jnp.float32)
    gain_two_f = gain_two.astype(jnp.float32)
    head_count = beta_full.shape[1]
    length = hidden_in.shape[1]
    residual = hidden_in.astype(jnp.float32)
    normed_one, factor_one = norm_rows(residual)
    h_one = (normed_one * gain_one_f).astype(jnp.bfloat16)
    queries = split_heads(project(h_one, query_full), head_count)
    key_rows = split_heads(project(h_one, key_full), head_count)
    values_low = split_heads(project(h_one, value_full).astype(jnp.bfloat16), head_count)
    house_raw = split_heads(project(h_one, house_full), head_count)
    beta_logits = project(h_one, beta_full).transpose(0, 2, 1)
    (scores_local, query_bar, key_bar, factors), local_back = jax.vjp(
        local_map, queries, key_rows, house_raw, beta_logits
    )
    scaling = 1.0 / math.sqrt(queries.shape[-1])
    chain_index = lax.axis_index("ctx")
    hop_total = lax.axis_size("ctx") - 1
    first_position = chain_index * length
    starts = doc_starts_local(segment_ids, doc_starts, first_position)
    offsets = jnp.arange(length, dtype=jnp.int32)
    causal = (offsets[None, :] <= offsets[:, None])[None]
    local_mask = (causal & (offsets[None, None, :] + first_position >= starts[:, :, None]))[:, None]

    def hop_mask(distance):
        key_pos = (chain_index - distance) * length + offsets
        return (key_pos[None, None, :] >= starts[:, :, None])[:, None]

    masked_local = jnp.where(local_mask, scores_local, NEGATIVE)
    local_max = jnp.max(masked_local, axis=-1)
    local_sum = jnp.sum(jnp.exp(masked_local - local_max[..., None]), axis=-1)
    key_send = key_bar.astype(jnp.bfloat16)
    identity = jnp.broadcast_to(jnp.eye(factors.shape[-1], dtype=jnp.float32), factors.shape)
    stack_rot = jnp.zeros((hop_total,) + query_bar.shape, jnp.bfloat16)
    stack_factors = jnp.zeros((hop_total,) + factors.shape, jnp.float32)

    def rotate(hop_step, hop_keys, chain, run_max, run_sum):
        query_rot = jnp.einsum("shqa,shab->shqb", query_bar, chain, precision=HIGHEST).astype(
            jnp.bfloat16
        )
        masked = jnp.where(
            hop_mask(hop_step + 1), cross_scores(query_rot, hop_keys, scaling), NEGATIVE
        )
        new_max = jnp.maximum(run_max, jnp.max(masked, axis=-1))
        new_sum = run_sum * jnp.exp(run_max - new_max) + jnp.sum(
            jnp.exp(masked - new_max[..., None]), axis=-1
        )
        return (query_rot, new_max, new_sum)

    stack_keys = jnp.zeros((hop_total,) + key_send.shape, jnp.bfloat16)
    stack_values = jnp.zeros((hop_total,) + values_low.shape, jnp.bfloat16)

    def forward_hop(hop_step, loop_state):
        (
            send_keys,
            send_values,
            send_factor,
            kept_keys,
            kept_values,
            kept_rot,
            kept_factors,
            run_max,
            run_sum,
        ) = loop_state
        got_keys, got_values = passed_along((send_keys, send_values), "ctx", 1)
        got_factor = passed_along(send_factor.astype(jnp.bfloat16), "ctx", 1).astype(
            send_factor.dtype
        )
        query_rot, run_max, run_sum = rotate(hop_step, got_keys, got_factor, run_max, run_sum)
        kept_keys = lax.dynamic_update_index_in_dim(kept_keys, got_keys, hop_step, 0)
        kept_values = lax.dynamic_update_index_in_dim(kept_values, got_values, hop_step, 0)
        kept_rot = lax.dynamic_update_index_in_dim(kept_rot, query_rot, hop_step, 0)
        kept_factors = lax.dynamic_update_index_in_dim(kept_factors, got_factor, hop_step, 0)
        next_factor = jnp.einsum("shab,shbc->shac", factors, got_factor, precision=HIGHEST)
        return (
            got_keys,
            got_values,
            next_factor,
            kept_keys,
            kept_values,
            kept_rot,
            kept_factors,
            run_max,
            run_sum,
        )

    loop_state = lax.fori_loop(
        0,
        hop_total,
        forward_hop,
        (
            key_send,
            values_low,
            identity,
            stack_keys,
            stack_values,
            stack_rot,
            stack_factors,
            local_max,
            local_sum,
        ),
    )
    stack_keys, stack_values, stack_rot, stack_factors = (
        loop_state[3],
        loop_state[4],
        loop_state[5],
        loop_state[6],
    )
    run_max, run_sum = (loop_state[7], loop_state[8])

    def fetch(hop_step):
        return (
            lax.dynamic_index_in_dim(stack_keys, hop_step, 0, keepdims=False),
            lax.dynamic_index_in_dim(stack_values, hop_step, 0, keepdims=False),
        )

    log_total = run_max + jnp.log(run_sum)

    def recall(hop_step):
        hop_keys, hop_values = fetch(hop_step)
        hop_factor = lax.dynamic_index_in_dim(stack_factors, hop_step, 0, keepdims=False)
        query_rot = lax.dynamic_index_in_dim(stack_rot, hop_step, 0, keepdims=False)
        masked = jnp.where(
            hop_mask(hop_step + 1), cross_scores(query_rot, hop_keys, scaling), NEGATIVE
        )
        hop_probs = jnp.exp(masked - log_total[..., None])
        return (hop_keys, hop_values, hop_factor, query_rot, hop_probs)

    probs_local = jnp.exp(masked_local - log_total[..., None])
    probs_local_low = probs_local.astype(jnp.bfloat16)
    attn_acc = weighted_values(probs_local_low, values_low)
    attn_rest = weighted_values(
        (probs_local - probs_local_low.astype(jnp.float32)).astype(jnp.bfloat16), values_low
    )

    def value_hop(hop_step, running):
        total_low, total_rest = running
        hop_keys, hop_values, hop_factor, query_rot, hop_probs = recall(hop_step)
        hop_low = hop_probs.astype(jnp.bfloat16)
        total_low = total_low + weighted_values(hop_low, hop_values)
        total_rest = total_rest + weighted_values(
            (hop_probs - hop_low.astype(jnp.float32)).astype(jnp.bfloat16), hop_values
        )
        return (total_low, total_rest)

    attn_acc, attn_rest = lax.fori_loop(0, hop_total, value_hop, (attn_acc, attn_rest))
    attn_low = join_heads(attn_acc.astype(jnp.bfloat16))
    branch = lax.psum(project_back(attn_low, out_full), "tp")
    middle = residual + branch
    normed_two, factor_two = norm_rows(middle)
    h_two = (normed_two * gain_two_f).astype(jnp.bfloat16)
    gate_proj = project(h_two, gate_full)
    up_proj = project(h_two, up_full)
    gate_sigmoid = jax.nn.sigmoid(gate_proj)
    silu_gate = gate_proj * gate_sigmoid
    hidden_low = (silu_gate * up_proj).astype(jnp.bfloat16)
    mlp_out = lax.psum(project_back(hidden_low, down_full).astype(jnp.bfloat16), "tp").astype(
        jnp.float32
    )
    block_out = (middle + mlp_out).astype(jnp.bfloat16)
    down_grad = weight_grad(output_grad, hidden_low)
    d_hidden = project(output_grad, down_full)
    d_gate = (d_hidden * up_proj * gate_sigmoid * (1.0 + gate_proj * (1.0 - gate_sigmoid))).astype(
        jnp.bfloat16
    )
    d_up = (d_hidden * silu_gate).astype(jnp.bfloat16)
    gate_grad = weight_grad(h_two, d_gate)
    up_grad = weight_grad(h_two, d_up)
    d_two = lax.psum(project_back(d_gate, gate_full) + project_back(d_up, up_full), "tp")
    gain_two_grad = jnp.sum(d_two * normed_two, axis=(0, 1))
    d_middle = output_grad.astype(jnp.float32) + norm_back(
        d_two, normed_two, factor_two, gain_two_f
    )
    d_branch = d_middle.astype(jnp.bfloat16)
    out_grad = weight_grad(d_branch, attn_low)
    d_attn = split_heads(project(d_branch, out_full).astype(jnp.bfloat16), head_count)
    d_probs_local = jnp.einsum(
        "shqd,shkd->shqk", d_attn, values_low, preferred_element_type=jnp.float32
    )
    row_delta = jnp.sum(d_attn.astype(jnp.float32) * (attn_acc + attn_rest), axis=-1)
    zero_factor = jnp.zeros(factors.shape, jnp.float32)
    zero_bar = jnp.zeros(query_bar.shape, jnp.float32)

    def back_hop(back_step, loop_state):
        carry_keys, carry_values, carry_factor, d_bar, d_factors = loop_state
        hop_step = hop_total - 1 - back_step
        hop_keys, hop_values, hop_factor, query_rot, hop_probs = recall(hop_step)
        d_probs = jnp.einsum(
            "shqd,shkd->shqk", d_attn, hop_values, preferred_element_type=jnp.float32
        )
        d_cross = (hop_probs * (d_probs - row_delta[..., None])).astype(jnp.bfloat16)
        d_rot = (
            jnp.einsum("shqk,shkd->shqd", d_cross, hop_keys, preferred_element_type=jnp.float32)
            * scaling
        )
        d_bar = d_bar + jnp.einsum("shqb,shab->shqa", d_rot, hop_factor, precision=HIGHEST)
        factor_local = jnp.einsum("shqa,shqb->shab", query_bar, d_rot, precision=HIGHEST)
        keys_total = (
            carry_keys
            + jnp.einsum("shqk,shqd->shkd", d_cross, query_rot, preferred_element_type=jnp.float32)
            * scaling
        )
        values_total = carry_values + jnp.einsum(
            "shqk,shqd->shkd",
            hop_probs.astype(jnp.bfloat16),
            d_attn,
            preferred_element_type=jnp.float32,
        )
        factor_total = factor_local + jnp.einsum(
            "shba,shbc->shac", factors, carry_factor, precision=HIGHEST
        )
        d_factors = d_factors + jnp.einsum(
            "shac,shbc->shab", carry_factor, hop_factor, precision=HIGHEST
        )
        carry_keys, carry_values, carry_factor = (
            passed_along(keys_total.astype(jnp.bfloat16), "ctx", -1).astype(keys_total.dtype),
            passed_along(values_total.astype(jnp.bfloat16), "ctx", -1).astype(values_total.dtype),
            passed_along(factor_total.astype(jnp.bfloat16), "ctx", -1).astype(factor_total.dtype),
        )
        return (carry_keys, carry_values, carry_factor, d_bar, d_factors)

    zero_rows = jnp.zeros(key_send.shape, jnp.float32)
    loop_state = lax.fori_loop(
        0, hop_total, back_hop, (zero_rows, zero_rows, zero_factor, zero_bar, zero_factor)
    )
    carry_keys, carry_values, d_bar, d_factors = (
        loop_state[0],
        loop_state[1],
        loop_state[3],
        loop_state[4],
    )
    d_local = probs_local * (d_probs_local - row_delta[..., None])
    values_sum = carry_values + jnp.einsum(
        "shqk,shqd->shkd", probs_local_low, d_attn, preferred_element_type=jnp.float32
    )
    d_queries, d_keys, d_house, d_betas = local_back((d_local, d_bar, carry_keys, d_factors))
    query_low = join_heads(d_queries.astype(jnp.bfloat16))
    key_low = join_heads(d_keys.astype(jnp.bfloat16))
    value_low = join_heads(values_sum.astype(jnp.bfloat16))
    house_low = join_heads(d_house.astype(jnp.bfloat16))
    beta_low = d_betas.transpose(0, 2, 1).astype(jnp.bfloat16)
    query_grad = weight_grad(h_one, query_low)
    key_grad = weight_grad(h_one, key_low)
    value_grad = weight_grad(h_one, value_low)
    house_grad = weight_grad(h_one, house_low)
    beta_grad = weight_grad(h_one, beta_low)
    partial_one = (
        project_back(query_low, query_full)
        + project_back(key_low, key_full)
        + project_back(value_low, value_full)
    )
    partial_one = (
        partial_one + project_back(house_low, house_full) + project_back(beta_low, beta_full)
    )
    d_one = lax.psum(partial_one.astype(jnp.bfloat16), "tp").astype(jnp.float32)
    gain_one_grad = jnp.sum(d_one * normed_one, axis=(0, 1))
    input_grad = (d_middle + norm_back(d_one, normed_one, factor_one, gain_one_f)).astype(
        jnp.bfloat16
    )

    def scattered(partial):
        first = lax.psum_scatter(partial, "fsdp", scatter_dimension=0, tiled=True)
        return lax.psum_scatter(first, "ctx", scatter_dimension=0, tiled=True)

    results = tuple(
        (
            scattered(gain_one_grad.astype(jnp.bfloat16)).astype(jnp.float32),
            scattered(query_grad.astype(jnp.bfloat16)).astype(jnp.float32),
            scattered(key_grad.astype(jnp.bfloat16)).astype(jnp.float32),
            scattered(value_grad.astype(jnp.bfloat16)).astype(jnp.float32),
            scattered(house_grad.astype(jnp.bfloat16)).astype(jnp.float32),
            scattered(beta_grad.astype(jnp.bfloat16)).astype(jnp.float32),
            scattered(out_grad.astype(jnp.bfloat16)).astype(jnp.float32),
            scattered(gain_two_grad.astype(jnp.bfloat16)).astype(jnp.float32),
            scattered(gate_grad.astype(jnp.bfloat16)).astype(jnp.float32),
            scattered(up_grad.astype(jnp.bfloat16)).astype(jnp.float32),
            scattered(down_grad.astype(jnp.bfloat16)).astype(jnp.float32),
        )
    )
    return (block_out, input_grad) + results


def halves(value):
    high = value.astype(jnp.bfloat16)
    return high, (value - high.astype(jnp.float32)).astype(jnp.bfloat16)


AB = (((1,), (0,)), ((), ()))
ABT = (((1,), (1,)), ((), ()))
ATB = (((0,), (0,)), ((), ()))


def mm(a, b, dims=AB):
    return lax.dot_general(a, b, dims, preferred_element_type=jnp.float32)


def mm3(a, b, dims=AB):
    left, right = dims[0][0][0], dims[0][1][0]
    return mm(
        jnp.concatenate([a[0], a[1], a[0]], axis=left),
        jnp.concatenate([b[0], b[0], b[1]], axis=right),
        dims,
    )


def each(function, *lists):
    return [function(*values) for values in zip(*lists)]


def square_index(size):
    row = lax.broadcasted_iota(jnp.int32, (size, size), 0)
    return row, lax.broadcasted_iota(jnp.int32, (size, size), 1)


def unit_lower_inverses(strict):
    size = strict[0].shape[0]
    part, half = size // 4, size // 2
    lane = lax.broadcasted_iota(jnp.int32, (part, size), 1)
    row = lax.broadcasted_iota(jnp.int32, (part, size), 0)
    block = lane // part
    col = lane - block * part
    own = [block == b for b in range(4)]
    zero = jnp.zeros((part, size), jnp.bfloat16)

    def side_by_side(matrix, below):
        packed = jnp.zeros((part, size), jnp.float32)
        for b in range(4 - below):
            packed = jnp.where(own[b], matrix[(b + below) * part : (b + below + 1) * part], packed)
        return packed

    def stacked(pair, order=(0, 1, 2, 3)):
        return tuple(
            jnp.concatenate(
                [zero if b is None else jnp.where(own[b], value, zero) for b in order], axis=0
            )
            for value in pair
        )

    diagonal = [side_by_side(matrix, 0) for matrix in strict]
    inverse = [
        jnp.where(row == col, 1.0, 0.0) - jnp.where((row >> 1) == (col >> 1), matrix, 0.0)
        for matrix in diagonal
    ]
    level = 1
    while (1 << level) < part:
        joined = ((row >> (level + 1)) == (col >> (level + 1))) & ((row >> level) != (col >> level))
        pairs = each(halves, inverse)
        steps = [
            mm3(halves(jnp.where(joined, matrix, 0.0)), stacked(pair))
            for matrix, pair in zip(diagonal, pairs)
        ]
        inverse = [
            value - mm3(pair, stacked(halves(step)))
            for value, pair, step in zip(inverse, pairs, steps)
        ]
        level += 1
    pairs = each(halves, inverse)
    even = own[0] | own[2]
    steps = [
        mm3(halves(jnp.where(even, side_by_side(matrix, 1), 0.0)), stacked(pair))
        for matrix, pair in zip(strict, pairs)
    ]
    corners = [
        -mm3(pair, stacked(halves(step), (None, 0, None, 2))) for pair, step in zip(pairs, steps)
    ]

    def joined_block(value, corner, n):
        lanes = slice(n * half, (n + 1) * half)
        upper = jnp.where(own[2 * n], value, 0.0)[:, lanes]
        return jnp.concatenate([upper, jnp.where(own[2 * n], corner, value)[:, lanes]], axis=0)

    first = [joined_block(value, corner, 0) for value, corner in zip(inverse, corners)]
    last = [joined_block(value, corner, 1) for value, corner in zip(inverse, corners)]
    steps = [mm3(halves(matrix[half:, :half]), halves(value)) for matrix, value in zip(strict, first)]
    lower = [-mm3(halves(value), halves(step)) for value, step in zip(last, steps)]
    blank = jnp.zeros((half, half), jnp.float32)
    return [
        jnp.concatenate(
            [
                jnp.concatenate([top, blank], axis=1),
                jnp.concatenate([left, right], axis=1),
            ],
            axis=0,
        )
        for top, left, right in zip(first, lower, last)
    ]


def unit_rows(raw):
    norm = lax.rsqrt(jnp.sum(raw * raw, axis=1, keepdims=True) + EPSILON)
    return raw * norm, norm


def below(matrix, row, col):
    return jnp.where(row > col, matrix, 0.0)


def key_halves(house_raw, keys, betas):
    row, col = square_index(keys[0].shape[0])
    house = [unit_rows(raw)[0] for raw in house_raw]
    scaled = [halves(beta * value) for beta, value in zip(betas, house)]
    strict = [below(mm3(a, halves(b), ABT), row, col) for a, b in zip(scaled, house)]
    house_key = [halves(below(mm3(a, halves(b), ABT), row, col)) for a, b in zip(scaled, keys)]
    inverses = unit_lower_inverses(strict)
    return inverses, [mm3(halves(a), b) for a, b in zip(inverses, house_key)]


def query_halves(queries, values, house_raw, keys, inverses, key_side, allowed):
    row, col = square_index(keys[0].shape[0])
    scaling = 1.0 / math.sqrt(queries[0].shape[1])
    q = each(halves, queries)
    query_house = [
        halves(jnp.where(row >= col, mm3(a, halves(unit_rows(raw)[0]), ABT), 0.0))
        for a, raw in zip(q, house_raw)
    ]
    scores = [mm3(a, halves(b), ABT) for a, b in zip(q, keys)]
    scores = [score - mm3(a, halves(b)) for score, a, b in zip(scores, query_house, key_side)]
    masked = [jnp.where(allowed, score * scaling, NEGATIVE) for score in scores]
    weights = [jnp.exp(value - jnp.max(value, axis=1, keepdims=True)) for value in masked]
    probs = [value / jnp.sum(value, axis=1, keepdims=True) for value in weights]
    attn = [mm(prob.astype(jnp.bfloat16), value) for prob, value in zip(probs, values)]
    return attn, probs, [mm3(a, halves(b)) for a, b in zip(query_house, inverses)]


def heads_backward(queries, keys, house_raw, values, betas, probs, key_side, query_side, d_attn):
    row, col = square_index(keys[0].shape[0])
    scaling = 1.0 / math.sqrt(queries[0].shape[1])
    house, norm = zip(*[unit_rows(raw) for raw in house_raw])
    d_values = [mm(prob.astype(jnp.bfloat16), d, ATB) for prob, d in zip(probs, d_attn)]
    d_probs = [mm(d, value, ABT) for d, value in zip(d_attn, values)]
    d_scores = [
        halves(prob * (d - jnp.sum(prob * d, axis=1, keepdims=True)) * scaling)
        for prob, d in zip(probs, d_probs)
    ]
    q, k, w = each(halves, queries), each(halves, keys), each(halves, house)
    scaled = [halves(beta * value) for beta, value in zip(betas, house)]
    side = each(halves, query_side)
    d_side = [-mm3(d, halves(value), ABT) for d, value in zip(d_scores, key_side)]
    d_query_house = [halves(jnp.where(row >= col, d, 0.0)) for d in d_side]
    d_strict = [halves(below(-mm3(a, halves(d), ATB), row, col)) for a, d in zip(side, d_side)]
    d_house_key = [halves(below(-mm3(a, d, ATB), row, col)) for a, d in zip(side, d_scores)]
    d_queries = [mm3(d, a) + mm3(e, b) for d, a, e, b in zip(d_scores, k, d_query_house, w)]
    d_keys = [
        mm3(d, a, ATB) + mm3(e, b, ATB) for d, a, e, b in zip(d_scores, q, d_house_key, scaled)
    ]
    d_scaled = [mm3(d, a) + mm3(e, b) for d, a, e, b in zip(d_strict, w, d_house_key, k)]
    d_house = [
        mm3(d, a, ATB) + mm3(e, b, ATB) for d, a, e, b in zip(d_strict, scaled, d_query_house, q)
    ]
    d_betas = [jnp.sum(d * value, axis=1, keepdims=True) for d, value in zip(d_scaled, house)]
    d_house = [d + beta * e for d, beta, e in zip(d_house, betas, d_scaled)]
    d_house_raw = [
        n * (d - value * jnp.sum(d * value, axis=1, keepdims=True))
        for n, d, value in zip(norm, d_house, house)
    ]
    d_logits = [d * beta * (1.0 - 0.5 * beta) for d, beta in zip(d_betas, betas)]
    return d_queries, d_keys, d_house_raw, d_values, d_logits


def head_slices(ref, first, heads, head):
    return [ref[:, first + n * head : first + (n + 1) * head] for n in range(heads)]


def started(pairs, sems):
    copies = [
        pltpu.make_async_copy(source, target, sems.at[n]) for n, (source, target) in enumerate(pairs)
    ]
    for copy in copies:
        copy.start()
    return copies


def token_rows(places, n, k, quarter):
    return pl.ds(pl.multiple_of(places[8 + n] + places[18 + k], 16), quarter)


def placed(gathered, whole, places):
    quarter = gathered.shape[1] // 4
    return [
        (
            gathered.at[n, pl.ds(k * quarter, quarter)],
            whole.at[pl.ds(pl.multiple_of(places[18 + k] + n * quarter, 16), quarter)],
        )
        for n in range(4)
        for k in range(4)
    ]


def split_tokens(whole, parts, places):
    quarter = parts[0].shape[0] // 4
    for n in range(4):
        for k in range(4):
            parts[n][pl.ds(k * quarter, quarter)] = whole[token_rows(places, n, k, quarter)]


def wide_row(row, rows):
    return jnp.broadcast_to(row, (rows, row.shape[1])).astype(jnp.bfloat16)


def own_blocks(places, source, target, sequence=26, at=0):
    quarter = target.shape[-2]
    rows = pl.ds(pl.multiple_of(places[22], 16), quarter)
    return [(source.at[places[sequence + k], rows], target.at[k + at]) for k in range(4)]


def message_kernel(places, hidden_in, ids, gain_one, gain_two, *refs):
    messages, blocks, sems = refs[0:4], refs[4], refs[5]
    quarter, features = blocks.shape[1], blocks.shape[2]
    rows, depth = ids.shape[1], gain_one.shape[0]
    copies = started(own_blocks(places, hidden_in, blocks), sems)
    for k in range(4):
        messages[k][:, features:] = jnp.zeros((quarter, 640), jnp.bfloat16)
        own_ids = ids[pl.ds(places[26 + k], 1)].astype(jnp.float32)
        messages[k][:, features : features + rows] = wide_row(own_ids, quarter)
        at = features + 128
        messages[k][:, at : at + depth] = wide_row(gain_one[...].astype(jnp.float32)[None], quarter)
        at += 256
        messages[k][:, at : at + depth] = wide_row(gain_two[...].astype(jnp.float32)[None], quarter)
    for copy in copies:
        copy.wait()
    for k in range(4):
        messages[k][:, :features] = blocks[k]


def attention_pack_kernel(places, house, key, beta, query, value, out, pack):
    at = 0
    for source in (house, key, beta, query, value, out):
        width = source.shape[1]
        if width < 128:
            pack[:, at : at + 128] = jnp.zeros((pack.shape[0], 128), jnp.bfloat16)
        pack[:, at : at + width] = source[...]
        at += max(width, 128)


def feed_forward_pack_kernel(places, output_grad, gate, up, down, *refs):
    messages, gives, keeps, blocks, sems = refs[0:4], refs[4:6], refs[6:8], refs[8], refs[9]
    copies = started(
        own_blocks(places, output_grad, blocks) + own_blocks(places, output_grad, blocks, 30, 4), sems
    )
    units = gate.shape[1] // 2
    part = units // 2
    for packs, start in ((keeps, places[23]), (gives, places[24])):
        for n in range(6):
            at = pl.ds(pl.multiple_of(start + n % 2 * part, 128), part)
            packs[n // 3][:, n % 3 * part : (n % 3 + 1) * part] = (gate, up, down)[n // 2][:, at]
    for copy in copies:
        copy.wait()
    for k in range(4):
        messages[k][0] = blocks[k]
        messages[k][1] = blocks[4 + k]


def out_message_kernel(places, *refs):
    out_parts, middle, messages = refs[0:4], refs[4], refs[5:9]
    quarter = middle.shape[0] // 4
    out = sum(part[...].astype(jnp.float32) for part in out_parts)
    own, pair = (middle[...] + out[0]).astype(jnp.bfloat16), out[1].astype(jnp.bfloat16)
    for k in range(4):
        messages[k][:quarter] = own[k * quarter : (k + 1) * quarter]
        messages[k][quarter:] = pair[(k ^ 2) * quarter : ((k ^ 2) + 1) * quarter]


def result_kernel(places, d_parts, d_middle, block, gain, gain_two_grad, *messages):
    quarter, features = block.shape[0] // 4, block.shape[1]
    d_one = sum(d_parts[n].astype(jnp.float32) for n in range(4))
    x = block[...].astype(jnp.float32)
    factor = lax.rsqrt(jnp.mean(x * x, axis=1, keepdims=True) + EPSILON)
    normed = x * factor
    scaled = d_one * gain[...]
    mean = jnp.mean(scaled * normed, axis=1, keepdims=True)
    in_grad = (d_middle[...] + factor * (scaled - normed * mean)).astype(jnp.bfloat16)
    gain_one_grad = jnp.sum(d_one * normed, axis=0, keepdims=True)
    row = lax.broadcasted_iota(jnp.int32, (quarter, 128), 0)
    for g, gains in enumerate((gain_one_grad, gain_two_grad[...])):
        packed = jnp.zeros((quarter, 128), jnp.float32)
        for n in range(features // 128):
            packed = jnp.where(row == n, gains[:, n * 128 : (n + 1) * 128], packed)
        at = features + g * 128
        for k in range(4):
            messages[k][:, at : at + 128] = packed.astype(jnp.bfloat16)
    for k in range(4):
        messages[k][:, :features] = in_grad[k * quarter : (k + 1) * quarter]


def spread_kernel(places, pieces, whole):
    quarter, features = whole.shape[1] // 4, whole.shape[2]
    for n in range(4):
        for k in range(4):
            rows = slice(k * quarter, (k + 1) * quarter)
            whole[pl.ds(places[26 + k], 1), n * quarter : (n + 1) * quarter] = pieces[
                n, rows, :features
            ][None]


def gradient_spread_kernel(places, pieces, whole, gains):
    quarter, features = whole.shape[1] // 4, whole.shape[2]
    spread_kernel(places, pieces, whole)
    gains[...] = sum(pieces[n, :quarter, features:].astype(jnp.float32) for n in range(4))


def weights_in_place(pieces, whole, places, first=0, count=None):
    depth = pieces[0].shape[0]
    width = count or pieces[0].shape[1]
    return [
        (
            pieces[n].at[:, pl.ds(first, width)],
            whole.at[pl.ds(pl.multiple_of(places[n], 64), depth), pl.ds(0, width)],
        )
        for n in range(8)
    ]


def keys_kernel(heads, places, *refs):
    weights, xs, gain = refs[0:8], refs[8], refs[9]
    h_all, proj, inverses, key_side = refs[10:14]
    w_all, weight_sems, x_sems, x_all = refs[14:18]
    x_copies = started(placed(xs, x_all, places), x_sems)
    w_copies = started(weights_in_place(weights, w_all, places, 0, w_all.shape[1]), weight_sems)
    for copy in x_copies:
        copy.wait()
    width = (proj.shape[1] - 128) // 2
    head = width // heads
    x = x_all[...].astype(jnp.float32)
    factor = lax.rsqrt(jnp.mean(x * x, axis=1, keepdims=True) + EPSILON)
    h_all[...] = (x * factor * gain[...]).astype(jnp.bfloat16)
    for copy in w_copies:
        copy.wait()
    proj[...] = mm(h_all[...], w_all[...])
    betas = 2.0 * jax.nn.sigmoid(proj[:, 2 * width :])
    results = key_halves(
        head_slices(proj, 0, heads, head),
        head_slices(proj, width, heads, head),
        [betas[:, n : n + 1] for n in range(heads)],
    )
    for n in range(heads):
        inverses[n], key_side[n] = results[0][n], results[1][n]


def queries_kernel(heads, places, *refs):
    weights, (h_all, proj_keys, inverses, key_side, id_row, id_col) = refs[0:8], refs[8:14]
    proj, attn, probs, query_side, parts = refs[14], refs[15], refs[16], refs[17], refs[18:22]
    w_all, total, sems = refs[22:25]
    skip = weights[0].shape[1] - w_all.shape[1]
    for copy in started(weights_in_place(weights, w_all, places, skip, w_all.shape[1]), sems):
        copy.wait()
    width = attn.shape[1]
    head = width // heads
    proj[...] = mm(h_all[...], w_all[:, : 2 * width])
    row, col = square_index(h_all.shape[0])
    results = query_halves(
        head_slices(proj, 0, heads, head),
        [value.astype(jnp.bfloat16) for value in head_slices(proj, width, heads, head)],
        head_slices(proj_keys, 0, heads, head),
        head_slices(proj_keys, width, heads, head),
        [inverses[n] for n in range(heads)],
        [key_side[n] for n in range(heads)],
        (col <= row) & (id_row[...] == id_col[...]),
    )
    for n in range(heads):
        attn[:, n * head : (n + 1) * head] = results[0][n].astype(jnp.bfloat16)
        probs[n], query_side[n] = results[1][n], results[2][n]
    total[...] = mm(attn[...], w_all[:, 2 * width :], ABT).astype(jnp.bfloat16)
    split_tokens(total, parts, places)


def feed_forward_kernel(places, *refs):
    weights, ins, grads = refs[0:16], refs[16:18], refs[18:22]
    two_parts, out_parts, keeps, sends = refs[22:30], refs[30:34], refs[34], refs[35]
    w_all, in_all, grad_all, total, weight_sems, in_sems, grad_sems = refs[36:43]
    rows, units, half = two_parts[0].shape[0], w_all.shape[1] // 3, w_all.shape[0] // 2

    def block(s, n):
        return pl.ds(pl.multiple_of(places[8 + n] * 4 + s * 4 * rows, 64), rows)

    depth, part = weights[0].shape[0], w_all.shape[1] // 2
    w_pairs = []
    for n in range(16):
        row = pl.ds(pl.multiple_of(places[n // 2], 64), depth)
        w_pairs.append((weights[n], w_all.at[row, pl.ds(n % 2 * part, part)]))
    w_copies = started(w_pairs, weight_sems)
    grad_copies = started(
        [
            (grads[n].at[s], grad_all.at[block(s, n)])
            for n in range(4)
            for s in range(2)
        ],
        grad_sems,
    )
    in_copies = started(
        [(ins[s].at[n], in_all.at[pl.ds((s * 4 + n) * rows, rows)]) for s in range(2) for n in range(4)],
        in_sems,
    )
    for copy in w_copies + grad_copies + in_copies:
        copy.wait()
    both = mm(in_all[...], w_all[:, : 2 * units])
    d_hidden = mm(grad_all[...], w_all[:, 2 * units :])
    gate, up = both[:, :units], both[:, units:]
    sigmoid = jax.nn.sigmoid(gate)
    silu = gate * sigmoid
    hidden = (silu * up).astype(jnp.bfloat16)
    d_gate = (d_hidden * up * sigmoid * (1.0 + gate * (1.0 - sigmoid))).astype(jnp.bfloat16)
    d_up = (d_hidden * silu).astype(jnp.bfloat16)
    for target in (keeps, sends):
        at = 2 * half
        for value in (d_gate, d_up, hidden):
            target[:, at : at + units] = value
            at += units
    d_both = keeps[:, 2 * half : 2 * half + 2 * units]
    total[...] = mm(d_both, w_all[:, : 2 * units], ABT).astype(jnp.bfloat16)
    for s in range(2):
        for n in range(4):
            two_parts[s * 4 + n][...] = total[block(s, n)]
    total[...] = mm(hidden, w_all[:, 2 * units :], ABT).astype(jnp.bfloat16)
    for s in range(2):
        for n in range(4):
            out_parts[n][s] = total[block(s, n)]
    for target, place in ((keeps, 12), (sends, 13)):
        lanes = pl.ds(pl.multiple_of(places[place], 128), half)
        target[:, :half] = in_all[:, lanes]
        target[:, half : 2 * half] = grad_all[:, lanes]


def attention_backward_kernel(heads, places, *refs):
    weights, ds = refs[0:8], refs[8]
    proj_keys, proj, probs, key_side, query_side, h_all, attn = refs[9:16]
    keeps, sends, parts = refs[16:19]
    w_first, w_second, d_all, d_attn, total, first_sems, second_sems, d_sems = refs[19:27]
    half, width = d_all.shape[1] // 2, d_attn.shape[1]
    d_keys_all = keeps.at[:, pl.ds(2 * half, 2 * width + 128)]
    d_queries_all = keeps.at[:, pl.ds(2 * half + 2 * width + 128, 2 * width)]
    cut, rest = w_first.shape[1], w_second.shape[1]
    second_copies = started(weights_in_place(weights, w_second, places, cut, rest), second_sems)
    d_copies = started(placed(ds, d_all, places), d_sems)
    first_copies = started(weights_in_place(weights, w_first, places, 0, cut), first_sems)
    for copy in d_copies + second_copies:
        copy.wait()
    head = width // heads
    d_attn[...] = mm(d_all[...], w_second[:, 2 * width :]).astype(jnp.bfloat16)
    betas = 2.0 * jax.nn.sigmoid(proj_keys[:, 2 * width :])
    lane = lax.broadcasted_iota(jnp.int32, betas.shape, 1)
    logits = jnp.zeros(betas.shape, jnp.float32)
    results = heads_backward(
        head_slices(proj, 0, heads, head),
        head_slices(proj_keys, width, heads, head),
        head_slices(proj_keys, 0, heads, head),
        [value.astype(jnp.bfloat16) for value in head_slices(proj, width, heads, head)],
        [betas[:, n : n + 1] for n in range(heads)],
        [probs[n] for n in range(heads)],
        [key_side[n] for n in range(heads)],
        [query_side[n] for n in range(heads)],
        head_slices(d_attn, 0, heads, head),
    )
    for n in range(heads):
        d_queries, d_keys, d_house, d_values, d_logit = [result[n] for result in results]
        low_at, high_at = slice(n * head, (n + 1) * head), slice(width + n * head, width + (n + 1) * head)
        d_keys_all[:, low_at] = d_house.astype(jnp.bfloat16)
        d_keys_all[:, high_at] = d_keys.astype(jnp.bfloat16)
        d_queries_all[:, low_at] = d_queries.astype(jnp.bfloat16)
        d_queries_all[:, high_at] = d_values.astype(jnp.bfloat16)
        logits = jnp.where(lane == n, d_logit, logits)
    d_keys_all[:, 2 * width :] = logits.astype(jnp.bfloat16)
    for copy in first_copies:
        copy.wait()
    keeps[:, keeps.shape[1] - width :] = attn[...]
    sends[:, 2 * half :] = keeps[:, 2 * half :]
    for target, place in ((keeps, 12), (sends, 13)):
        lanes = pl.ds(pl.multiple_of(places[place], 128), half)
        target[:, :half] = h_all[:, lanes]
        target[:, half : 2 * half] = d_all[:, lanes]
    total[...] = (
        mm(d_keys_all[...], w_first[...], ABT) + mm(d_queries_all[...], w_second[:, : 2 * width], ABT)
    ).astype(jnp.bfloat16)
    quarter = parts.shape[1] // 4
    for n in range(4):
        for k in range(4):
            rows = pl.ds(pl.multiple_of(places[18 + k] + n * quarter, 16), quarter)
            parts[n, k * quarter : (k + 1) * quarter] = total[rows]


def weight_grad_kernel(groups, places, mine, came, *refs):
    outs, total = refs[:-1], refs[-1]
    half, at = total.shape[0], 0
    for left, start, width in groups:
        lefts, rights = slice(left * half, (left + 1) * half), slice(start, start + width)
        total[:, at : at + width] = (
            mm(mine[:, lefts], mine[:, rights], ATB) + mm(came[:, lefts], came[:, rights], ATB)
        ).astype(jnp.bfloat16)
        at += width
    depth, at = outs[0].shape[1], 0
    for n in range(0, len(outs), 2):
        width = outs[n].shape[2]
        for k in range(4):
            rows = pl.ds(pl.multiple_of(places[14 + k], 64), depth)
            outs[n + k % 2][k // 2] = total[rows, at : at + width]
        at += width


VMEM_BYTES = 56 * 1024 * 1024


def call(kernel, outs, scratch, places, operands, spaces, micros, out_spaces=None):
    vmem = pl.BlockSpec(memory_space=pltpu.VMEM)
    kinds = {"v": vmem, "a": pl.BlockSpec(memory_space=pl.ANY)}
    return pl.pallas_call(
        kernel,
        out_shape=[jax.ShapeDtypeStruct(shape, kind) for shape, kind in outs],
        in_specs=[pl.BlockSpec(memory_space=pltpu.SMEM)] + [kinds[s] for s in spaces],
        out_specs=[kinds[s] for s in out_spaces or "v" * len(outs)],
        scratch_shapes=scratch,
        compiler_params=pltpu.CompilerParams(vmem_limit_bytes=VMEM_BYTES),
        cost_estimate=pl.CostEstimate(
            flops=int(micros * 1e6), transcendentals=0, bytes_accessed=int(micros * 1e4)
        ),
    )(places, *operands)


def swap(block, axis, distance):
    size = lax.axis_size(axis)
    return lax.ppermute(block, axis, [(i, i ^ distance) for i in range(size)])


def gathered_tp(block):
    return lax.all_gather(block, "tp", axis=0)


def all_tp(block):
    return [block] + [swap(block, "tp", n) for n in (1, 2, 3)]


def to_owners(messages):
    return [messages[0]] + [swap(messages[n], "ctx", n) for n in (1, 2, 3)]


def sum_tp(parts):
    return [parts[0]] + [swap(parts[n], "tp", n) for n in (1, 2, 3)]


def add_up(blocks):
    total = blocks[0].astype(jnp.float32)
    for block in blocks[1:]:
        total = total + block.astype(jnp.float32)
    return total


def other_core(block):
    return swap(block, "fsdp", 1)


def whole_sequences(
    hidden_in,
    segment_ids,
    doc_starts,
    norm1_gain,
    w_query,
    w_key,
    w_value,
    w_house,
    w_beta,
    w_out,
    norm2_gain,
    w_gate,
    w_up,
    w_down,
    output_grad,
):
    low, wide = jnp.bfloat16, jnp.float32
    core, chain, column = lax.axis_index("fsdp"), lax.axis_index("ctx"), lax.axis_index("tp")
    rows, features = hidden_in.shape[1], hidden_in.shape[2]
    depth, width, heads = w_query.shape[0], w_query.shape[1], w_beta.shape[1]
    length, half, quarter = 4 * rows, features // 2, rows // 4
    units, used = w_gate.shape[1] // 2, 4 * width + 128
    near = jnp.arange(4, dtype=jnp.int32)
    upper = (chain // 2).astype(jnp.int32)
    places = jnp.concatenate(
        [
            (core * 4 + (chain ^ near)) * depth,
            ((1 - core) * 4 + (chain ^ near)) * depth,
            (column ^ near) * quarter,
            jnp.stack([core, 1 - core]) * half,
            (chain ^ near) * depth,
            (chain ^ near) * rows,
            jnp.stack([column * quarter, upper * units, (1 - upper) * units, upper]),
            chain ^ near,
            chain ^ near ^ 2,
        ]
    ).astype(jnp.int32)
    step = lax.optimization_barrier
    block = pltpu.VMEM((4, quarter, features), low)
    token_messages = call(
        message_kernel,
        [((quarter, features + 640), low)] * 4,
        [block, pltpu.SemaphoreType.DMA((4,))],
        places,
        [hidden_in, segment_ids, norm1_gain, norm2_gain],
        "avvv",
        2,
    )
    (pack,) = call(
        attention_pack_kernel,
        [((depth, used + width), low)],
        [],
        places,
        [w_house, w_key, w_beta, w_query, w_value, w_out],
        "v" * 6,
        2,
    )
    packed = call(
        feed_forward_pack_kernel,
        [((2, quarter, features), low)] * 4
        + [((depth, 3 * units // 2), low)] * 4,
        [pltpu.VMEM((8, quarter, features), low), pltpu.SemaphoreType.DMA((8,))],
        places,
        [output_grad, w_gate, w_up, w_down],
        "avvv",
        3,
    )
    x_messages, pack, grad_messages, gives, ffn_keeps = step(
        (to_owners(token_messages), pack, packed[:4], packed[4:6], packed[6:8])
    )

    pack_two, pack_one = swap(pack, "ctx", 2), swap(pack, "ctx", 1)
    x_block = jnp.concatenate([message[:, :features] for message in x_messages])
    x_pieces = gathered_tp(x_block)
    info = jnp.stack([message[0, features:] for message in x_messages])
    chosen = near[:, None] == (near[None, :] ^ chain)
    info = jnp.sum(jnp.where(chosen[:, :, None], info[None].astype(wide), 0.0), axis=1)
    ids = info[:, :rows].reshape(length)
    gains = jnp.concatenate(
        [info[:, 128 : 128 + depth], info[:, 384 : 384 + depth]], axis=1
    ).astype(low)
    id_row, id_col = ids[None, :], ids[:, None]
    id_row, id_col, pack_two, pack_one, x_pieces, pack, gains, grad_messages, gives = step(
        (id_row, id_col, pack_two, pack_one, x_pieces, pack, gains, grad_messages, gives)
    )

    pack_three = swap(pack_two, "ctx", 1)
    grad_messages = to_owners(grad_messages)
    pack_three, pack_two, pack_one, pack, gains, gives, grad_messages, ffn_keeps = step(
        (pack_three, pack_two, pack_one, pack, gains, gives, grad_messages, ffn_keeps)
    )

    attn_weights = [pack, pack_one, pack_two, pack_three]
    attn_weights = attn_weights + [other_core(piece) for piece in attn_weights]
    gains_other = other_core(gains)
    gains = jnp.where(core == 0, jnp.stack([gains, gains_other]), jnp.stack([gains_other, gains]))
    gain_one = gains[:, :, :depth].reshape(1, features).astype(wide)
    gain_two = gains[:, :, depth:].reshape(1, features).astype(wide)
    give_two = [swap(gives[0], "ctx", 2)]
    keep_one = [swap(ffn_keeps[0], "ctx", 1)]
    grads = jnp.stack(
        [
            jnp.concatenate([message[0] for message in grad_messages]),
            jnp.concatenate([grad_messages[n ^ 2][1] for n in range(4)]),
        ]
    )
    own_grad = grads[0]
    grad_pieces = all_tp(grads)
    square = ((heads, length, length), wide)
    h_all, proj_keys, inverses, key_side = call(
        functools.partial(keys_kernel, heads),
        [((length, features), low), ((length, 2 * width + 128), wide), square, square],
        [
            pltpu.VMEM((features, 2 * width + 128), low),
            pltpu.SemaphoreType.DMA((8,)),
            pltpu.SemaphoreType.DMA((16,)),
            pltpu.VMEM((length, features), low),
        ],
        places,
        [*attn_weights, x_pieces, gain_one],
        "a" * 9 + "v",
        20,
    )
    outs = call(
        functools.partial(queries_kernel, heads),
        [((length, 2 * width), wide), ((length, width), low), square, square]
        + [((rows, features), low)] * 4,
        [
            pltpu.VMEM((features, 3 * width), low),
            pltpu.VMEM((length, features), low),
            pltpu.SemaphoreType.DMA((8,)),
        ],
        places,
        [*attn_weights, h_all, proj_keys, inverses, key_side, id_row, id_col],
        "a" * 8 + "v" * 6,
        9,
    )
    proj, attn, probs, query_side = outs[:4]
    give_two, branch_parts, keep_one, grad_pieces, give_last, ffn_keeps = step(
        (give_two, outs[4:], keep_one, grad_pieces, gives[1], ffn_keeps)
    )
    give_two = give_two + [swap(give_last, "ctx", 2)]
    give_three = [swap(give_two[0], "ctx", 1)]
    middle = x_block.astype(wide) + add_up(sum_tp(branch_parts))
    normed_two, factor_two = norm_rows(middle)
    h_two = (normed_two * gain_two).astype(low)
    give_two, give_three, ffn_keeps, h_two = step((give_two, give_three, ffn_keeps, h_two))

    h_pair = swap(h_two, "ctx", 2)
    give_three = give_three + [swap(give_two[1], "ctx", 1)]
    keep_one = keep_one + [swap(ffn_keeps[1], "ctx", 1)]
    h_own = gathered_tp(h_two)
    h_pair, give_three, h_own, keep_one, give_two = step(
        (h_pair, give_three, h_own, keep_one, give_two)
    )
    ffn_weights = [*ffn_keeps, *keep_one, *give_two, *give_three]
    ffn_weights = ffn_weights + [other_core(piece) for piece in ffn_weights]
    h_pair = gathered_tp(h_pair)

    tokens = 2 * length
    pair = ((2, rows, features), low)
    outs = call(
        feed_forward_kernel,
        [((rows, features), low)] * 8 + [pair] * 4 + [((tokens, features + 3 * units), low)] * 2,
        [
            pltpu.VMEM((features, 3 * units), low),
            pltpu.VMEM((tokens, features), low),
            pltpu.VMEM((tokens, features), low),
            pltpu.VMEM((tokens, features), low),
            pltpu.SemaphoreType.DMA((16,)),
            pltpu.SemaphoreType.DMA((8,)),
            pltpu.SemaphoreType.DMA((8,)),
        ],
        places,
        [*ffn_weights, h_own, h_pair, *grad_pieces],
        "a" * 22,
        12,
    )
    own_parts, pair_parts, out_parts, keeps, sends = outs[:4], outs[4:8], outs[8:12], outs[12], outs[13]

    def grads_of(mine, came, groups, pieces=1):
        total = sum(group[2] for group in groups)
        return call(
            functools.partial(weight_grad_kernel, groups),
            [((2, depth, total // pieces), low)] * (2 * pieces),
            [pltpu.VMEM((half, total), low)],
            places,
            [mine, came],
            "vv",
            total / 400.0,
        )

    pair_sum = add_up(sum_tp(pair_parts)).astype(low)
    came, pair_sum, own_parts = step((other_core(sends), pair_sum, own_parts))

    two_other = swap(pair_sum, "ctx", 2)
    own_sum = add_up(sum_tp(own_parts))
    ffn_grads = grads_of(
        keeps, came, ((0, features, 2 * units), (1, features + 2 * units, units)), 2
    )
    d_two = own_sum + two_other.astype(wide)
    gain_two_grad = jnp.sum(d_two * normed_two, axis=0, keepdims=True)
    d_middle = own_grad.astype(wide) + norm_back(d_two, normed_two, factor_two, gain_two)
    d_low, ffn_grads = step((d_middle.astype(low), tuple(ffn_grads)))

    ffn_came = [swap(ffn_grads[1], "ctx", 1)]
    d_pieces = gathered_tp(d_low)
    ffn_sums = [add_up([ffn_grads[0], ffn_came[0]])]
    ffn_leave = ffn_sums[0][1].astype(low)
    d_pieces, out_parts, ffn_leave, ffn_far = step((d_pieces, out_parts, ffn_leave, ffn_grads[3]))

    ffn_other = [swap(ffn_leave, "ctx", 2)]
    ffn_came = ffn_came + [swap(ffn_far, "ctx", 1)]
    out_received = sum_tp(out_parts)
    back = call(
        functools.partial(attention_backward_kernel, heads),
        [((length, features + used + width), low)] * 2 + [((4, rows, features), low)],
        [
            pltpu.VMEM((features, 2 * width + 128), low),
            pltpu.VMEM((features, 3 * width), low),
            pltpu.VMEM((length, features), low),
            pltpu.VMEM((length, width), low),
            pltpu.VMEM((length, features), low),
            pltpu.SemaphoreType.DMA((8,)),
            pltpu.SemaphoreType.DMA((8,)),
            pltpu.SemaphoreType.DMA((16,)),
        ],
        places,
        [*attn_weights, d_pieces, proj_keys, proj, probs, key_side, query_side, h_all, attn],
        "a" * 9 + "v" * 7,
        14,
    )
    ffn_sums = ffn_sums + [add_up([ffn_grads[2], ffn_came[1]])]
    ffn_leave, ffn_other, out_received, (keeps, sends, d_parts) = step(
        (ffn_sums[1][1].astype(low), ffn_other, out_received, tuple(back))
    )

    came, keeps, d_parts, out_received, ffn_leave = step(
        (other_core(sends), keeps, d_parts, out_received, ffn_leave)
    )

    ffn_other = ffn_other + [swap(ffn_leave, "ctx", 2)]
    query_start = features + 2 * width + 128
    near_two, far_two = grads_of(
        keeps, came, ((0, query_start, 2 * width), (1, query_start + 2 * width, width))
    )
    out_received, near_two, far_two, keeps = step((out_received, near_two, far_two, keeps))
    two_came = swap(far_two, "ctx", 1)
    out_messages = call(
        out_message_kernel,
        [((2 * quarter, features), low)] * 4,
        [],
        places,
        [*out_received, middle],
        "v" * 5,
        2,
    )
    out_messages, keeps = step((tuple(out_messages), keeps))
    out_messages = to_owners(out_messages)
    near_one, far_one = grads_of(keeps, came, ((0, features, 2 * width + 128),))
    d_parts, near_one, far_one = step((d_parts, near_one, far_one))
    d_received = lax.all_to_all(d_parts, "tp", 0, 0)
    messages = call(
        result_kernel,
        [((quarter, features + 256), low)] * 4,
        [],
        places,
        [d_received, d_middle, x_block, gain_one, gain_two_grad],
        "v" * 5,
        3,
    )
    two_sum = add_up([near_two, two_came])
    two_leave, near_one, far_one, messages, out_messages, ffn_other = step(
        (two_sum[1].astype(low), near_one, far_one, tuple(messages), out_messages, ffn_other)
    )

    one_came = swap(far_one, "ctx", 1)
    query_other = swap(two_leave, "ctx", 2)
    messages = step(to_owners(messages))
    owned = jnp.concatenate([message[:, :features] for message in messages])
    gain_sum = add_up([message[:, features:] for message in messages]).astype(low)
    owned = jnp.concatenate([owned, jnp.pad(gain_sum, ((0, 3 * quarter), (0, 0)))], axis=1)
    input_grad, gain_total = call(
        gradient_spread_kernel,
        [((4, rows, features), low), ((quarter, 256), wide)],
        [],
        places,
        [gathered_tp(owned)],
        "v",
        3,
    )
    one_sum = add_up([near_one, one_came])
    out_block = jnp.concatenate(
        [add_up([out_messages[n][:quarter], out_messages[n ^ 2][quarter:]]) for n in range(4)]
    ).astype(low)
    one_leave, input_grad, gain_total, query_other, out_block = step(
        (one_sum[1].astype(low), input_grad, gain_total, query_other, out_block)
    )

    key_other = swap(one_leave, "ctx", 2)
    block_out = call(
        spread_kernel, [((4, rows, features), low)], [], places, [gathered_tp(out_block)], "v", 2
    )[0]
    gain_total = gain_total + other_core(gain_total)
    gain_total = jnp.concatenate(
        [gain_total[: features // 128, :128], gain_total[: features // 128, 128:]]
    ).reshape(2, features)
    gain_total = lax.dynamic_slice_in_dim(gain_total, (core * 4 + chain) * depth, depth, axis=1)
    query_grads = two_sum[0] + query_other.astype(wide)
    key_grads = one_sum[0] + key_other.astype(wide)

    ffn_kept = jnp.concatenate([total[0] for total in ffn_sums], axis=1)
    ffn_other = jnp.concatenate(ffn_other, axis=1).astype(wide)

    def ffn_result(n):
        kept = ffn_kept[:, n * units : (n + 1) * units]
        came = ffn_other[:, n * units : (n + 1) * units]
        return jnp.concatenate(
            [jnp.where(upper == 1, came, kept), jnp.where(upper == 1, kept, came)], axis=1
        )

    return (
        block_out,
        input_grad,
        gain_total[0],
        query_grads[:, :width],
        key_grads[:, width : 2 * width],
        query_grads[:, width : 2 * width],
        key_grads[:, :width],
        key_grads[:, 2 * width : 2 * width + heads],
        query_grads[:, 2 * width :],
        gain_total[1],
        ffn_result(0),
        ffn_result(1),
        ffn_result(2),
    )


def shards(*args):
    sizes = [lax.axis_size(axis) for axis in ("fsdp", "ctx", "tp")]
    if sizes == [2, 4, 4] and args[0].shape[:2] == (4, 64):
        return whole_sequences(*args)
    return ring_of_groups(*args)


def solution(mesh):
    in_specs = (
        P("fsdp", "ctx", None),
        P("fsdp", "ctx"),
        P("fsdp", "ctx"),
        P(("fsdp", "ctx")),
        P(("fsdp", "ctx"), "tp"),
        P(("fsdp", "ctx"), "tp"),
        P(("fsdp", "ctx"), "tp"),
        P(("fsdp", "ctx"), "tp"),
        P(("fsdp", "ctx"), "tp"),
        P(("fsdp", "ctx"), "tp"),
        P(("fsdp", "ctx")),
        P(("fsdp", "ctx"), "tp"),
        P(("fsdp", "ctx"), "tp"),
        P(("fsdp", "ctx"), "tp"),
        P("fsdp", "ctx", None),
    )
    out_specs = (
        P("fsdp", "ctx", None),
        P("fsdp", "ctx", None),
        P(("fsdp", "ctx")),
        P(("fsdp", "ctx"), "tp"),
        P(("fsdp", "ctx"), "tp"),
        P(("fsdp", "ctx"), "tp"),
        P(("fsdp", "ctx"), "tp"),
        P(("fsdp", "ctx"), "tp"),
        P(("fsdp", "ctx"), "tp"),
        P(("fsdp", "ctx")),
        P(("fsdp", "ctx"), "tp"),
        P(("fsdp", "ctx"), "tp"),
        P(("fsdp", "ctx"), "tp"),
    )
    return jax.shard_map(shards, mesh=mesh, in_specs=in_specs, out_specs=out_specs, check_vma=False)
```

```python
import functools
import math

import jax
import jax.numpy as jnp
from jax import lax
from jax.experimental import pallas as pl
from jax.experimental.pallas import tpu as pltpu
from jax.sharding import PartitionSpec as P

EPSILON = 1e-06
HIGHEST = lax.Precision.HIGHEST
NEGATIVE = -1e30


def passed_along(block, axis, distance):
    devices = range(lax.axis_size(axis))
    route = [(i - distance, i) for i in devices if i - distance in devices]
    return lax.ppermute(block, axis, route)


def group_algebra(queries, key_rows, house, betas):
    length = queries.shape[0]
    scaling = 1.0 / math.sqrt(queries.shape[1])
    row_index = lax.broadcasted_iota(jnp.int32, (length, length), 0)
    column_index = lax.broadcasted_iota(jnp.int32, (length, length), 1)
    strict_below = row_index > column_index
    house_gram = jnp.dot(house, house.T, precision=HIGHEST)
    system = jnp.where(strict_below, house_gram, 0.0) + jnp.diag(1.0 / betas)
    identity = jnp.eye(length, dtype=house.dtype)
    inverse = jax.scipy.linalg.solve_triangular(system, identity, lower=True)
    query_house = jnp.where(
        row_index >= column_index, jnp.dot(queries, house.T, precision=HIGHEST), 0.0
    )
    house_key = jnp.where(strict_below, jnp.dot(house, key_rows.T, precision=HIGHEST), 0.0)
    query_side = jnp.dot(query_house, inverse, precision=HIGHEST)
    key_side = jnp.dot(inverse, house_key, precision=HIGHEST)
    scores = (
        jnp.dot(queries, key_rows.T, precision=HIGHEST)
        - jnp.dot(query_side, house_key, precision=HIGHEST)
    ) * scaling
    query_bar = queries - jnp.dot(query_side, house, precision=HIGHEST)
    key_bar = key_rows - jnp.dot(key_side.T, house, precision=HIGHEST)
    inner = jnp.dot(inverse, house, precision=HIGHEST)
    factor = jnp.eye(house.shape[1], dtype=house.dtype) - jnp.dot(house.T, inner, precision=HIGHEST)
    return (scores, query_bar, key_bar, factor)


def local_map(queries, key_rows, house_raw, beta_logits):
    house = house_raw * lax.rsqrt(jnp.sum(house_raw * house_raw, axis=-1, keepdims=True) + EPSILON)
    betas = 2.0 * jax.nn.sigmoid(beta_logits)
    return jax.vmap(jax.vmap(group_algebra))(queries, key_rows, house, betas)


def doc_starts_local(segment_ids, group_first, first_position):
    length = segment_ids.shape[-1]
    previous = jnp.concatenate([segment_ids[..., :1], segment_ids[..., :-1]], axis=-1)
    offsets = lax.broadcasted_iota(jnp.int32, segment_ids.shape, segment_ids.ndim - 1)
    boundary = (offsets > 0) & (segment_ids != previous)
    marks = jnp.where(boundary, offsets + first_position, -1)
    row_index = lax.broadcasted_iota(jnp.int32, (length, length), 0)
    column_index = lax.broadcasted_iota(jnp.int32, (length, length), 1)
    seen = jnp.where(column_index <= row_index, marks[..., None, :], -1)
    return jnp.maximum(jnp.max(seen, axis=-1), group_first)


def norm_rows(values):
    factor = lax.rsqrt(jnp.mean(values * values, axis=-1, keepdims=True) + EPSILON)
    return (values * factor, factor)


def norm_back(gradient, normed, factor, norm_gain):
    scaled = gradient * norm_gain
    return factor * (scaled - normed * jnp.mean(scaled * normed, axis=-1, keepdims=True))


def split_heads(tensor, head_count):
    seq_count, length, total_width = tensor.shape
    return tensor.reshape(seq_count, length, head_count, total_width // head_count).transpose(
        0, 2, 1, 3
    )


def join_heads(tensor):
    seq_count, head_count, length, head_width = tensor.shape
    return tensor.transpose(0, 2, 1, 3).reshape(seq_count, length, head_count * head_width)


def project(inputs, weight):
    return jnp.einsum("scd,df->scf", inputs, weight, preferred_element_type=jnp.float32)


def project_back(gradient, weight):
    return jnp.einsum("scf,df->scd", gradient, weight, preferred_element_type=jnp.float32)


def weight_grad(inputs, gradient):
    return jnp.einsum("scd,scf->df", inputs, gradient, preferred_element_type=jnp.float32)


def cross_scores(query_rot, key_low, scaling):
    return (
        jnp.einsum("shqd,shkd->shqk", query_rot, key_low, preferred_element_type=jnp.float32)
        * scaling
    )


def weighted_values(weights, values_in):
    return jnp.einsum("shqk,shkd->shqd", weights, values_in, preferred_element_type=jnp.float32)


def ring_of_groups(
    hidden_in,
    segment_ids,
    doc_starts,
    norm1_gain,
    w_query,
    w_key,
    w_value,
    w_house,
    w_beta,
    w_out,
    norm2_gain,
    w_gate,
    w_up,
    w_down,
    output_grad,
):
    gathered = (
        lax.all_gather(norm1_gain, ("fsdp", "ctx"), axis=0, tiled=True),
        lax.all_gather(w_query, ("fsdp", "ctx"), axis=0, tiled=True),
        lax.all_gather(w_key, ("fsdp", "ctx"), axis=0, tiled=True),
        lax.all_gather(w_value, ("fsdp", "ctx"), axis=0, tiled=True),
        lax.all_gather(w_house, ("fsdp", "ctx"), axis=0, tiled=True),
        lax.all_gather(w_beta, ("fsdp", "ctx"), axis=0, tiled=True),
        lax.all_gather(w_out, ("fsdp", "ctx"), axis=0, tiled=True),
        lax.all_gather(norm2_gain, ("fsdp", "ctx"), axis=0, tiled=True),
        lax.all_gather(w_gate, ("fsdp", "ctx"), axis=0, tiled=True),
        lax.all_gather(w_up, ("fsdp", "ctx"), axis=0, tiled=True),
        lax.all_gather(w_down, ("fsdp", "ctx"), axis=0, tiled=True),
    )
    (
        gain_one,
        query_full,
        key_full,
        value_full,
        house_full,
        beta_full,
        out_full,
        gain_two,
        gate_full,
        up_full,
        down_full,
    ) = gathered
    gain_one_f = gain_one.astype(jnp.float32)
    gain_two_f = gain_two.astype(jnp.float32)
    head_count = beta_full.shape[1]
    length = hidden_in.shape[1]
    residual = hidden_in.astype(jnp.float32)
    normed_one, factor_one = norm_rows(residual)
    h_one = (normed_one * gain_one_f).astype(jnp.bfloat16)
    queries = split_heads(project(h_one, query_full), head_count)
    key_rows = split_heads(project(h_one, key_full), head_count)
    values_low = split_heads(project(h_one, value_full).astype(jnp.bfloat16), head_count)
    house_raw = split_heads(project(h_one, house_full), head_count)
    beta_logits = project(h_one, beta_full).transpose(0, 2, 1)
    (scores_local, query_bar, key_bar, factors), local_back = jax.vjp(
        local_map, queries, key_rows, house_raw, beta_logits
    )
    scaling = 1.0 / math.sqrt(queries.shape[-1])
    chain_index = lax.axis_index("ctx")
    hop_total = lax.axis_size("ctx") - 1
    first_position = chain_index * length
    starts = doc_starts_local(segment_ids, doc_starts, first_position)
    offsets = jnp.arange(length, dtype=jnp.int32)
    causal = (offsets[None, :] <= offsets[:, None])[None]
    local_mask = (causal & (offsets[None, None, :] + first_position >= starts[:, :, None]))[:, None]

    def hop_mask(distance):
        key_pos = (chain_index - distance) * length + offsets
        return (key_pos[None, None, :] >= starts[:, :, None])[:, None]

    masked_local = jnp.where(local_mask, scores_local, NEGATIVE)
    local_max = jnp.max(masked_local, axis=-1)
    local_sum = jnp.sum(jnp.exp(masked_local - local_max[..., None]), axis=-1)
    key_send = key_bar.astype(jnp.bfloat16)
    identity = jnp.broadcast_to(jnp.eye(factors.shape[-1], dtype=jnp.float32), factors.shape)
    stack_rot = jnp.zeros((hop_total,) + query_bar.shape, jnp.bfloat16)
    stack_factors = jnp.zeros((hop_total,) + factors.shape, jnp.float32)

    def rotate(hop_step, hop_keys, chain, run_max, run_sum):
        query_rot = jnp.einsum("shqa,shab->shqb", query_bar, chain, precision=HIGHEST).astype(
            jnp.bfloat16
        )
        masked = jnp.where(
            hop_mask(hop_step + 1), cross_scores(query_rot, hop_keys, scaling), NEGATIVE
        )
        new_max = jnp.maximum(run_max, jnp.max(masked, axis=-1))
        new_sum = run_sum * jnp.exp(run_max - new_max) + jnp.sum(
            jnp.exp(masked - new_max[..., None]), axis=-1
        )
        return (query_rot, new_max, new_sum)

    stack_keys = jnp.zeros((hop_total,) + key_send.shape, jnp.bfloat16)
    stack_values = jnp.zeros((hop_total,) + values_low.shape, jnp.bfloat16)

    def forward_hop(hop_step, loop_state):
        (
            send_keys,
            send_values,
            send_factor,
            kept_keys,
            kept_values,
            kept_rot,
            kept_factors,
            run_max,
            run_sum,
        ) = loop_state
        got_keys, got_values = passed_along((send_keys, send_values), "ctx", 1)
        got_factor = passed_along(send_factor.astype(jnp.bfloat16), "ctx", 1).astype(
            send_factor.dtype
        )
        query_rot, run_max, run_sum = rotate(hop_step, got_keys, got_factor, run_max, run_sum)
        kept_keys = lax.dynamic_update_index_in_dim(kept_keys, got_keys, hop_step, 0)
        kept_values = lax.dynamic_update_index_in_dim(kept_values, got_values, hop_step, 0)
        kept_rot = lax.dynamic_update_index_in_dim(kept_rot, query_rot, hop_step, 0)
        kept_factors = lax.dynamic_update_index_in_dim(kept_factors, got_factor, hop_step, 0)
        next_factor = jnp.einsum("shab,shbc->shac", factors, got_factor, precision=HIGHEST)
        return (
            got_keys,
            got_values,
            next_factor,
            kept_keys,
            kept_values,
            kept_rot,
            kept_factors,
            run_max,
            run_sum,
        )

    loop_state = lax.fori_loop(
        0,
        hop_total,
        forward_hop,
        (
            key_send,
            values_low,
            identity,
            stack_keys,
            stack_values,
            stack_rot,
            stack_factors,
            local_max,
            local_sum,
        ),
    )
    stack_keys, stack_values, stack_rot, stack_factors = (
        loop_state[3],
        loop_state[4],
        loop_state[5],
        loop_state[6],
    )
    run_max, run_sum = (loop_state[7], loop_state[8])

    def fetch(hop_step):
        return (
            lax.dynamic_index_in_dim(stack_keys, hop_step, 0, keepdims=False),
            lax.dynamic_index_in_dim(stack_values, hop_step, 0, keepdims=False),
        )

    log_total = run_max + jnp.log(run_sum)

    def recall(hop_step):
        hop_keys, hop_values = fetch(hop_step)
        hop_factor = lax.dynamic_index_in_dim(stack_factors, hop_step, 0, keepdims=False)
        query_rot = lax.dynamic_index_in_dim(stack_rot, hop_step, 0, keepdims=False)
        masked = jnp.where(
            hop_mask(hop_step + 1), cross_scores(query_rot, hop_keys, scaling), NEGATIVE
        )
        hop_probs = jnp.exp(masked - log_total[..., None])
        return (hop_keys, hop_values, hop_factor, query_rot, hop_probs)

    probs_local = jnp.exp(masked_local - log_total[..., None])
    probs_local_low = probs_local.astype(jnp.bfloat16)
    attn_acc = weighted_values(probs_local_low, values_low)
    attn_rest = weighted_values(
        (probs_local - probs_local_low.astype(jnp.float32)).astype(jnp.bfloat16), values_low
    )

    def value_hop(hop_step, running):
        total_low, total_rest = running
        hop_keys, hop_values, hop_factor, query_rot, hop_probs = recall(hop_step)
        hop_low = hop_probs.astype(jnp.bfloat16)
        total_low = total_low + weighted_values(hop_low, hop_values)
        total_rest = total_rest + weighted_values(
            (hop_probs - hop_low.astype(jnp.float32)).astype(jnp.bfloat16), hop_values
        )
        return (total_low, total_rest)

    attn_acc, attn_rest = lax.fori_loop(0, hop_total, value_hop, (attn_acc, attn_rest))
    attn_low = join_heads(attn_acc.astype(jnp.bfloat16))
    branch = lax.psum(project_back(attn_low, out_full), "tp")
    middle = residual + branch
    normed_two, factor_two = norm_rows(middle)
    h_two = (normed_two * gain_two_f).astype(jnp.bfloat16)
    gate_proj = project(h_two, gate_full)
    up_proj = project(h_two, up_full)
    gate_sigmoid = jax.nn.sigmoid(gate_proj)
    silu_gate = gate_proj * gate_sigmoid
    hidden_low = (silu_gate * up_proj).astype(jnp.bfloat16)
    mlp_out = lax.psum(project_back(hidden_low, down_full).astype(jnp.bfloat16), "tp").astype(
        jnp.float32
    )
    block_out = (middle + mlp_out).astype(jnp.bfloat16)
    down_grad = weight_grad(output_grad, hidden_low)
    d_hidden = project(output_grad, down_full)
    d_gate = (d_hidden * up_proj * gate_sigmoid * (1.0 + gate_proj * (1.0 - gate_sigmoid))).astype(
        jnp.bfloat16
    )
    d_up = (d_hidden * silu_gate).astype(jnp.bfloat16)
    gate_grad = weight_grad(h_two, d_gate)
    up_grad = weight_grad(h_two, d_up)
    d_two = lax.psum(project_back(d_gate, gate_full) + project_back(d_up, up_full), "tp")
    gain_two_grad = jnp.sum(d_two * normed_two, axis=(0, 1))
    d_middle = output_grad.astype(jnp.float32) + norm_back(
        d_two, normed_two, factor_two, gain_two_f
    )
    d_branch = d_middle.astype(jnp.bfloat16)
    out_grad = weight_grad(d_branch, attn_low)
    d_attn = split_heads(project(d_branch, out_full).astype(jnp.bfloat16), head_count)
    d_probs_local = jnp.einsum(
        "shqd,shkd->shqk", d_attn, values_low, preferred_element_type=jnp.float32
    )
    row_delta = jnp.sum(d_attn.astype(jnp.float32) * (attn_acc + attn_rest), axis=-1)
    zero_factor = jnp.zeros(factors.shape, jnp.float32)
    zero_bar = jnp.zeros(query_bar.shape, jnp.float32)

    def back_hop(back_step, loop_state):
        carry_keys, carry_values, carry_factor, d_bar, d_factors = loop_state
        hop_step = hop_total - 1 - back_step
        hop_keys, hop_values, hop_factor, query_rot, hop_probs = recall(hop_step)
        d_probs = jnp.einsum(
            "shqd,shkd->shqk", d_attn, hop_values, preferred_element_type=jnp.float32
        )
        d_cross = (hop_probs * (d_probs - row_delta[..., None])).astype(jnp.bfloat16)
        d_rot = (
            jnp.einsum("shqk,shkd->shqd", d_cross, hop_keys, preferred_element_type=jnp.float32)
            * scaling
        )
        d_bar = d_bar + jnp.einsum("shqb,shab->shqa", d_rot, hop_factor, precision=HIGHEST)
        factor_local = jnp.einsum("shqa,shqb->shab", query_bar, d_rot, precision=HIGHEST)
        keys_total = (
            carry_keys
            + jnp.einsum("shqk,shqd->shkd", d_cross, query_rot, preferred_element_type=jnp.float32)
            * scaling
        )
        values_total = carry_values + jnp.einsum(
            "shqk,shqd->shkd",
            hop_probs.astype(jnp.bfloat16),
            d_attn,
            preferred_element_type=jnp.float32,
        )
        factor_total = factor_local + jnp.einsum(
            "shba,shbc->shac", factors, carry_factor, precision=HIGHEST
        )
        d_factors = d_factors + jnp.einsum(
            "shac,shbc->shab", carry_factor, hop_factor, precision=HIGHEST
        )
        carry_keys, carry_values, carry_factor = (
            passed_along(keys_total.astype(jnp.bfloat16), "ctx", -1).astype(keys_total.dtype),
            passed_along(values_total.astype(jnp.bfloat16), "ctx", -1).astype(values_total.dtype),
            passed_along(factor_total.astype(jnp.bfloat16), "ctx", -1).astype(factor_total.dtype),
        )
        return (carry_keys, carry_values, carry_factor, d_bar, d_factors)

    zero_rows = jnp.zeros(key_send.shape, jnp.float32)
    loop_state = lax.fori_loop(
        0, hop_total, back_hop, (zero_rows, zero_rows, zero_factor, zero_bar, zero_factor)
    )
    carry_keys, carry_values, d_bar, d_factors = (
        loop_state[0],
        loop_state[1],
        loop_state[3],
        loop_state[4],
    )
    d_local = probs_local * (d_probs_local - row_delta[..., None])
    values_sum = carry_values + jnp.einsum(
        "shqk,shqd->shkd", probs_local_low, d_attn, preferred_element_type=jnp.float32
    )
    d_queries, d_keys, d_house, d_betas = local_back((d_local, d_bar, carry_keys, d_factors))
    query_low = join_heads(d_queries.astype(jnp.bfloat16))
    key_low = join_heads(d_keys.astype(jnp.bfloat16))
    value_low = join_heads(values_sum.astype(jnp.bfloat16))
    house_low = join_heads(d_house.astype(jnp.bfloat16))
    beta_low = d_betas.transpose(0, 2, 1).astype(jnp.bfloat16)
    query_grad = weight_grad(h_one, query_low)
    key_grad = weight_grad(h_one, key_low)
    value_grad = weight_grad(h_one, value_low)
    house_grad = weight_grad(h_one, house_low)
    beta_grad = weight_grad(h_one, beta_low)
    partial_one = (
        project_back(query_low, query_full)
        + project_back(key_low, key_full)
        + project_back(value_low, value_full)
    )
    partial_one = (
        partial_one + project_back(house_low, house_full) + project_back(beta_low, beta_full)
    )
    d_one = lax.psum(partial_one.astype(jnp.bfloat16), "tp").astype(jnp.float32)
    gain_one_grad = jnp.sum(d_one * normed_one, axis=(0, 1))
    input_grad = (d_middle + norm_back(d_one, normed_one, factor_one, gain_one_f)).astype(
        jnp.bfloat16
    )

    def scattered(partial):
        first = lax.psum_scatter(partial, "fsdp", scatter_dimension=0, tiled=True)
        return lax.psum_scatter(first, "ctx", scatter_dimension=0, tiled=True)

    results = tuple(
        (
            scattered(gain_one_grad.astype(jnp.bfloat16)).astype(jnp.float32),
            scattered(query_grad.astype(jnp.bfloat16)).astype(jnp.float32),
            scattered(key_grad.astype(jnp.bfloat16)).astype(jnp.float32),
            scattered(value_grad.astype(jnp.bfloat16)).astype(jnp.float32),
            scattered(house_grad.astype(jnp.bfloat16)).astype(jnp.float32),
            scattered(beta_grad.astype(jnp.bfloat16)).astype(jnp.float32),
            scattered(out_grad.astype(jnp.bfloat16)).astype(jnp.float32),
            scattered(gain_two_grad.astype(jnp.bfloat16)).astype(jnp.float32),
            scattered(gate_grad.astype(jnp.bfloat16)).astype(jnp.float32),
            scattered(up_grad.astype(jnp.bfloat16)).astype(jnp.float32),
            scattered(down_grad.astype(jnp.bfloat16)).astype(jnp.float32),
        )
    )
    return (block_out, input_grad) + results


def halves(value):
    high = value.astype(jnp.bfloat16)
    return high, (value - high.astype(jnp.float32)).astype(jnp.bfloat16)


AB = (((1,), (0,)), ((), ()))
ABT = (((1,), (1,)), ((), ()))
ATB = (((0,), (0,)), ((), ()))


def mm(a, b, dims=AB):
    return lax.dot_general(a, b, dims, preferred_element_type=jnp.float32)


def mm3(a, b, dims=AB):
    left, right = dims[0][0][0], dims[0][1][0]
    return mm(
        jnp.concatenate([a[0], a[1], a[0]], axis=left),
        jnp.concatenate([b[0], b[0], b[1]], axis=right),
        dims,
    )


def each(function, *lists):
    return [function(*values) for values in zip(*lists)]


def square_index(size):
    row = lax.broadcasted_iota(jnp.int32, (size, size), 0)
    return row, lax.broadcasted_iota(jnp.int32, (size, size), 1)


def unit_lower_inverses(strict):
    size = strict[0].shape[0]
    part, half = size // 4, size // 2
    lane = lax.broadcasted_iota(jnp.int32, (part, size), 1)
    row = lax.broadcasted_iota(jnp.int32, (part, size), 0)
    block = lane // part
    col = lane - block * part
    own = [block == b for b in range(4)]
    zero = jnp.zeros((part, size), jnp.bfloat16)

    def side_by_side(matrix, below):
        packed = jnp.zeros((part, size), jnp.float32)
        for b in range(4 - below):
            packed = jnp.where(own[b], matrix[(b + below) * part : (b + below + 1) * part], packed)
        return packed

    def stacked(pair, order=(0, 1, 2, 3)):
        return tuple(
            jnp.concatenate(
                [zero if b is None else jnp.where(own[b], value, zero) for b in order], axis=0
            )
            for value in pair
        )

    diagonal = [side_by_side(matrix, 0) for matrix in strict]
    inverse = [
        jnp.where(row == col, 1.0, 0.0) - jnp.where((row >> 1) == (col >> 1), matrix, 0.0)
        for matrix in diagonal
    ]
    level = 1
    while (1 << level) < part:
        joined = ((row >> (level + 1)) == (col >> (level + 1))) & ((row >> level) != (col >> level))
        pairs = each(halves, inverse)
        steps = [
            mm3(halves(jnp.where(joined, matrix, 0.0)), stacked(pair))
            for matrix, pair in zip(diagonal, pairs)
        ]
        inverse = [
            value - mm3(pair, stacked(halves(step)))
            for value, pair, step in zip(inverse, pairs, steps)
        ]
        level += 1
    pairs = each(halves, inverse)
    even = own[0] | own[2]
    steps = [
        mm3(halves(jnp.where(even, side_by_side(matrix, 1), 0.0)), stacked(pair))
        for matrix, pair in zip(strict, pairs)
    ]
    corners = [
        -mm3(pair, stacked(halves(step), (None, 0, None, 2))) for pair, step in zip(pairs, steps)
    ]

    def joined_block(value, corner, n):
        lanes = slice(n * half, (n + 1) * half)
        upper = jnp.where(own[2 * n], value, 0.0)[:, lanes]
        return jnp.concatenate([upper, jnp.where(own[2 * n], corner, value)[:, lanes]], axis=0)

    first = [joined_block(value, corner, 0) for value, corner in zip(inverse, corners)]
    last = [joined_block(value, corner, 1) for value, corner in zip(inverse, corners)]
    steps = [mm3(halves(matrix[half:, :half]), halves(value)) for matrix, value in zip(strict, first)]
    lower = [-mm3(halves(value), halves(step)) for value, step in zip(last, steps)]
    blank = jnp.zeros((half, half), jnp.float32)
    return [
        jnp.concatenate(
            [
                jnp.concatenate([top, blank], axis=1),
                jnp.concatenate([left, right], axis=1),
            ],
            axis=0,
        )
        for top, left, right in zip(first, lower, last)
    ]


def unit_rows(raw):
    norm = lax.rsqrt(jnp.sum(raw * raw, axis=1, keepdims=True) + EPSILON)
    return raw * norm, norm


def below(matrix, row, col):
    return jnp.where(row > col, matrix, 0.0)


def key_halves(house_raw, keys, betas):
    row, col = square_index(keys[0].shape[0])
    house = [unit_rows(raw)[0] for raw in house_raw]
    scaled = [halves(beta * value) for beta, value in zip(betas, house)]
    strict = [below(mm3(a, halves(b), ABT), row, col) for a, b in zip(scaled, house)]
    house_key = [halves(below(mm3(a, halves(b), ABT), row, col)) for a, b in zip(scaled, keys)]
    inverses = unit_lower_inverses(strict)
    return inverses, [mm3(halves(a), b) for a, b in zip(inverses, house_key)]


def query_halves(queries, values, house_raw, keys, inverses, key_side, allowed):
    row, col = square_index(keys[0].shape[0])
    scaling = 1.0 / math.sqrt(queries[0].shape[1])
    q = each(halves, queries)
    query_house = [
        halves(jnp.where(row >= col, mm3(a, halves(unit_rows(raw)[0]), ABT), 0.0))
        for a, raw in zip(q, house_raw)
    ]
    scores = [mm3(a, halves(b), ABT) for a, b in zip(q, keys)]
    scores = [score - mm3(a, halves(b)) for score, a, b in zip(scores, query_house, key_side)]
    masked = [jnp.where(allowed, score * scaling, NEGATIVE) for score in scores]
    weights = [jnp.exp(value - jnp.max(value, axis=1, keepdims=True)) for value in masked]
    probs = [value / jnp.sum(value, axis=1, keepdims=True) for value in weights]
    attn = [mm(prob.astype(jnp.bfloat16), value) for prob, value in zip(probs, values)]
    return attn, probs, [mm3(a, halves(b)) for a, b in zip(query_house, inverses)]


def heads_backward(queries, keys, house_raw, values, betas, probs, key_side, query_side, d_attn):
    row, col = square_index(keys[0].shape[0])
    scaling = 1.0 / math.sqrt(queries[0].shape[1])
    house, norm = zip(*[unit_rows(raw) for raw in house_raw])
    d_values = [mm(prob.astype(jnp.bfloat16), d, ATB) for prob, d in zip(probs, d_attn)]
    d_probs = [mm(d, value, ABT) for d, value in zip(d_attn, values)]
    d_scores = [
        halves(prob * (d - jnp.sum(prob * d, axis=1, keepdims=True)) * scaling)
        for prob, d in zip(probs, d_probs)
    ]
    q, k, w = each(halves, queries), each(halves, keys), each(halves, house)
    scaled = [halves(beta * value) for beta, value in zip(betas, house)]
    side = each(halves, query_side)
    d_side = [-mm3(d, halves(value), ABT) for d, value in zip(d_scores, key_side)]
    d_query_house = [halves(jnp.where(row >= col, d, 0.0)) for d in d_side]
    d_strict = [halves(below(-mm3(a, halves(d), ATB), row, col)) for a, d in zip(side, d_side)]
    d_house_key = [halves(below(-mm3(a, d, ATB), row, col)) for a, d in zip(side, d_scores)]
    d_queries = [mm3(d, a) + mm3(e, b) for d, a, e, b in zip(d_scores, k, d_query_house, w)]
    d_keys = [
        mm3(d, a, ATB) + mm3(e, b, ATB) for d, a, e, b in zip(d_scores, q, d_house_key, scaled)
    ]
    d_scaled = [mm3(d, a) + mm3(e, b) for d, a, e, b in zip(d_strict, w, d_house_key, k)]
    d_house = [
        mm3(d, a, ATB) + mm3(e, b, ATB) for d, a, e, b in zip(d_strict, scaled, d_query_house, q)
    ]
    d_betas = [jnp.sum(d * value, axis=1, keepdims=True) for d, value in zip(d_scaled, house)]
    d_house = [d + beta * e for d, beta, e in zip(d_house, betas, d_scaled)]
    d_house_raw = [
        n * (d - value * jnp.sum(d * value, axis=1, keepdims=True))
        for n, d, value in zip(norm, d_house, house)
    ]
    d_logits = [d * beta * (1.0 - 0.5 * beta) for d, beta in zip(d_betas, betas)]
    return d_queries, d_keys, d_house_raw, d_values, d_logits


def head_slices(ref, first, heads, head):
    return [ref[:, first + n * head : first + (n + 1) * head] for n in range(heads)]


def started(pairs, sems):
    copies = [
        pltpu.make_async_copy(source, target, sems.at[n]) for n, (source, target) in enumerate(pairs)
    ]
    for copy in copies:
        copy.start()
    return copies


def token_rows(places, n, k, quarter):
    return pl.ds(pl.multiple_of(places[8 + n] + places[18 + k], 16), quarter)


def placed(gathered, whole, places):
    quarter = gathered.shape[1] // 4
    return [
        (
            gathered.at[n, pl.ds(k * quarter, quarter)],
            whole.at[pl.ds(pl.multiple_of(places[18 + k] + n * quarter, 16), quarter)],
        )
        for n in range(4)
        for k in range(4)
    ]


def split_tokens(whole, parts, places):
    quarter = parts[0].shape[0] // 4
    for n in range(4):
        for k in range(4):
            parts[n][pl.ds(k * quarter, quarter)] = whole[token_rows(places, n, k, quarter)]


def wide_row(row, rows):
    return jnp.broadcast_to(row, (rows, row.shape[1])).astype(jnp.bfloat16)


def own_blocks(places, source, target, sequence=26, at=0):
    quarter = target.shape[-2]
    rows = pl.ds(pl.multiple_of(places[22], 16), quarter)
    return [(source.at[places[sequence + k], rows], target.at[k + at]) for k in range(4)]


def message_kernel(places, hidden_in, ids, gain_one, gain_two, *refs):
    messages, blocks, sems = refs[0:4], refs[4], refs[5]
    quarter, features = blocks.shape[1], blocks.shape[2]
    rows, depth = ids.shape[1], gain_one.shape[0]
    copies = started(own_blocks(places, hidden_in, blocks), sems)
    for k in range(4):
        messages[k][:, features:] = jnp.zeros((quarter, 640), jnp.bfloat16)
        own_ids = ids[pl.ds(places[26 + k], 1)].astype(jnp.float32)
        messages[k][:, features : features + rows] = wide_row(own_ids, quarter)
        at = features + 128
        messages[k][:, at : at + depth] = wide_row(gain_one[...].astype(jnp.float32)[None], quarter)
        at += 256
        messages[k][:, at : at + depth] = wide_row(gain_two[...].astype(jnp.float32)[None], quarter)
    for copy in copies:
        copy.wait()
    for k in range(4):
        messages[k][:, :features] = blocks[k]


def attention_pack_kernel(places, house, key, beta, query, value, out, pack):
    at = 0
    for source in (house, key, beta, query, value, out):
        width = source.shape[1]
        if width < 128:
            pack[:, at : at + 128] = jnp.zeros((pack.shape[0], 128), jnp.bfloat16)
        pack[:, at : at + width] = source[...]
        at += max(width, 128)


def feed_forward_pack_kernel(places, output_grad, gate, up, down, *refs):
    messages, gives, keeps, blocks, sems = refs[0:4], refs[4:6], refs[6:8], refs[8], refs[9]
    copies = started(
        own_blocks(places, output_grad, blocks) + own_blocks(places, output_grad, blocks, 30, 4), sems
    )
    units = gate.shape[1] // 2
    part = units // 2
    for packs, start in ((keeps, places[23]), (gives, places[24])):
        for n in range(6):
            at = pl.ds(pl.multiple_of(start + n % 2 * part, 128), part)
            packs[n // 3][:, n % 3 * part : (n % 3 + 1) * part] = (gate, up, down)[n // 2][:, at]
    for copy in copies:
        copy.wait()
    for k in range(4):
        messages[k][0] = blocks[k]
        messages[k][1] = blocks[4 + k]


def out_message_kernel(places, *refs):
    out_parts, middle, messages = refs[0:4], refs[4], refs[5:9]
    quarter = middle.shape[0] // 4
    out = sum(part[...].astype(jnp.float32) for part in out_parts)
    own, pair = (middle[...] + out[0]).astype(jnp.bfloat16), out[1].astype(jnp.bfloat16)
    for k in range(4):
        messages[k][:quarter] = own[k * quarter : (k + 1) * quarter]
        messages[k][quarter:] = pair[(k ^ 2) * quarter : ((k ^ 2) + 1) * quarter]


def result_kernel(places, d_parts, d_middle, block, gain, gain_two_grad, *messages):
    quarter, features = block.shape[0] // 4, block.shape[1]
    d_one = sum(d_parts[n].astype(jnp.float32) for n in range(4))
    x = block[...].astype(jnp.float32)
    factor = lax.rsqrt(jnp.mean(x * x, axis=1, keepdims=True) + EPSILON)
    normed = x * factor
    scaled = d_one * gain[...]
    mean = jnp.mean(scaled * normed, axis=1, keepdims=True)
    in_grad = (d_middle[...] + factor * (scaled - normed * mean)).astype(jnp.bfloat16)
    gain_one_grad = jnp.sum(d_one * normed, axis=0, keepdims=True)
    row = lax.broadcasted_iota(jnp.int32, (quarter, 128), 0)
    for g, gains in enumerate((gain_one_grad, gain_two_grad[...])):
        packed = jnp.zeros((quarter, 128), jnp.float32)
        for n in range(features // 128):
            packed = jnp.where(row == n, gains[:, n * 128 : (n + 1) * 128], packed)
        at = features + g * 128
        for k in range(4):
            messages[k][:, at : at + 128] = packed.astype(jnp.bfloat16)
    for k in range(4):
        messages[k][:, :features] = in_grad[k * quarter : (k + 1) * quarter]


def spread_kernel(places, pieces, whole):
    quarter, features = whole.shape[1] // 4, whole.shape[2]
    for n in range(4):
        for k in range(4):
            rows = slice(k * quarter, (k + 1) * quarter)
            whole[pl.ds(places[26 + k], 1), n * quarter : (n + 1) * quarter] = pieces[
                n, rows, :features
            ][None]


def gradient_spread_kernel(places, pieces, whole, gains):
    quarter, features = whole.shape[1] // 4, whole.shape[2]
    spread_kernel(places, pieces, whole)
    gains[...] = sum(pieces[n, :quarter, features:].astype(jnp.float32) for n in range(4))


def weights_in_place(pieces, whole, places, first=0, count=None):
    depth = pieces[0].shape[0]
    width = count or pieces[0].shape[1]
    return [
        (
            pieces[n].at[:, pl.ds(first, width)],
            whole.at[pl.ds(pl.multiple_of(places[n], 64), depth), pl.ds(0, width)],
        )
        for n in range(8)
    ]


def keys_kernel(heads, places, *refs):
    weights, xs, gain = refs[0:8], refs[8], refs[9]
    h_all, proj, inverses, key_side = refs[10:14]
    w_all, weight_sems, x_sems, x_all = refs[14:18]
    x_copies = started(placed(xs, x_all, places), x_sems)
    w_copies = started(weights_in_place(weights, w_all, places, 0, w_all.shape[1]), weight_sems)
    for copy in x_copies:
        copy.wait()
    width = (proj.shape[1] - 128) // 2
    head = width // heads
    x = x_all[...].astype(jnp.float32)
    factor = lax.rsqrt(jnp.mean(x * x, axis=1, keepdims=True) + EPSILON)
    h_all[...] = (x * factor * gain[...]).astype(jnp.bfloat16)
    for copy in w_copies:
        copy.wait()
    proj[...] = mm(h_all[...], w_all[...])
    betas = 2.0 * jax.nn.sigmoid(proj[:, 2 * width :])
    results = key_halves(
        head_slices(proj, 0, heads, head),
        head_slices(proj, width, heads, head),
        [betas[:, n : n + 1] for n in range(heads)],
    )
    for n in range(heads):
        inverses[n], key_side[n] = results[0][n], results[1][n]


def queries_kernel(heads, places, *refs):
    weights, (h_all, proj_keys, inverses, key_side, id_row, id_col) = refs[0:8], refs[8:14]
    proj, attn, probs, query_side, parts = refs[14], refs[15], refs[16], refs[17], refs[18:22]
    w_all, total, sems = refs[22:25]
    skip = weights[0].shape[1] - w_all.shape[1]
    for copy in started(weights_in_place(weights, w_all, places, skip, w_all.shape[1]), sems):
        copy.wait()
    width = attn.shape[1]
    head = width // heads
    proj[...] = mm(h_all[...], w_all[:, : 2 * width])
    row, col = square_index(h_all.shape[0])
    results = query_halves(
        head_slices(proj, 0, heads, head),
        [value.astype(jnp.bfloat16) for value in head_slices(proj, width, heads, head)],
        head_slices(proj_keys, 0, heads, head),
        head_slices(proj_keys, width, heads, head),
        [inverses[n] for n in range(heads)],
        [key_side[n] for n in range(heads)],
        (col <= row) & (id_row[...] == id_col[...]),
    )
    for n in range(heads):
        attn[:, n * head : (n + 1) * head] = results[0][n].astype(jnp.bfloat16)
        probs[n], query_side[n] = results[1][n], results[2][n]
    total[...] = mm(attn[...], w_all[:, 2 * width :], ABT).astype(jnp.bfloat16)
    split_tokens(total, parts, places)


def feed_forward_kernel(places, *refs):
    weights, ins, grads = refs[0:16], refs[16:18], refs[18:22]
    two_parts, out_parts, keeps, sends = refs[22:30], refs[30:34], refs[34], refs[35]
    w_all, in_all, grad_all, total, weight_sems, in_sems, grad_sems = refs[36:43]
    rows, units, half = two_parts[0].shape[0], w_all.shape[1] // 3, w_all.shape[0] // 2

    def block(s, n):
        return pl.ds(pl.multiple_of(places[8 + n] * 4 + s * 4 * rows, 64), rows)

    depth, part = weights[0].shape[0], w_all.shape[1] // 2
    w_pairs = []
    for n in range(16):
        row = pl.ds(pl.multiple_of(places[n // 2], 64), depth)
        w_pairs.append((weights[n], w_all.at[row, pl.ds(n % 2 * part, part)]))
    w_copies = started(w_pairs, weight_sems)
    grad_copies = started(
        [
            (grads[n].at[s], grad_all.at[block(s, n)])
            for n in range(4)
            for s in range(2)
        ],
        grad_sems,
    )
    in_copies = started(
        [(ins[s].at[n], in_all.at[pl.ds((s * 4 + n) * rows, rows)]) for s in range(2) for n in range(4)],
        in_sems,
    )
    for copy in w_copies + grad_copies + in_copies:
        copy.wait()
    both = mm(in_all[...], w_all[:, : 2 * units])
    d_hidden = mm(grad_all[...], w_all[:, 2 * units :])
    gate, up = both[:, :units], both[:, units:]
    sigmoid = jax.nn.sigmoid(gate)
    silu = gate * sigmoid
    hidden = (silu * up).astype(jnp.bfloat16)
    d_gate = (d_hidden * up * sigmoid * (1.0 + gate * (1.0 - sigmoid))).astype(jnp.bfloat16)
    d_up = (d_hidden * silu).astype(jnp.bfloat16)
    for target in (keeps, sends):
        at = 2 * half
        for value in (d_gate, d_up, hidden):
            target[:, at : at + units] = value
            at += units
    d_both = keeps[:, 2 * half : 2 * half + 2 * units]
    total[...] = mm(d_both, w_all[:, : 2 * units], ABT).astype(jnp.bfloat16)
    for s in range(2):
        for n in range(4):
            two_parts[s * 4 + n][...] = total[block(s, n)]
    total[...] = mm(hidden, w_all[:, 2 * units :], ABT).astype(jnp.bfloat16)
    for s in range(2):
        for n in range(4):
            out_parts[n][s] = total[block(s, n)]
    for target, place in ((keeps, 12), (sends, 13)):
        lanes = pl.ds(pl.multiple_of(places[place], 128), half)
        target[:, :half] = in_all[:, lanes]
        target[:, half : 2 * half] = grad_all[:, lanes]


def attention_backward_kernel(heads, places, *refs):
    weights, ds = refs[0:8], refs[8]
    proj_keys, proj, probs, key_side, query_side, h_all, attn = refs[9:16]
    keeps, sends, parts = refs[16:19]
    w_first, w_second, d_all, d_attn, total, first_sems, second_sems, d_sems = refs[19:27]
    half, width = d_all.shape[1] // 2, d_attn.shape[1]
    d_keys_all = keeps.at[:, pl.ds(2 * half, 2 * width + 128)]
    d_queries_all = keeps.at[:, pl.ds(2 * half + 2 * width + 128, 2 * width)]
    cut, rest = w_first.shape[1], w_second.shape[1]
    second_copies = started(weights_in_place(weights, w_second, places, cut, rest), second_sems)
    d_copies = started(placed(ds, d_all, places), d_sems)
    first_copies = started(weights_in_place(weights, w_first, places, 0, cut), first_sems)
    for copy in d_copies + second_copies:
        copy.wait()
    head = width // heads
    d_attn[...] = mm(d_all[...], w_second[:, 2 * width :]).astype(jnp.bfloat16)
    betas = 2.0 * jax.nn.sigmoid(proj_keys[:, 2 * width :])
    lane = lax.broadcasted_iota(jnp.int32, betas.shape, 1)
    logits = jnp.zeros(betas.shape, jnp.float32)
    results = heads_backward(
        head_slices(proj, 0, heads, head),
        head_slices(proj_keys, width, heads, head),
        head_slices(proj_keys, 0, heads, head),
        [value.astype(jnp.bfloat16) for value in head_slices(proj, width, heads, head)],
        [betas[:, n : n + 1] for n in range(heads)],
        [probs[n] for n in range(heads)],
        [key_side[n] for n in range(heads)],
        [query_side[n] for n in range(heads)],
        head_slices(d_attn, 0, heads, head),
    )
    for n in range(heads):
        d_queries, d_keys, d_house, d_values, d_logit = [result[n] for result in results]
        low_at, high_at = slice(n * head, (n + 1) * head), slice(width + n * head, width + (n + 1) * head)
        d_keys_all[:, low_at] = d_house.astype(jnp.bfloat16)
        d_keys_all[:, high_at] = d_keys.astype(jnp.bfloat16)
        d_queries_all[:, low_at] = d_queries.astype(jnp.bfloat16)
        d_queries_all[:, high_at] = d_values.astype(jnp.bfloat16)
        logits = jnp.where(lane == n, d_logit, logits)
    d_keys_all[:, 2 * width :] = logits.astype(jnp.bfloat16)
    for copy in first_copies:
        copy.wait()
    keeps[:, keeps.shape[1] - width :] = attn[...]
    sends[:, 2 * half :] = keeps[:, 2 * half :]
    for target, place in ((keeps, 12), (sends, 13)):
        lanes = pl.ds(pl.multiple_of(places[place], 128), half)
        target[:, :half] = h_all[:, lanes]
        target[:, half : 2 * half] = d_all[:, lanes]
    total[...] = (
        mm(d_keys_all[...], w_first[...], ABT) + mm(d_queries_all[...], w_second[:, : 2 * width], ABT)
    ).astype(jnp.bfloat16)
    quarter = parts.shape[1] // 4
    for n in range(4):
        for k in range(4):
            rows = pl.ds(pl.multiple_of(places[18 + k] + n * quarter, 16), quarter)
            parts[n, k * quarter : (k + 1) * quarter] = total[rows]


def weight_grad_kernel(groups, places, mine, came, *refs):
    outs, total = refs[:-1], refs[-1]
    half, at = total.shape[0], 0
    for left, start, width in groups:
        lefts, rights = slice(left * half, (left + 1) * half), slice(start, start + width)
        total[:, at : at + width] = (
            mm(mine[:, lefts], mine[:, rights], ATB) + mm(came[:, lefts], came[:, rights], ATB)
        ).astype(jnp.bfloat16)
        at += width
    depth, at = outs[0].shape[1], 0
    for n in range(0, len(outs), 2):
        width = outs[n].shape[2]
        for k in range(4):
            rows = pl.ds(pl.multiple_of(places[14 + k], 64), depth)
            outs[n + k % 2][k // 2] = total[rows, at : at + width]
        at += width


VMEM_BYTES = 56 * 1024 * 1024


def call(kernel, outs, scratch, places, operands, spaces, micros, out_spaces=None):
    vmem = pl.BlockSpec(memory_space=pltpu.VMEM)
    kinds = {"v": vmem, "a": pl.BlockSpec(memory_space=pl.ANY)}
    return pl.pallas_call(
        kernel,
        out_shape=[jax.ShapeDtypeStruct(shape, kind) for shape, kind in outs],
        in_specs=[pl.BlockSpec(memory_space=pltpu.SMEM)] + [kinds[s] for s in spaces],
        out_specs=[kinds[s] for s in out_spaces or "v" * len(outs)],
        scratch_shapes=scratch,
        compiler_params=pltpu.CompilerParams(vmem_limit_bytes=VMEM_BYTES),
        cost_estimate=pl.CostEstimate(
            flops=int(micros * 1e6), transcendentals=0, bytes_accessed=int(micros * 1e4)
        ),
    )(places, *operands)


def swap(block, axis, distance):
    size = lax.axis_size(axis)
    return lax.ppermute(block, axis, [(i, i ^ distance) for i in range(size)])


def gathered_tp(block):
    return lax.all_gather(block, "tp", axis=0)


def all_tp(block):
    return [block] + [swap(block, "tp", n) for n in (1, 2, 3)]


def to_owners(messages):
    return [messages[0]] + [swap(messages[n], "ctx", n) for n in (1, 2, 3)]


def sum_tp(parts):
    return [parts[0]] + [swap(parts[n], "tp", n) for n in (1, 2, 3)]


def add_up(blocks):
    total = blocks[0].astype(jnp.float32)
    for block in blocks[1:]:
        total = total + block.astype(jnp.float32)
    return total


def other_core(block):
    return swap(block, "fsdp", 1)


def whole_sequences(
    hidden_in,
    segment_ids,
    doc_starts,
    norm1_gain,
    w_query,
    w_key,
    w_value,
    w_house,
    w_beta,
    w_out,
    norm2_gain,
    w_gate,
    w_up,
    w_down,
    output_grad,
):
    low, wide = jnp.bfloat16, jnp.float32
    core, chain, column = lax.axis_index("fsdp"), lax.axis_index("ctx"), lax.axis_index("tp")
    rows, features = hidden_in.shape[1], hidden_in.shape[2]
    depth, width, heads = w_query.shape[0], w_query.shape[1], w_beta.shape[1]
    length, half, quarter = 4 * rows, features // 2, rows // 4
    units, used = w_gate.shape[1] // 2, 4 * width + 128
    near = jnp.arange(4, dtype=jnp.int32)
    upper = (chain // 2).astype(jnp.int32)
    places = jnp.concatenate(
        [
            (core * 4 + (chain ^ near)) * depth,
            ((1 - core) * 4 + (chain ^ near)) * depth,
            (column ^ near) * quarter,
            jnp.stack([core, 1 - core]) * half,
            (chain ^ near) * depth,
            (chain ^ near) * rows,
            jnp.stack([column * quarter, upper * units, (1 - upper) * units, upper]),
            chain ^ near,
            chain ^ near ^ 2,
        ]
    ).astype(jnp.int32)
    step = lax.optimization_barrier
    block = pltpu.VMEM((4, quarter, features), low)
    token_messages = call(
        message_kernel,
        [((quarter, features + 640), low)] * 4,
        [block, pltpu.SemaphoreType.DMA((4,))],
        places,
        [hidden_in, segment_ids, norm1_gain, norm2_gain],
        "avvv",
        2,
    )
    (pack,) = call(
        attention_pack_kernel,
        [((depth, used + width), low)],
        [],
        places,
        [w_house, w_key, w_beta, w_query, w_value, w_out],
        "v" * 6,
        2,
    )
    x_messages, pack, output_grad = step((to_owners(token_messages), pack, output_grad))
    packed = call(
        feed_forward_pack_kernel,
        [((2, quarter, features), low)] * 4
        + [((depth, 3 * units // 2), low)] * 4,
        [pltpu.VMEM((8, quarter, features), low), pltpu.SemaphoreType.DMA((8,))],
        places,
        [output_grad, w_gate, w_up, w_down],
        "avvv",
        3,
    )
    grad_messages, gives, ffn_keeps = packed[:4], packed[4:6], packed[6:8]

    pack_two, pack_one = swap(pack, "ctx", 2), swap(pack, "ctx", 1)
    x_block = jnp.concatenate([message[:, :features] for message in x_messages])
    x_pieces = gathered_tp(x_block)
    info = jnp.stack([message[0, features:] for message in x_messages])
    chosen = near[:, None] == (near[None, :] ^ chain)
    info = jnp.sum(jnp.where(chosen[:, :, None], info[None].astype(wide), 0.0), axis=1)
    ids = info[:, :rows].reshape(length)
    gains = jnp.concatenate(
        [info[:, 128 : 128 + depth], info[:, 384 : 384 + depth]], axis=1
    ).astype(low)
    id_row, id_col = ids[None, :], ids[:, None]
    id_row, id_col, pack_two, pack_one, x_pieces, pack, gains, grad_messages, gives = step(
        (id_row, id_col, pack_two, pack_one, x_pieces, pack, gains, grad_messages, gives)
    )

    pack_three = swap(pack_two, "ctx", 1)
    gains_other = other_core(gains)
    gains = jnp.where(core == 0, jnp.stack([gains, gains_other]), jnp.stack([gains_other, gains]))
    gain_one = gains[:, :, :depth].reshape(1, features).astype(wide)
    gain_two = gains[:, :, depth:].reshape(1, features).astype(wide)
    grad_messages = to_owners(grad_messages)
    pack_three, pack_two, pack_one, pack, gain_one, gives, grad_messages, ffn_keeps = step(
        (pack_three, pack_two, pack_one, pack, gain_one, gives, grad_messages, ffn_keeps)
    )

    attn_weights = [pack, pack_one, pack_two, pack_three]
    attn_weights = attn_weights + [other_core(piece) for piece in attn_weights]
    give_two = [swap(gives[0], "ctx", 2)]
    keep_one = [swap(ffn_keeps[0], "ctx", 1)]
    grads = jnp.stack(
        [
            jnp.concatenate([message[0] for message in grad_messages]),
            jnp.concatenate([grad_messages[n ^ 2][1] for n in range(4)]),
        ]
    )
    own_grad = grads[0]
    grad_pieces = all_tp(grads)
    square = ((heads, length, length), wide)
    h_all, proj_keys, inverses, key_side = call(
        functools.partial(keys_kernel, heads),
        [((length, features), low), ((length, 2 * width + 128), wide), square, square],
        [
            pltpu.VMEM((features, 2 * width + 128), low),
            pltpu.SemaphoreType.DMA((8,)),
            pltpu.SemaphoreType.DMA((16,)),
            pltpu.VMEM((length, features), low),
        ],
        places,
        [*attn_weights, x_pieces, gain_one],
        "a" * 9 + "v",
        20,
    )
    outs = call(
        functools.partial(queries_kernel, heads),
        [((length, 2 * width), wide), ((length, width), low), square, square]
        + [((rows, features), low)] * 4,
        [
            pltpu.VMEM((features, 3 * width), low),
            pltpu.VMEM((length, features), low),
            pltpu.SemaphoreType.DMA((8,)),
        ],
        places,
        [*attn_weights, h_all, proj_keys, inverses, key_side, id_row, id_col],
        "a" * 8 + "v" * 6,
        9,
    )
    proj, attn, probs, query_side = outs[:4]
    give_two, branch_parts, keep_one, grad_pieces, give_last, ffn_keeps = step(
        (give_two, outs[4:], keep_one, grad_pieces, gives[1], ffn_keeps)
    )
    give_two = give_two + [swap(give_last, "ctx", 2)]
    give_three = [swap(give_two[0], "ctx", 1)]
    middle = x_block.astype(wide) + add_up(sum_tp(branch_parts))
    normed_two, factor_two = norm_rows(middle)
    h_two = (normed_two * gain_two).astype(low)
    give_two, give_three, ffn_keeps, h_two = step((give_two, give_three, ffn_keeps, h_two))

    h_pair = swap(h_two, "ctx", 2)
    give_three = give_three + [swap(give_two[1], "ctx", 1)]
    keep_one = keep_one + [swap(ffn_keeps[1], "ctx", 1)]
    h_own = gathered_tp(h_two)
    h_pair, give_three, h_own, keep_one, give_two = step(
        (h_pair, give_three, h_own, keep_one, give_two)
    )
    ffn_weights = [*ffn_keeps, *keep_one, *give_two, *give_three]
    ffn_weights = ffn_weights + [other_core(piece) for piece in ffn_weights]
    h_pair = gathered_tp(h_pair)

    tokens = 2 * length
    pair = ((2, rows, features), low)
    outs = call(
        feed_forward_kernel,
        [((rows, features), low)] * 8 + [pair] * 4 + [((tokens, features + 3 * units), low)] * 2,
        [
            pltpu.VMEM((features, 3 * units), low),
            pltpu.VMEM((tokens, features), low),
            pltpu.VMEM((tokens, features), low),
            pltpu.VMEM((tokens, features), low),
            pltpu.SemaphoreType.DMA((16,)),
            pltpu.SemaphoreType.DMA((8,)),
            pltpu.SemaphoreType.DMA((8,)),
        ],
        places,
        [*ffn_weights, h_own, h_pair, *grad_pieces],
        "a" * 22,
        12,
    )
    own_parts, pair_parts, out_parts, keeps, sends = outs[:4], outs[4:8], outs[8:12], outs[12], outs[13]

    def grads_of(mine, came, groups, pieces=1):
        total = sum(group[2] for group in groups)
        return call(
            functools.partial(weight_grad_kernel, groups),
            [((2, depth, total // pieces), low)] * (2 * pieces),
            [pltpu.VMEM((half, total), low)],
            places,
            [mine, came],
            "vv",
            total / 400.0,
        )

    pair_sum = add_up(sum_tp(pair_parts)).astype(low)
    came, pair_sum, own_parts = step((other_core(sends), pair_sum, own_parts))

    two_other = swap(pair_sum, "ctx", 2)
    own_sum = add_up(sum_tp(own_parts))
    ffn_grads = grads_of(
        keeps, came, ((0, features, 2 * units), (1, features + 2 * units, units)), 2
    )
    d_two = own_sum + two_other.astype(wide)
    gain_two_grad = jnp.sum(d_two * normed_two, axis=0, keepdims=True)
    d_middle = own_grad.astype(wide) + norm_back(d_two, normed_two, factor_two, gain_two)
    d_low, ffn_grads = step((d_middle.astype(low), tuple(ffn_grads)))

    ffn_came = [swap(ffn_grads[1], "ctx", 1)]
    d_pieces = gathered_tp(d_low)
    ffn_sums = [add_up([ffn_grads[0], ffn_came[0]])]
    ffn_leave = ffn_sums[0][1].astype(low)
    d_pieces, out_parts, ffn_leave, ffn_far = step((d_pieces, out_parts, ffn_leave, ffn_grads[3]))

    ffn_other = [swap(ffn_leave, "ctx", 2)]
    ffn_came = ffn_came + [swap(ffn_far, "ctx", 1)]
    out_received = sum_tp(out_parts)
    back = call(
        functools.partial(attention_backward_kernel, heads),
        [((length, features + used + width), low)] * 2 + [((4, rows, features), low)],
        [
            pltpu.VMEM((features, 2 * width + 128), low),
            pltpu.VMEM((features, 3 * width), low),
            pltpu.VMEM((length, features), low),
            pltpu.VMEM((length, width), low),
            pltpu.VMEM((length, features), low),
            pltpu.SemaphoreType.DMA((8,)),
            pltpu.SemaphoreType.DMA((8,)),
            pltpu.SemaphoreType.DMA((16,)),
        ],
        places,
        [*attn_weights, d_pieces, proj_keys, proj, probs, key_side, query_side, h_all, attn],
        "a" * 9 + "v" * 7,
        14,
    )
    ffn_sums = ffn_sums + [add_up([ffn_grads[2], ffn_came[1]])]
    ffn_leave, ffn_other, out_received, (keeps, sends, d_parts) = step(
        (ffn_sums[1][1].astype(low), ffn_other, out_received, tuple(back))
    )

    out_messages = call(
        out_message_kernel,
        [((2 * quarter, features), low)] * 4,
        [],
        places,
        [*out_received, middle],
        "v" * 5,
        2,
    )
    came, keeps, d_parts, out_messages, ffn_leave = step(
        (other_core(sends), keeps, d_parts, tuple(out_messages), ffn_leave)
    )

    ffn_other = ffn_other + [swap(ffn_leave, "ctx", 2)]
    query_start = features + 2 * width + 128
    near_two, far_two = grads_of(
        keeps, came, ((0, query_start, 2 * width), (1, query_start + 2 * width, width))
    )
    out_messages, near_two, far_two, keeps = step((out_messages, near_two, far_two, keeps))
    two_came = swap(far_two, "ctx", 1)
    out_messages = to_owners(out_messages)
    near_one, far_one = grads_of(keeps, came, ((0, features, 2 * width + 128),))
    d_parts, near_one, far_one = step((d_parts, near_one, far_one))
    d_received = lax.all_to_all(d_parts, "tp", 0, 0)
    messages = call(
        result_kernel,
        [((quarter, features + 256), low)] * 4,
        [],
        places,
        [d_received, d_middle, x_block, gain_one, gain_two_grad],
        "v" * 5,
        3,
    )
    two_sum = add_up([near_two, two_came])
    two_leave, near_one, far_one, messages, out_messages, ffn_other = step(
        (two_sum[1].astype(low), near_one, far_one, tuple(messages), out_messages, ffn_other)
    )

    one_came = swap(far_one, "ctx", 1)
    query_other = swap(two_leave, "ctx", 2)
    messages = step(to_owners(messages))
    owned = jnp.concatenate([message[:, :features] for message in messages])
    gain_sum = add_up([message[:, features:] for message in messages]).astype(low)
    owned = jnp.concatenate([owned, jnp.pad(gain_sum, ((0, 3 * quarter), (0, 0)))], axis=1)
    input_grad, gain_total = call(
        gradient_spread_kernel,
        [((4, rows, features), low), ((quarter, 256), wide)],
        [],
        places,
        [gathered_tp(owned)],
        "v",
        3,
    )
    one_sum = add_up([near_one, one_came])
    out_block = jnp.concatenate(
        [add_up([out_messages[n][:quarter], out_messages[n ^ 2][quarter:]]) for n in range(4)]
    ).astype(low)
    one_leave, input_grad, gain_total, query_other, out_block = step(
        (one_sum[1].astype(low), input_grad, gain_total, query_other, out_block)
    )

    key_other = swap(one_leave, "ctx", 2)
    block_out = call(
        spread_kernel, [((4, rows, features), low)], [], places, [gathered_tp(out_block)], "v", 2
    )[0]
    gain_total = gain_total + other_core(gain_total)
    gain_total = jnp.concatenate(
        [gain_total[: features // 128, :128], gain_total[: features // 128, 128:]]
    ).reshape(2, features)
    gain_total = lax.dynamic_slice_in_dim(gain_total, (core * 4 + chain) * depth, depth, axis=1)
    query_grads = two_sum[0] + query_other.astype(wide)
    key_grads = one_sum[0] + key_other.astype(wide)

    ffn_kept = jnp.concatenate([total[0] for total in ffn_sums], axis=1)
    ffn_other = jnp.concatenate(ffn_other, axis=1).astype(wide)

    def ffn_result(n):
        kept = ffn_kept[:, n * units : (n + 1) * units]
        came = ffn_other[:, n * units : (n + 1) * units]
        return jnp.concatenate(
            [jnp.where(upper == 1, came, kept), jnp.where(upper == 1, kept, came)], axis=1
        )

    return (
        block_out,
        input_grad,
        gain_total[0],
        query_grads[:, :width],
        key_grads[:, width : 2 * width],
        query_grads[:, width : 2 * width],
        key_grads[:, :width],
        key_grads[:, 2 * width : 2 * width + heads],
        query_grads[:, 2 * width :],
        gain_total[1],
        ffn_result(0),
        ffn_result(1),
        ffn_result(2),
    )


def shards(*args):
    sizes = [lax.axis_size(axis) for axis in ("fsdp", "ctx", "tp")]
    if sizes == [2, 4, 4] and args[0].shape[:2] == (4, 64):
        return whole_sequences(*args)
    return ring_of_groups(*args)


def solution(mesh):
    in_specs = (
        P("fsdp", "ctx", None),
        P("fsdp", "ctx"),
        P("fsdp", "ctx"),
        P(("fsdp", "ctx")),
        P(("fsdp", "ctx"), "tp"),
        P(("fsdp", "ctx"), "tp"),
        P(("fsdp", "ctx"), "tp"),
        P(("fsdp", "ctx"), "tp"),
        P(("fsdp", "ctx"), "tp"),
        P(("fsdp", "ctx"), "tp"),
        P(("fsdp", "ctx")),
        P(("fsdp", "ctx"), "tp"),
        P(("fsdp", "ctx"), "tp"),
        P(("fsdp", "ctx"), "tp"),
        P("fsdp", "ctx", None),
    )
    out_specs = (
        P("fsdp", "ctx", None),
        P("fsdp", "ctx", None),
        P(("fsdp", "ctx")),
        P(("fsdp", "ctx"), "tp"),
        P(("fsdp", "ctx"), "tp"),
        P(("fsdp", "ctx"), "tp"),
        P(("fsdp", "ctx"), "tp"),
        P(("fsdp", "ctx"), "tp"),
        P(("fsdp", "ctx"), "tp"),
        P(("fsdp", "ctx")),
        P(("fsdp", "ctx"), "tp"),
        P(("fsdp", "ctx"), "tp"),
        P(("fsdp", "ctx"), "tp"),
    )
    return jax.shard_map(shards, mesh=mesh, in_specs=in_specs, out_specs=out_specs, check_vma=False)
```

```python
import functools
import math

import jax
import jax.numpy as jnp
from jax import lax
from jax.experimental import pallas as pl
from jax.experimental.pallas import tpu as pltpu
from jax.sharding import PartitionSpec as P

EPSILON = 1e-06
HIGHEST = lax.Precision.HIGHEST
NEGATIVE = -1e30


def passed_along(block, axis, distance):
    devices = range(lax.axis_size(axis))
    route = [(i - distance, i) for i in devices if i - distance in devices]
    return lax.ppermute(block, axis, route)


def group_algebra(queries, key_rows, house, betas):
    length = queries.shape[0]
    scaling = 1.0 / math.sqrt(queries.shape[1])
    row_index = lax.broadcasted_iota(jnp.int32, (length, length), 0)
    column_index = lax.broadcasted_iota(jnp.int32, (length, length), 1)
    strict_below = row_index > column_index
    house_gram = jnp.dot(house, house.T, precision=HIGHEST)
    system = jnp.where(strict_below, house_gram, 0.0) + jnp.diag(1.0 / betas)
    identity = jnp.eye(length, dtype=house.dtype)
    inverse = jax.scipy.linalg.solve_triangular(system, identity, lower=True)
    query_house = jnp.where(
        row_index >= column_index, jnp.dot(queries, house.T, precision=HIGHEST), 0.0
    )
    house_key = jnp.where(strict_below, jnp.dot(house, key_rows.T, precision=HIGHEST), 0.0)
    query_side = jnp.dot(query_house, inverse, precision=HIGHEST)
    key_side = jnp.dot(inverse, house_key, precision=HIGHEST)
    scores = (
        jnp.dot(queries, key_rows.T, precision=HIGHEST)
        - jnp.dot(query_side, house_key, precision=HIGHEST)
    ) * scaling
    query_bar = queries - jnp.dot(query_side, house, precision=HIGHEST)
    key_bar = key_rows - jnp.dot(key_side.T, house, precision=HIGHEST)
    inner = jnp.dot(inverse, house, precision=HIGHEST)
    factor = jnp.eye(house.shape[1], dtype=house.dtype) - jnp.dot(house.T, inner, precision=HIGHEST)
    return (scores, query_bar, key_bar, factor)


def local_map(queries, key_rows, house_raw, beta_logits):
    house = house_raw * lax.rsqrt(jnp.sum(house_raw * house_raw, axis=-1, keepdims=True) + EPSILON)
    betas = 2.0 * jax.nn.sigmoid(beta_logits)
    return jax.vmap(jax.vmap(group_algebra))(queries, key_rows, house, betas)


def doc_starts_local(segment_ids, group_first, first_position):
    length = segment_ids.shape[-1]
    previous = jnp.concatenate([segment_ids[..., :1], segment_ids[..., :-1]], axis=-1)
    offsets = lax.broadcasted_iota(jnp.int32, segment_ids.shape, segment_ids.ndim - 1)
    boundary = (offsets > 0) & (segment_ids != previous)
    marks = jnp.where(boundary, offsets + first_position, -1)
    row_index = lax.broadcasted_iota(jnp.int32, (length, length), 0)
    column_index = lax.broadcasted_iota(jnp.int32, (length, length), 1)
    seen = jnp.where(column_index <= row_index, marks[..., None, :], -1)
    return jnp.maximum(jnp.max(seen, axis=-1), group_first)


def norm_rows(values):
    factor = lax.rsqrt(jnp.mean(values * values, axis=-1, keepdims=True) + EPSILON)
    return (values * factor, factor)


def norm_back(gradient, normed, factor, norm_gain):
    scaled = gradient * norm_gain
    return factor * (scaled - normed * jnp.mean(scaled * normed, axis=-1, keepdims=True))


def split_heads(tensor, head_count):
    seq_count, length, total_width = tensor.shape
    return tensor.reshape(seq_count, length, head_count, total_width // head_count).transpose(
        0, 2, 1, 3
    )


def join_heads(tensor):
    seq_count, head_count, length, head_width = tensor.shape
    return tensor.transpose(0, 2, 1, 3).reshape(seq_count, length, head_count * head_width)


def project(inputs, weight):
    return jnp.einsum("scd,df->scf", inputs, weight, preferred_element_type=jnp.float32)


def project_back(gradient, weight):
    return jnp.einsum("scf,df->scd", gradient, weight, preferred_element_type=jnp.float32)


def weight_grad(inputs, gradient):
    return jnp.einsum("scd,scf->df", inputs, gradient, preferred_element_type=jnp.float32)


def cross_scores(query_rot, key_low, scaling):
    return (
        jnp.einsum("shqd,shkd->shqk", query_rot, key_low, preferred_element_type=jnp.float32)
        * scaling
    )


def weighted_values(weights, values_in):
    return jnp.einsum("shqk,shkd->shqd", weights, values_in, preferred_element_type=jnp.float32)


def ring_of_groups(
    hidden_in,
    segment_ids,
    doc_starts,
    norm1_gain,
    w_query,
    w_key,
    w_value,
    w_house,
    w_beta,
    w_out,
    norm2_gain,
    w_gate,
    w_up,
    w_down,
    output_grad,
):
    gathered = (
        lax.all_gather(norm1_gain, ("fsdp", "ctx"), axis=0, tiled=True),
        lax.all_gather(w_query, ("fsdp", "ctx"), axis=0, tiled=True),
        lax.all_gather(w_key, ("fsdp", "ctx"), axis=0, tiled=True),
        lax.all_gather(w_value, ("fsdp", "ctx"), axis=0, tiled=True),
        lax.all_gather(w_house, ("fsdp", "ctx"), axis=0, tiled=True),
        lax.all_gather(w_beta, ("fsdp", "ctx"), axis=0, tiled=True),
        lax.all_gather(w_out, ("fsdp", "ctx"), axis=0, tiled=True),
        lax.all_gather(norm2_gain, ("fsdp", "ctx"), axis=0, tiled=True),
        lax.all_gather(w_gate, ("fsdp", "ctx"), axis=0, tiled=True),
        lax.all_gather(w_up, ("fsdp", "ctx"), axis=0, tiled=True),
        lax.all_gather(w_down, ("fsdp", "ctx"), axis=0, tiled=True),
    )
    (
        gain_one,
        query_full,
        key_full,
        value_full,
        house_full,
        beta_full,
        out_full,
        gain_two,
        gate_full,
        up_full,
        down_full,
    ) = gathered
    gain_one_f = gain_one.astype(jnp.float32)
    gain_two_f = gain_two.astype(jnp.float32)
    head_count = beta_full.shape[1]
    length = hidden_in.shape[1]
    residual = hidden_in.astype(jnp.float32)
    normed_one, factor_one = norm_rows(residual)
    h_one = (normed_one * gain_one_f).astype(jnp.bfloat16)
    queries = split_heads(project(h_one, query_full), head_count)
    key_rows = split_heads(project(h_one, key_full), head_count)
    values_low = split_heads(project(h_one, value_full).astype(jnp.bfloat16), head_count)
    house_raw = split_heads(project(h_one, house_full), head_count)
    beta_logits = project(h_one, beta_full).transpose(0, 2, 1)
    (scores_local, query_bar, key_bar, factors), local_back = jax.vjp(
        local_map, queries, key_rows, house_raw, beta_logits
    )
    scaling = 1.0 / math.sqrt(queries.shape[-1])
    chain_index = lax.axis_index("ctx")
    hop_total = lax.axis_size("ctx") - 1
    first_position = chain_index * length
    starts = doc_starts_local(segment_ids, doc_starts, first_position)
    offsets = jnp.arange(length, dtype=jnp.int32)
    causal = (offsets[None, :] <= offsets[:, None])[None]
    local_mask = (causal & (offsets[None, None, :] + first_position >= starts[:, :, None]))[:, None]

    def hop_mask(distance):
        key_pos = (chain_index - distance) * length + offsets
        return (key_pos[None, None, :] >= starts[:, :, None])[:, None]

    masked_local = jnp.where(local_mask, scores_local, NEGATIVE)
    local_max = jnp.max(masked_local, axis=-1)
    local_sum = jnp.sum(jnp.exp(masked_local - local_max[..., None]), axis=-1)
    key_send = key_bar.astype(jnp.bfloat16)
    identity = jnp.broadcast_to(jnp.eye(factors.shape[-1], dtype=jnp.float32), factors.shape)
    stack_rot = jnp.zeros((hop_total,) + query_bar.shape, jnp.bfloat16)
    stack_factors = jnp.zeros((hop_total,) + factors.shape, jnp.float32)

    def rotate(hop_step, hop_keys, chain, run_max, run_sum):
        query_rot = jnp.einsum("shqa,shab->shqb", query_bar, chain, precision=HIGHEST).astype(
            jnp.bfloat16
        )
        masked = jnp.where(
            hop_mask(hop_step + 1), cross_scores(query_rot, hop_keys, scaling), NEGATIVE
        )
        new_max = jnp.maximum(run_max, jnp.max(masked, axis=-1))
        new_sum = run_sum * jnp.exp(run_max - new_max) + jnp.sum(
            jnp.exp(masked - new_max[..., None]), axis=-1
        )
        return (query_rot, new_max, new_sum)

    stack_keys = jnp.zeros((hop_total,) + key_send.shape, jnp.bfloat16)
    stack_values = jnp.zeros((hop_total,) + values_low.shape, jnp.bfloat16)

    def forward_hop(hop_step, loop_state):
        (
            send_keys,
            send_values,
            send_factor,
            kept_keys,
            kept_values,
            kept_rot,
            kept_factors,
            run_max,
            run_sum,
        ) = loop_state
        got_keys, got_values = passed_along((send_keys, send_values), "ctx", 1)
        got_factor = passed_along(send_factor.astype(jnp.bfloat16), "ctx", 1).astype(
            send_factor.dtype
        )
        query_rot, run_max, run_sum = rotate(hop_step, got_keys, got_factor, run_max, run_sum)
        kept_keys = lax.dynamic_update_index_in_dim(kept_keys, got_keys, hop_step, 0)
        kept_values = lax.dynamic_update_index_in_dim(kept_values, got_values, hop_step, 0)
        kept_rot = lax.dynamic_update_index_in_dim(kept_rot, query_rot, hop_step, 0)
        kept_factors = lax.dynamic_update_index_in_dim(kept_factors, got_factor, hop_step, 0)
        next_factor = jnp.einsum("shab,shbc->shac", factors, got_factor, precision=HIGHEST)
        return (
            got_keys,
            got_values,
            next_factor,
            kept_keys,
            kept_values,
            kept_rot,
            kept_factors,
            run_max,
            run_sum,
        )

    loop_state = lax.fori_loop(
        0,
        hop_total,
        forward_hop,
        (
            key_send,
            values_low,
            identity,
            stack_keys,
            stack_values,
            stack_rot,
            stack_factors,
            local_max,
            local_sum,
        ),
    )
    stack_keys, stack_values, stack_rot, stack_factors = (
        loop_state[3],
        loop_state[4],
        loop_state[5],
        loop_state[6],
    )
    run_max, run_sum = (loop_state[7], loop_state[8])

    def fetch(hop_step):
        return (
            lax.dynamic_index_in_dim(stack_keys, hop_step, 0, keepdims=False),
            lax.dynamic_index_in_dim(stack_values, hop_step, 0, keepdims=False),
        )

    log_total = run_max + jnp.log(run_sum)

    def recall(hop_step):
        hop_keys, hop_values = fetch(hop_step)
        hop_factor = lax.dynamic_index_in_dim(stack_factors, hop_step, 0, keepdims=False)
        query_rot = lax.dynamic_index_in_dim(stack_rot, hop_step, 0, keepdims=False)
        masked = jnp.where(
            hop_mask(hop_step + 1), cross_scores(query_rot, hop_keys, scaling), NEGATIVE
        )
        hop_probs = jnp.exp(masked - log_total[..., None])
        return (hop_keys, hop_values, hop_factor, query_rot, hop_probs)

    probs_local = jnp.exp(masked_local - log_total[..., None])
    probs_local_low = probs_local.astype(jnp.bfloat16)
    attn_acc = weighted_values(probs_local_low, values_low)
    attn_rest = weighted_values(
        (probs_local - probs_local_low.astype(jnp.float32)).astype(jnp.bfloat16), values_low
    )

    def value_hop(hop_step, running):
        total_low, total_rest = running
        hop_keys, hop_values, hop_factor, query_rot, hop_probs = recall(hop_step)
        hop_low = hop_probs.astype(jnp.bfloat16)
        total_low = total_low + weighted_values(hop_low, hop_values)
        total_rest = total_rest + weighted_values(
            (hop_probs - hop_low.astype(jnp.float32)).astype(jnp.bfloat16), hop_values
        )
        return (total_low, total_rest)

    attn_acc, attn_rest = lax.fori_loop(0, hop_total, value_hop, (attn_acc, attn_rest))
    attn_low = join_heads(attn_acc.astype(jnp.bfloat16))
    branch = lax.psum(project_back(attn_low, out_full), "tp")
    middle = residual + branch
    normed_two, factor_two = norm_rows(middle)
    h_two = (normed_two * gain_two_f).astype(jnp.bfloat16)
    gate_proj = project(h_two, gate_full)
    up_proj = project(h_two, up_full)
    gate_sigmoid = jax.nn.sigmoid(gate_proj)
    silu_gate = gate_proj * gate_sigmoid
    hidden_low = (silu_gate * up_proj).astype(jnp.bfloat16)
    mlp_out = lax.psum(project_back(hidden_low, down_full).astype(jnp.bfloat16), "tp").astype(
        jnp.float32
    )
    block_out = (middle + mlp_out).astype(jnp.bfloat16)
    down_grad = weight_grad(output_grad, hidden_low)
    d_hidden = project(output_grad, down_full)
    d_gate = (d_hidden * up_proj * gate_sigmoid * (1.0 + gate_proj * (1.0 - gate_sigmoid))).astype(
        jnp.bfloat16
    )
    d_up = (d_hidden * silu_gate).astype(jnp.bfloat16)
    gate_grad = weight_grad(h_two, d_gate)
    up_grad = weight_grad(h_two, d_up)
    d_two = lax.psum(project_back(d_gate, gate_full) + project_back(d_up, up_full), "tp")
    gain_two_grad = jnp.sum(d_two * normed_two, axis=(0, 1))
    d_middle = output_grad.astype(jnp.float32) + norm_back(
        d_two, normed_two, factor_two, gain_two_f
    )
    d_branch = d_middle.astype(jnp.bfloat16)
    out_grad = weight_grad(d_branch, attn_low)
    d_attn = split_heads(project(d_branch, out_full).astype(jnp.bfloat16), head_count)
    d_probs_local = jnp.einsum(
        "shqd,shkd->shqk", d_attn, values_low, preferred_element_type=jnp.float32
    )
    row_delta = jnp.sum(d_attn.astype(jnp.float32) * (attn_acc + attn_rest), axis=-1)
    zero_factor = jnp.zeros(factors.shape, jnp.float32)
    zero_bar = jnp.zeros(query_bar.shape, jnp.float32)

    def back_hop(back_step, loop_state):
        carry_keys, carry_values, carry_factor, d_bar, d_factors = loop_state
        hop_step = hop_total - 1 - back_step
        hop_keys, hop_values, hop_factor, query_rot, hop_probs = recall(hop_step)
        d_probs = jnp.einsum(
            "shqd,shkd->shqk", d_attn, hop_values, preferred_element_type=jnp.float32
        )
        d_cross = (hop_probs * (d_probs - row_delta[..., None])).astype(jnp.bfloat16)
        d_rot = (
            jnp.einsum("shqk,shkd->shqd", d_cross, hop_keys, preferred_element_type=jnp.float32)
            * scaling
        )
        d_bar = d_bar + jnp.einsum("shqb,shab->shqa", d_rot, hop_factor, precision=HIGHEST)
        factor_local = jnp.einsum("shqa,shqb->shab", query_bar, d_rot, precision=HIGHEST)
        keys_total = (
            carry_keys
            + jnp.einsum("shqk,shqd->shkd", d_cross, query_rot, preferred_element_type=jnp.float32)
            * scaling
        )
        values_total = carry_values + jnp.einsum(
            "shqk,shqd->shkd",
            hop_probs.astype(jnp.bfloat16),
            d_attn,
            preferred_element_type=jnp.float32,
        )
        factor_total = factor_local + jnp.einsum(
            "shba,shbc->shac", factors, carry_factor, precision=HIGHEST
        )
        d_factors = d_factors + jnp.einsum(
            "shac,shbc->shab", carry_factor, hop_factor, precision=HIGHEST
        )
        carry_keys, carry_values, carry_factor = (
            passed_along(keys_total.astype(jnp.bfloat16), "ctx", -1).astype(keys_total.dtype),
            passed_along(values_total.astype(jnp.bfloat16), "ctx", -1).astype(values_total.dtype),
            passed_along(factor_total.astype(jnp.bfloat16), "ctx", -1).astype(factor_total.dtype),
        )
        return (carry_keys, carry_values, carry_factor, d_bar, d_factors)

    zero_rows = jnp.zeros(key_send.shape, jnp.float32)
    loop_state = lax.fori_loop(
        0, hop_total, back_hop, (zero_rows, zero_rows, zero_factor, zero_bar, zero_factor)
    )
    carry_keys, carry_values, d_bar, d_factors = (
        loop_state[0],
        loop_state[1],
        loop_state[3],
        loop_state[4],
    )
    d_local = probs_local * (d_probs_local - row_delta[..., None])
    values_sum = carry_values + jnp.einsum(
        "shqk,shqd->shkd", probs_local_low, d_attn, preferred_element_type=jnp.float32
    )
    d_queries, d_keys, d_house, d_betas = local_back((d_local, d_bar, carry_keys, d_factors))
    query_low = join_heads(d_queries.astype(jnp.bfloat16))
    key_low = join_heads(d_keys.astype(jnp.bfloat16))
    value_low = join_heads(values_sum.astype(jnp.bfloat16))
    house_low = join_heads(d_house.astype(jnp.bfloat16))
    beta_low = d_betas.transpose(0, 2, 1).astype(jnp.bfloat16)
    query_grad = weight_grad(h_one, query_low)
    key_grad = weight_grad(h_one, key_low)
    value_grad = weight_grad(h_one, value_low)
    house_grad = weight_grad(h_one, house_low)
    beta_grad = weight_grad(h_one, beta_low)
    partial_one = (
        project_back(query_low, query_full)
        + project_back(key_low, key_full)
        + project_back(value_low, value_full)
    )
    partial_one = (
        partial_one + project_back(house_low, house_full) + project_back(beta_low, beta_full)
    )
    d_one = lax.psum(partial_one.astype(jnp.bfloat16), "tp").astype(jnp.float32)
    gain_one_grad = jnp.sum(d_one * normed_one, axis=(0, 1))
    input_grad = (d_middle + norm_back(d_one, normed_one, factor_one, gain_one_f)).astype(
        jnp.bfloat16
    )

    def scattered(partial):
        first = lax.psum_scatter(partial, "fsdp", scatter_dimension=0, tiled=True)
        return lax.psum_scatter(first, "ctx", scatter_dimension=0, tiled=True)

    results = tuple(
        (
            scattered(gain_one_grad.astype(jnp.bfloat16)).astype(jnp.float32),
            scattered(query_grad.astype(jnp.bfloat16)).astype(jnp.float32),
            scattered(key_grad.astype(jnp.bfloat16)).astype(jnp.float32),
            scattered(value_grad.astype(jnp.bfloat16)).astype(jnp.float32),
            scattered(house_grad.astype(jnp.bfloat16)).astype(jnp.float32),
            scattered(beta_grad.astype(jnp.bfloat16)).astype(jnp.float32),
            scattered(out_grad.astype(jnp.bfloat16)).astype(jnp.float32),
            scattered(gain_two_grad.astype(jnp.bfloat16)).astype(jnp.float32),
            scattered(gate_grad.astype(jnp.bfloat16)).astype(jnp.float32),
            scattered(up_grad.astype(jnp.bfloat16)).astype(jnp.float32),
            scattered(down_grad.astype(jnp.bfloat16)).astype(jnp.float32),
        )
    )
    return (block_out, input_grad) + results


def halves(value):
    high = value.astype(jnp.bfloat16)
    return high, (value - high.astype(jnp.float32)).astype(jnp.bfloat16)


AB = (((1,), (0,)), ((), ()))
ABT = (((1,), (1,)), ((), ()))
ATB = (((0,), (0,)), ((), ()))


def mm(a, b, dims=AB):
    return lax.dot_general(a, b, dims, preferred_element_type=jnp.float32)


def mm3(a, b, dims=AB):
    left, right = dims[0][0][0], dims[0][1][0]
    return mm(
        jnp.concatenate([a[0], a[1], a[0]], axis=left),
        jnp.concatenate([b[0], b[0], b[1]], axis=right),
        dims,
    )


def each(function, *lists):
    return [function(*values) for values in zip(*lists)]


def square_index(size):
    row = lax.broadcasted_iota(jnp.int32, (size, size), 0)
    return row, lax.broadcasted_iota(jnp.int32, (size, size), 1)


def unit_lower_inverses(strict):
    size = strict[0].shape[0]
    part, half = size // 4, size // 2
    lane = lax.broadcasted_iota(jnp.int32, (part, size), 1)
    row = lax.broadcasted_iota(jnp.int32, (part, size), 0)
    block = lane // part
    col = lane - block * part
    own = [block == b for b in range(4)]
    zero = jnp.zeros((part, size), jnp.bfloat16)

    def side_by_side(matrix, below):
        packed = jnp.zeros((part, size), jnp.float32)
        for b in range(4 - below):
            packed = jnp.where(own[b], matrix[(b + below) * part : (b + below + 1) * part], packed)
        return packed

    def stacked(pair, order=(0, 1, 2, 3)):
        return tuple(
            jnp.concatenate(
                [zero if b is None else jnp.where(own[b], value, zero) for b in order], axis=0
            )
            for value in pair
        )

    diagonal = [side_by_side(matrix, 0) for matrix in strict]
    inverse = [
        jnp.where(row == col, 1.0, 0.0) - jnp.where((row >> 1) == (col >> 1), matrix, 0.0)
        for matrix in diagonal
    ]
    level = 1
    while (1 << level) < part:
        joined = ((row >> (level + 1)) == (col >> (level + 1))) & ((row >> level) != (col >> level))
        pairs = each(halves, inverse)
        steps = [
            mm3(halves(jnp.where(joined, matrix, 0.0)), stacked(pair))
            for matrix, pair in zip(diagonal, pairs)
        ]
        inverse = [
            value - mm3(pair, stacked(halves(step)))
            for value, pair, step in zip(inverse, pairs, steps)
        ]
        level += 1
    pairs = each(halves, inverse)
    even = own[0] | own[2]
    steps = [
        mm3(halves(jnp.where(even, side_by_side(matrix, 1), 0.0)), stacked(pair))
        for matrix, pair in zip(strict, pairs)
    ]
    corners = [
        -mm3(pair, stacked(halves(step), (None, 0, None, 2))) for pair, step in zip(pairs, steps)
    ]

    def joined_block(value, corner, n):
        lanes = slice(n * half, (n + 1) * half)
        upper = jnp.where(own[2 * n], value, 0.0)[:, lanes]
        return jnp.concatenate([upper, jnp.where(own[2 * n], corner, value)[:, lanes]], axis=0)

    first = [joined_block(value, corner, 0) for value, corner in zip(inverse, corners)]
    last = [joined_block(value, corner, 1) for value, corner in zip(inverse, corners)]
    steps = [mm3(halves(matrix[half:, :half]), halves(value)) for matrix, value in zip(strict, first)]
    lower = [-mm3(halves(value), halves(step)) for value, step in zip(last, steps)]
    blank = jnp.zeros((half, half), jnp.float32)
    return [
        jnp.concatenate(
            [
                jnp.concatenate([top, blank], axis=1),
                jnp.concatenate([left, right], axis=1),
            ],
            axis=0,
        )
        for top, left, right in zip(first, lower, last)
    ]


def unit_rows(raw):
    norm = lax.rsqrt(jnp.sum(raw * raw, axis=1, keepdims=True) + EPSILON)
    return raw * norm, norm


def below(matrix, row, col):
    return jnp.where(row > col, matrix, 0.0)


def key_halves(house_raw, keys, betas):
    row, col = square_index(keys[0].shape[0])
    house = [unit_rows(raw)[0] for raw in house_raw]
    scaled = [halves(beta * value) for beta, value in zip(betas, house)]
    strict = [below(mm3(a, halves(b), ABT), row, col) for a, b in zip(scaled, house)]
    house_key = [halves(below(mm3(a, halves(b), ABT), row, col)) for a, b in zip(scaled, keys)]
    inverses = unit_lower_inverses(strict)
    return inverses, [mm3(halves(a), b) for a, b in zip(inverses, house_key)]


def query_halves(queries, values, house_raw, keys, inverses, key_side, allowed):
    row, col = square_index(keys[0].shape[0])
    scaling = 1.0 / math.sqrt(queries[0].shape[1])
    q = each(halves, queries)
    query_house = [
        halves(jnp.where(row >= col, mm3(a, halves(unit_rows(raw)[0]), ABT), 0.0))
        for a, raw in zip(q, house_raw)
    ]
    scores = [mm3(a, halves(b), ABT) for a, b in zip(q, keys)]
    scores = [score - mm3(a, halves(b)) for score, a, b in zip(scores, query_house, key_side)]
    masked = [jnp.where(allowed, score * scaling, NEGATIVE) for score in scores]
    weights = [jnp.exp(value - jnp.max(value, axis=1, keepdims=True)) for value in masked]
    probs = [value / jnp.sum(value, axis=1, keepdims=True) for value in weights]
    attn = [mm(prob.astype(jnp.bfloat16), value) for prob, value in zip(probs, values)]
    return attn, probs, [mm3(a, halves(b)) for a, b in zip(query_house, inverses)]


def heads_backward(queries, keys, house_raw, values, betas, probs, key_side, query_side, d_attn):
    row, col = square_index(keys[0].shape[0])
    scaling = 1.0 / math.sqrt(queries[0].shape[1])
    house, norm = zip(*[unit_rows(raw) for raw in house_raw])
    d_values = [mm(prob.astype(jnp.bfloat16), d, ATB) for prob, d in zip(probs, d_attn)]
    d_probs = [mm(d, value, ABT) for d, value in zip(d_attn, values)]
    d_scores = [
        halves(prob * (d - jnp.sum(prob * d, axis=1, keepdims=True)) * scaling)
        for prob, d in zip(probs, d_probs)
    ]
    q, k, w = each(halves, queries), each(halves, keys), each(halves, house)
    scaled = [halves(beta * value) for beta, value in zip(betas, house)]
    side = each(halves, query_side)
    d_side = [-mm3(d, halves(value), ABT) for d, value in zip(d_scores, key_side)]
    d_query_house = [halves(jnp.where(row >= col, d, 0.0)) for d in d_side]
    d_strict = [halves(below(-mm3(a, halves(d), ATB), row, col)) for a, d in zip(side, d_side)]
    d_house_key = [halves(below(-mm3(a, d, ATB), row, col)) for a, d in zip(side, d_scores)]
    d_queries = [mm3(d, a) + mm3(e, b) for d, a, e, b in zip(d_scores, k, d_query_house, w)]
    d_keys = [
        mm3(d, a, ATB) + mm3(e, b, ATB) for d, a, e, b in zip(d_scores, q, d_house_key, scaled)
    ]
    d_scaled = [mm3(d, a) + mm3(e, b) for d, a, e, b in zip(d_strict, w, d_house_key, k)]
    d_house = [
        mm3(d, a, ATB) + mm3(e, b, ATB) for d, a, e, b in zip(d_strict, scaled, d_query_house, q)
    ]
    d_betas = [jnp.sum(d * value, axis=1, keepdims=True) for d, value in zip(d_scaled, house)]
    d_house = [d + beta * e for d, beta, e in zip(d_house, betas, d_scaled)]
    d_house_raw = [
        n * (d - value * jnp.sum(d * value, axis=1, keepdims=True))
        for n, d, value in zip(norm, d_house, house)
    ]
    d_logits = [d * beta * (1.0 - 0.5 * beta) for d, beta in zip(d_betas, betas)]
    return d_queries, d_keys, d_house_raw, d_values, d_logits


def head_slices(ref, first, heads, head):
    return [ref[:, first + n * head : first + (n + 1) * head] for n in range(heads)]


def started(pairs, sems):
    copies = [
        pltpu.make_async_copy(source, target, sems.at[n]) for n, (source, target) in enumerate(pairs)
    ]
    for copy in copies:
        copy.start()
    return copies


def token_rows(places, n, k, quarter):
    return pl.ds(pl.multiple_of(places[8 + n] + places[18 + k], 16), quarter)


def placed(gathered, whole, places):
    quarter = gathered.shape[1] // 4
    return [
        (
            gathered.at[n, pl.ds(k * quarter, quarter)],
            whole.at[pl.ds(pl.multiple_of(places[18 + k] + n * quarter, 16), quarter)],
        )
        for n in range(4)
        for k in range(4)
    ]


def split_tokens(whole, parts, places):
    quarter = parts[0].shape[0] // 4
    for n in range(4):
        for k in range(4):
            parts[n][pl.ds(k * quarter, quarter)] = whole[token_rows(places, n, k, quarter)]


def wide_row(row, rows):
    return jnp.broadcast_to(row, (rows, row.shape[1])).astype(jnp.bfloat16)


def own_blocks(places, source, target, sequence=26, at=0):
    quarter = target.shape[-2]
    rows = pl.ds(pl.multiple_of(places[22], 16), quarter)
    return [(source.at[places[sequence + k], rows], target.at[k + at]) for k in range(4)]


def message_kernel(places, hidden_in, ids, gain_one, gain_two, *refs):
    messages, blocks, sems = refs[0:4], refs[4], refs[5]
    quarter, features = blocks.shape[1], blocks.shape[2]
    rows, depth = ids.shape[1], gain_one.shape[0]
    copies = started(own_blocks(places, hidden_in, blocks), sems)
    for k in range(4):
        messages[k][:, features:] = jnp.zeros((quarter, 640), jnp.bfloat16)
        own_ids = ids[pl.ds(places[26 + k], 1)].astype(jnp.float32)
        messages[k][:, features : features + rows] = wide_row(own_ids, quarter)
        at = features + 128
        messages[k][:, at : at + depth] = wide_row(gain_one[...].astype(jnp.float32)[None], quarter)
        at += 256
        messages[k][:, at : at + depth] = wide_row(gain_two[...].astype(jnp.float32)[None], quarter)
    for copy in copies:
        copy.wait()
    for k in range(4):
        messages[k][:, :features] = blocks[k]


def attention_pack_kernel(places, house, key, beta, query, value, out, pack):
    at = 0
    for source in (house, key, beta, query, value, out):
        width = source.shape[1]
        if width < 128:
            pack[:, at : at + 128] = jnp.zeros((pack.shape[0], 128), jnp.bfloat16)
        pack[:, at : at + width] = source[...]
        at += max(width, 128)


def feed_forward_pack_kernel(places, output_grad, gate, up, down, *refs):
    messages, gives, keeps, blocks, sems = refs[0:4], refs[4:6], refs[6:8], refs[8], refs[9]
    copies = started(
        own_blocks(places, output_grad, blocks) + own_blocks(places, output_grad, blocks, 30, 4), sems
    )
    units = gate.shape[1] // 2
    part = units // 2
    for packs, start in ((keeps, places[23]), (gives, places[24])):
        for n in range(6):
            at = pl.ds(pl.multiple_of(start + n % 2 * part, 128), part)
            packs[n // 3][:, n % 3 * part : (n % 3 + 1) * part] = (gate, up, down)[n // 2][:, at]
    for copy in copies:
        copy.wait()
    for k in range(4):
        messages[k][0] = blocks[k]
        messages[k][1] = blocks[4 + k]


def out_message_kernel(places, *refs):
    out_parts, middle, messages = refs[0:4], refs[4], refs[5:9]
    quarter = middle.shape[0] // 4
    out = sum(part[...].astype(jnp.float32) for part in out_parts)
    own, pair = (middle[...] + out[0]).astype(jnp.bfloat16), out[1].astype(jnp.bfloat16)
    for k in range(4):
        messages[k][:quarter] = own[k * quarter : (k + 1) * quarter]
        messages[k][quarter:] = pair[(k ^ 2) * quarter : ((k ^ 2) + 1) * quarter]


def result_kernel(places, d_parts, d_middle, block, gain, gain_two_grad, *messages):
    quarter, features = block.shape[0] // 4, block.shape[1]
    d_one = sum(d_parts[n].astype(jnp.float32) for n in range(4))
    x = block[...].astype(jnp.float32)
    factor = lax.rsqrt(jnp.mean(x * x, axis=1, keepdims=True) + EPSILON)
    normed = x * factor
    scaled = d_one * gain[...]
    mean = jnp.mean(scaled * normed, axis=1, keepdims=True)
    in_grad = (d_middle[...] + factor * (scaled - normed * mean)).astype(jnp.bfloat16)
    gain_one_grad = jnp.sum(d_one * normed, axis=0, keepdims=True)
    row = lax.broadcasted_iota(jnp.int32, (quarter, 128), 0)
    for g, gains in enumerate((gain_one_grad, gain_two_grad[...])):
        packed = jnp.zeros((quarter, 128), jnp.float32)
        for n in range(features // 128):
            packed = jnp.where(row == n, gains[:, n * 128 : (n + 1) * 128], packed)
        at = features + g * 128
        for k in range(4):
            messages[k][:, at : at + 128] = packed.astype(jnp.bfloat16)
    for k in range(4):
        messages[k][:, :features] = in_grad[k * quarter : (k + 1) * quarter]


def spread_kernel(places, pieces, whole):
    quarter, features = whole.shape[1] // 4, whole.shape[2]
    for n in range(4):
        for k in range(4):
            rows = slice(k * quarter, (k + 1) * quarter)
            whole[pl.ds(places[26 + k], 1), n * quarter : (n + 1) * quarter] = pieces[
                n, rows, :features
            ][None]


def gradient_spread_kernel(places, pieces, whole, gains):
    quarter, features = whole.shape[1] // 4, whole.shape[2]
    spread_kernel(places, pieces, whole)
    gains[...] = sum(pieces[n, :quarter, features:].astype(jnp.float32) for n in range(4))


def weights_in_place(pieces, whole, places, first=0, count=None):
    depth = pieces[0].shape[0]
    width = count or pieces[0].shape[1]
    return [
        (
            pieces[n].at[:, pl.ds(first, width)],
            whole.at[pl.ds(pl.multiple_of(places[n], 64), depth), pl.ds(0, width)],
        )
        for n in range(8)
    ]


def keys_kernel(heads, places, *refs):
    weights, xs, gain = refs[0:8], refs[8], refs[9]
    h_all, proj, inverses, key_side = refs[10:14]
    w_all, weight_sems, x_sems, x_all = refs[14:18]
    x_copies = started(placed(xs, x_all, places), x_sems)
    w_copies = started(weights_in_place(weights, w_all, places, 0, w_all.shape[1]), weight_sems)
    for copy in x_copies:
        copy.wait()
    width = (proj.shape[1] - 128) // 2
    head = width // heads
    x = x_all[...].astype(jnp.float32)
    factor = lax.rsqrt(jnp.mean(x * x, axis=1, keepdims=True) + EPSILON)
    h_all[...] = (x * factor * gain[...]).astype(jnp.bfloat16)
    for copy in w_copies:
        copy.wait()
    proj[...] = mm(h_all[...], w_all[...])
    betas = 2.0 * jax.nn.sigmoid(proj[:, 2 * width :])
    results = key_halves(
        head_slices(proj, 0, heads, head),
        head_slices(proj, width, heads, head),
        [betas[:, n : n + 1] for n in range(heads)],
    )
    for n in range(heads):
        inverses[n], key_side[n] = results[0][n], results[1][n]


def queries_kernel(heads, places, *refs):
    weights, (h_all, proj_keys, inverses, key_side, id_row, id_col) = refs[0:8], refs[8:14]
    proj, attn, probs, query_side, parts = refs[14], refs[15], refs[16], refs[17], refs[18:22]
    w_all, total, sems = refs[22:25]
    skip = weights[0].shape[1] - w_all.shape[1]
    for copy in started(weights_in_place(weights, w_all, places, skip, w_all.shape[1]), sems):
        copy.wait()
    width = attn.shape[1]
    head = width // heads
    proj[...] = mm(h_all[...], w_all[:, : 2 * width])
    row, col = square_index(h_all.shape[0])
    results = query_halves(
        head_slices(proj, 0, heads, head),
        [value.astype(jnp.bfloat16) for value in head_slices(proj, width, heads, head)],
        head_slices(proj_keys, 0, heads, head),
        head_slices(proj_keys, width, heads, head),
        [inverses[n] for n in range(heads)],
        [key_side[n] for n in range(heads)],
        (col <= row) & (id_row[...] == id_col[...]),
    )
    for n in range(heads):
        attn[:, n * head : (n + 1) * head] = results[0][n].astype(jnp.bfloat16)
        probs[n], query_side[n] = results[1][n], results[2][n]
    total[...] = mm(attn[...], w_all[:, 2 * width :], ABT).astype(jnp.bfloat16)
    split_tokens(total, parts, places)


def token_copies(gathered, whole, rows):
    return [
        (gathered[s].at[n], whole.at[pl.ds((s * 4 + n) * rows, rows)]) for s in range(2) for n in range(4)
    ]


def exchanged_copies(pieces, whole, places, rows):
    return [
        (pieces[n].at[s], whole.at[token_block(places, s, n, rows)]) for n in range(4) for s in range(2)
    ]


def token_block(places, s, n, rows):
    return pl.ds(pl.multiple_of(places[8 + n] * 4 + s * 4 * rows, 64), rows)


def feed_forward_kernel(places, *refs):
    weights, ins, grads = refs[0:16], refs[16:18], refs[18:22]
    two_parts, common = refs[22:30], refs[30]
    w_all, in_all, grad_all, total, weight_sems, in_sems, grad_sems = refs[31:38]
    rows, units = two_parts[0].shape[0], w_all.shape[1] // 3
    depth, part = weights[0].shape[0], w_all.shape[1] // 2
    w_pairs = []
    for n in range(16):
        row = pl.ds(pl.multiple_of(places[n // 2], 64), depth)
        w_pairs.append((weights[n], w_all.at[row, pl.ds(n % 2 * part, part)]))
    w_copies = started(w_pairs, weight_sems)
    grad_copies = started(exchanged_copies(grads, grad_all, places, rows), grad_sems)
    in_copies = started(token_copies(ins, in_all, rows), in_sems)
    for copy in w_copies + in_copies:
        copy.wait()
    both = mm(in_all[...], w_all[:, : 2 * units])
    for copy in grad_copies:
        copy.wait()
    d_hidden = mm(grad_all[...], w_all[:, 2 * units :])
    gate, up = both[:, :units], both[:, units:]
    sigmoid = jax.nn.sigmoid(gate)
    silu = gate * sigmoid
    d_gate = d_hidden * up * sigmoid * (1.0 + gate * (1.0 - sigmoid))
    for n, value in enumerate((d_gate, d_hidden * silu, silu * up)):
        common[:, n * units : (n + 1) * units] = value.astype(jnp.bfloat16)
    total[...] = mm(common[:, : 2 * units], w_all[:, : 2 * units], ABT).astype(jnp.bfloat16)
    for s in range(2):
        for n in range(4):
            two_parts[s * 4 + n][...] = total[token_block(places, s, n, rows)]


def feed_forward_rest_kernel(places, *refs):
    weights, ins, grads, common = refs[0:8], refs[8:10], refs[10:14], refs[14]
    out_parts, mine, other = refs[15:19], refs[19], refs[20]
    w_all, in_all, grad_all, total, weight_sems, in_sems, grad_sems = refs[21:28]
    rows, units = out_parts[0].shape[1], w_all.shape[1]
    depth, half = weights[0].shape[0], w_all.shape[0] // 2
    lanes = pl.ds(weights[0].shape[1] - units, units)
    w_copies = started(
        [
            (
                weights[n].at[:, lanes],
                w_all.at[pl.ds(pl.multiple_of(places[n], 64), depth)],
            )
            for n in range(8)
        ],
        weight_sems,
    )
    grad_copies = started(exchanged_copies(grads, grad_all, places, rows), grad_sems)
    in_copies = started(token_copies(ins, in_all, rows), in_sems)
    for copy in in_copies + grad_copies:
        copy.wait()
    for target, place in ((other, 13), (mine, 12)):
        at = pl.ds(pl.multiple_of(places[place], 128), half)
        target[:, :half] = in_all[:, at]
        target[:, half:] = grad_all[:, at]
    for copy in w_copies:
        copy.wait()
    total[...] = mm(common[:, 2 * units :], w_all[...], ABT).astype(jnp.bfloat16)
    for s in range(2):
        for n in range(4):
            out_parts[n][s] = total[token_block(places, s, n, rows)]


def attention_backward_kernel(heads, places, *refs):
    weights, ds = refs[0:8], refs[8]
    proj_keys, proj, probs, key_side, query_side, h_all, attn = refs[9:16]
    keeps, sends, parts = refs[16:19]
    w_first, w_second, d_all, d_attn, total, first_sems, second_sems, d_sems = refs[19:27]
    half, width = d_all.shape[1] // 2, d_attn.shape[1]
    d_keys_all = keeps.at[:, pl.ds(2 * half, 2 * width + 128)]
    d_queries_all = keeps.at[:, pl.ds(2 * half + 2 * width + 128, 2 * width)]
    cut, rest = w_first.shape[1], w_second.shape[1]
    second_copies = started(weights_in_place(weights, w_second, places, cut, rest), second_sems)
    d_copies = started(placed(ds, d_all, places), d_sems)
    first_copies = started(weights_in_place(weights, w_first, places, 0, cut), first_sems)
    for copy in d_copies + second_copies:
        copy.wait()
    head = width // heads
    d_attn[...] = mm(d_all[...], w_second[:, 2 * width :]).astype(jnp.bfloat16)
    betas = 2.0 * jax.nn.sigmoid(proj_keys[:, 2 * width :])
    lane = lax.broadcasted_iota(jnp.int32, betas.shape, 1)
    logits = jnp.zeros(betas.shape, jnp.float32)
    results = heads_backward(
        head_slices(proj, 0, heads, head),
        head_slices(proj_keys, width, heads, head),
        head_slices(proj_keys, 0, heads, head),
        [value.astype(jnp.bfloat16) for value in head_slices(proj, width, heads, head)],
        [betas[:, n : n + 1] for n in range(heads)],
        [probs[n] for n in range(heads)],
        [key_side[n] for n in range(heads)],
        [query_side[n] for n in range(heads)],
        head_slices(d_attn, 0, heads, head),
    )
    for n in range(heads):
        d_queries, d_keys, d_house, d_values, d_logit = [result[n] for result in results]
        low_at, high_at = slice(n * head, (n + 1) * head), slice(width + n * head, width + (n + 1) * head)
        d_keys_all[:, low_at] = d_house.astype(jnp.bfloat16)
        d_keys_all[:, high_at] = d_keys.astype(jnp.bfloat16)
        d_queries_all[:, low_at] = d_queries.astype(jnp.bfloat16)
        d_queries_all[:, high_at] = d_values.astype(jnp.bfloat16)
        logits = jnp.where(lane == n, d_logit, logits)
    d_keys_all[:, 2 * width :] = logits.astype(jnp.bfloat16)
    for copy in first_copies:
        copy.wait()
    keeps[:, keeps.shape[1] - width :] = attn[...]
    sends[:, 2 * half :] = keeps[:, 2 * half :]
    for target, place in ((keeps, 12), (sends, 13)):
        lanes = pl.ds(pl.multiple_of(places[place], 128), half)
        target[:, :half] = h_all[:, lanes]
        target[:, half : 2 * half] = d_all[:, lanes]
    total[...] = (
        mm(d_keys_all[...], w_first[...], ABT) + mm(d_queries_all[...], w_second[:, : 2 * width], ABT)
    ).astype(jnp.bfloat16)
    quarter = parts.shape[1] // 4
    for n in range(4):
        for k in range(4):
            rows = pl.ds(pl.multiple_of(places[18 + k] + n * quarter, 16), quarter)
            parts[n, k * quarter : (k + 1) * quarter] = total[rows]


def weight_grad_kernel(groups, count, places, *refs):
    mine, came, outs, total = refs[0:count], refs[count : 2 * count], refs[2 * count : -1], refs[-1]
    right = count - 1
    half, at = total.shape[0], 0
    for left, start, width in groups:
        lefts, rights = slice(left * half, (left + 1) * half), slice(start, start + width)
        total[:, at : at + width] = (
            mm(mine[0][:, lefts], mine[right][:, rights], ATB)
            + mm(came[0][:, lefts], came[right][:, rights], ATB)
        ).astype(jnp.bfloat16)
        at += width
    depth, at = outs[0].shape[1], 0
    for n in range(0, len(outs), 2):
        width = outs[n].shape[2]
        for k in range(4):
            rows = pl.ds(pl.multiple_of(places[14 + k], 64), depth)
            outs[n + k % 2][k // 2] = total[rows, at : at + width]
        at += width


VMEM_BYTES = 56 * 1024 * 1024


def call(kernel, outs, scratch, places, operands, spaces, micros, out_spaces=None):
    vmem = pl.BlockSpec(memory_space=pltpu.VMEM)
    kinds = {"v": vmem, "a": pl.BlockSpec(memory_space=pl.ANY)}
    return pl.pallas_call(
        kernel,
        out_shape=[jax.ShapeDtypeStruct(shape, kind) for shape, kind in outs],
        in_specs=[pl.BlockSpec(memory_space=pltpu.SMEM)] + [kinds[s] for s in spaces],
        out_specs=[kinds[s] for s in out_spaces or "v" * len(outs)],
        scratch_shapes=scratch,
        compiler_params=pltpu.CompilerParams(vmem_limit_bytes=VMEM_BYTES),
        cost_estimate=pl.CostEstimate(
            flops=int(micros * 1e6), transcendentals=0, bytes_accessed=int(micros * 1e4)
        ),
    )(places, *operands)


def swap(block, axis, distance):
    size = lax.axis_size(axis)
    return lax.ppermute(block, axis, [(i, i ^ distance) for i in range(size)])


def gathered_tp(block):
    return lax.all_gather(block, "tp", axis=0)


def all_tp(block):
    return [block] + [swap(block, "tp", n) for n in (1, 2, 3)]


def to_owners(messages):
    return [messages[0]] + [swap(messages[n], "ctx", n) for n in (1, 2, 3)]


def sum_tp(parts):
    return [parts[0]] + [swap(parts[n], "tp", n) for n in (1, 2, 3)]


def add_up(blocks):
    total = blocks[0].astype(jnp.float32)
    for block in blocks[1:]:
        total = total + block.astype(jnp.float32)
    return total


def other_core(block):
    return swap(block, "fsdp", 1)


def whole_sequences(
    hidden_in,
    segment_ids,
    doc_starts,
    norm1_gain,
    w_query,
    w_key,
    w_value,
    w_house,
    w_beta,
    w_out,
    norm2_gain,
    w_gate,
    w_up,
    w_down,
    output_grad,
):
    low, wide = jnp.bfloat16, jnp.float32
    core, chain, column = lax.axis_index("fsdp"), lax.axis_index("ctx"), lax.axis_index("tp")
    rows, features = hidden_in.shape[1], hidden_in.shape[2]
    depth, width, heads = w_query.shape[0], w_query.shape[1], w_beta.shape[1]
    length, half, quarter = 4 * rows, features // 2, rows // 4
    units, used = w_gate.shape[1] // 2, 4 * width + 128
    near = jnp.arange(4, dtype=jnp.int32)
    upper = (chain // 2).astype(jnp.int32)
    places = jnp.concatenate(
        [
            (core * 4 + (chain ^ near)) * depth,
            ((1 - core) * 4 + (chain ^ near)) * depth,
            (column ^ near) * quarter,
            jnp.stack([core, 1 - core]) * half,
            (chain ^ near) * depth,
            (chain ^ near) * rows,
            jnp.stack([column * quarter, upper * units, (1 - upper) * units, upper]),
            chain ^ near,
            chain ^ near ^ 2,
        ]
    ).astype(jnp.int32)
    step = lax.optimization_barrier
    block = pltpu.VMEM((4, quarter, features), low)
    token_messages = call(
        message_kernel,
        [((quarter, features + 640), low)] * 4,
        [block, pltpu.SemaphoreType.DMA((4,))],
        places,
        [hidden_in, segment_ids, norm1_gain, norm2_gain],
        "avvv",
        2,
    )
    (pack,) = call(
        attention_pack_kernel,
        [((depth, used + width), low)],
        [],
        places,
        [w_house, w_key, w_beta, w_query, w_value, w_out],
        "v" * 6,
        2,
    )
    x_messages, pack, output_grad = step((to_owners(token_messages), pack, output_grad))
    packed = call(
        feed_forward_pack_kernel,
        [((2, quarter, features), low)] * 4
        + [((depth, 3 * units // 2), low)] * 4,
        [pltpu.VMEM((8, quarter, features), low), pltpu.SemaphoreType.DMA((8,))],
        places,
        [output_grad, w_gate, w_up, w_down],
        "avvv",
        3,
    )
    grad_messages, gives, ffn_keeps = packed[:4], packed[4:6], packed[6:8]

    pack_two, pack_one = swap(pack, "ctx", 2), swap(pack, "ctx", 1)
    x_block = jnp.concatenate([message[:, :features] for message in x_messages])
    x_pieces = gathered_tp(x_block)
    info = jnp.stack([message[0, features:] for message in x_messages])
    chosen = near[:, None] == (near[None, :] ^ chain)
    info = jnp.sum(jnp.where(chosen[:, :, None], info[None].astype(wide), 0.0), axis=1)
    ids = info[:, :rows].reshape(length)
    gains = jnp.concatenate(
        [info[:, 128 : 128 + depth], info[:, 384 : 384 + depth]], axis=1
    ).astype(low)
    id_row, id_col = ids[None, :], ids[:, None]
    id_row, id_col, pack_two, pack_one, x_pieces, pack, gains, grad_messages, gives = step(
        (id_row, id_col, pack_two, pack_one, x_pieces, pack, gains, grad_messages, gives)
    )

    pack_three = swap(pack_two, "ctx", 1)
    gains_other = other_core(gains)
    gains = jnp.where(core == 0, jnp.stack([gains, gains_other]), jnp.stack([gains_other, gains]))
    gain_one = gains[:, :, :depth].reshape(1, features).astype(wide)
    gain_two = gains[:, :, depth:].reshape(1, features).astype(wide)
    grad_messages = to_owners(grad_messages)
    pack_three, pack_two, pack_one, pack, gain_one, gives, grad_messages, ffn_keeps = step(
        (pack_three, pack_two, pack_one, pack, gain_one, gives, grad_messages, ffn_keeps)
    )

    attn_weights = [pack, pack_one, pack_two, pack_three]
    attn_weights = attn_weights + [other_core(piece) for piece in attn_weights]
    give_two = [swap(gives[0], "ctx", 2)]
    keep_one = [swap(ffn_keeps[0], "ctx", 1)]
    grads = jnp.stack(
        [
            jnp.concatenate([message[0] for message in grad_messages]),
            jnp.concatenate([grad_messages[n ^ 2][1] for n in range(4)]),
        ]
    )
    own_grad = grads[0]
    grad_pieces = all_tp(grads)
    square = ((heads, length, length), wide)
    h_all, proj_keys, inverses, key_side = call(
        functools.partial(keys_kernel, heads),
        [((length, features), low), ((length, 2 * width + 128), wide), square, square],
        [
            pltpu.VMEM((features, 2 * width + 128), low),
            pltpu.SemaphoreType.DMA((8,)),
            pltpu.SemaphoreType.DMA((16,)),
            pltpu.VMEM((length, features), low),
        ],
        places,
        [*attn_weights, x_pieces, gain_one],
        "a" * 9 + "v",
        20,
    )
    outs = call(
        functools.partial(queries_kernel, heads),
        [((length, 2 * width), wide), ((length, width), low), square, square]
        + [((rows, features), low)] * 4,
        [
            pltpu.VMEM((features, 3 * width), low),
            pltpu.VMEM((length, features), low),
            pltpu.SemaphoreType.DMA((8,)),
        ],
        places,
        [*attn_weights, h_all, proj_keys, inverses, key_side, id_row, id_col],
        "a" * 8 + "v" * 6,
        9,
    )
    proj, attn, probs, query_side = outs[:4]
    give_two, branch_parts, keep_one, grad_pieces, give_last, ffn_keeps = step(
        (give_two, outs[4:], keep_one, grad_pieces, gives[1], ffn_keeps)
    )
    give_two = give_two + [swap(give_last, "ctx", 2)]
    give_three = [swap(give_two[0], "ctx", 1)]
    middle = x_block.astype(wide) + add_up(sum_tp(branch_parts))
    normed_two, factor_two = norm_rows(middle)
    h_two = (normed_two * gain_two).astype(low)
    give_two, give_three, ffn_keeps, h_two = step((give_two, give_three, ffn_keeps, h_two))

    h_pair = swap(h_two, "ctx", 2)
    give_three = give_three + [swap(give_two[1], "ctx", 1)]
    keep_one = keep_one + [swap(ffn_keeps[1], "ctx", 1)]
    h_own = gathered_tp(h_two)
    h_pair, give_three, h_own, keep_one, give_two = step(
        (h_pair, give_three, h_own, keep_one, give_two)
    )
    ffn_weights = [*ffn_keeps, *keep_one, *give_two, *give_three]
    ffn_weights = ffn_weights + [other_core(piece) for piece in ffn_weights]
    h_pair = gathered_tp(h_pair)

    tokens = 2 * length
    pair = ((2, rows, features), low)
    outs = call(
        feed_forward_kernel,
        [((rows, features), low)] * 8 + [((tokens, 3 * units), low)],
        [
            pltpu.VMEM((features, 3 * units), low),
            pltpu.VMEM((tokens, features), low),
            pltpu.VMEM((tokens, features), low),
            pltpu.VMEM((tokens, features), low),
            pltpu.SemaphoreType.DMA((16,)),
            pltpu.SemaphoreType.DMA((8,)),
            pltpu.SemaphoreType.DMA((8,)),
        ],
        places,
        [*ffn_weights, h_own, h_pair, *grad_pieces],
        "a" * 22,
        12,
    )
    own_parts, pair_parts, common = outs[:4], outs[4:8], outs[8]
    rest = call(
        feed_forward_rest_kernel,
        [pair] * 4 + [((tokens, features), low)] * 2,
        [
            pltpu.VMEM((features, units), low),
            pltpu.VMEM((tokens, features), low),
            pltpu.VMEM((tokens, features), low),
            pltpu.VMEM((tokens, features), low),
            pltpu.SemaphoreType.DMA((8,)),
            pltpu.SemaphoreType.DMA((8,)),
            pltpu.SemaphoreType.DMA((8,)),
        ],
        places,
        [*ffn_weights[1::2], h_own, h_pair, *grad_pieces, common],
        "a" * 14 + "v",
        4,
    )
    out_parts, keeps, sends = rest[:4], rest[4], rest[5]

    def grads_of(mine, came, groups, pieces=1):
        total = sum(group[2] for group in groups)
        return call(
            functools.partial(weight_grad_kernel, groups, len(mine)),
            [((2, depth, total // pieces), low)] * (2 * pieces),
            [pltpu.VMEM((half, total), low)],
            places,
            [*mine, *came],
            "v" * (2 * len(mine)),
            total / 400.0,
        )

    pair_sum = add_up(sum_tp(pair_parts)).astype(low)
    common_came, pair_sum, own_parts, keeps, sends, out_parts = step(
        (other_core(common), pair_sum, own_parts, keeps, sends, out_parts)
    )
    came = (other_core(sends), common_came)

    two_other = swap(pair_sum, "ctx", 2)
    own_received = sum_tp(own_parts)
    ffn_grads = grads_of(
        (keeps, common), came, ((0, 0, 2 * units), (1, 2 * units, units)), 2
    )
    own_received, two_other, ffn_grads = step((own_received, two_other, tuple(ffn_grads)))
    d_two = add_up(own_received + [two_other])
    gain_two_grad = jnp.sum(d_two * normed_two, axis=0, keepdims=True)
    d_middle = own_grad.astype(wide) + norm_back(d_two, normed_two, factor_two, gain_two)
    d_low, ffn_grads = step((d_middle.astype(low), tuple(ffn_grads)))

    ffn_came = [swap(ffn_grads[1], "ctx", 1)]
    d_pieces = gathered_tp(d_low)
    ffn_sums = [add_up([ffn_grads[0], ffn_came[0]])]
    ffn_leave = ffn_sums[0][1].astype(low)
    d_pieces, out_parts, ffn_leave, ffn_far = step((d_pieces, out_parts, ffn_leave, ffn_grads[3]))

    ffn_other = [swap(ffn_leave, "ctx", 2)]
    ffn_came = ffn_came + [swap(ffn_far, "ctx", 1)]
    out_received = sum_tp(out_parts)
    back = call(
        functools.partial(attention_backward_kernel, heads),
        [((length, features + used + width), low)] * 2 + [((4, rows, features), low)],
        [
            pltpu.VMEM((features, 2 * width + 128), low),
            pltpu.VMEM((features, 3 * width), low),
            pltpu.VMEM((length, features), low),
            pltpu.VMEM((length, width), low),
            pltpu.VMEM((length, features), low),
            pltpu.SemaphoreType.DMA((8,)),
            pltpu.SemaphoreType.DMA((8,)),
            pltpu.SemaphoreType.DMA((16,)),
        ],
        places,
        [*attn_weights, d_pieces, proj_keys, proj, probs, key_side, query_side, h_all, attn],
        "a" * 9 + "v" * 7,
        14,
    )
    ffn_sums = ffn_sums + [add_up([ffn_grads[2], ffn_came[1]])]
    ffn_leave, ffn_other, out_received, (keeps, sends, d_parts) = step(
        (ffn_sums[1][1].astype(low), ffn_other, out_received, tuple(back))
    )

    out_messages = call(
        out_message_kernel,
        [((2 * quarter, features), low)] * 4,
        [],
        places,
        [*out_received, middle],
        "v" * 5,
        2,
    )
    came, keeps, d_parts, out_messages, ffn_leave = step(
        (other_core(sends), keeps, d_parts, tuple(out_messages), ffn_leave)
    )

    ffn_other = ffn_other + [swap(ffn_leave, "ctx", 2)]
    query_start = features + 2 * width + 128
    near_two, far_two = grads_of(
        (keeps,), (came,), ((0, query_start, 2 * width), (1, query_start + 2 * width, width))
    )
    out_messages, near_two, far_two, keeps = step((out_messages, near_two, far_two, keeps))
    two_came = swap(far_two, "ctx", 1)
    out_messages = to_owners(out_messages)
    near_one, far_one = grads_of((keeps,), (came,), ((0, features, 2 * width + 128),))
    d_parts, near_one, far_one = step((d_parts, near_one, far_one))
    d_received = lax.all_to_all(d_parts, "tp", 0, 0)
    messages = call(
        result_kernel,
        [((quarter, features + 256), low)] * 4,
        [],
        places,
        [d_received, d_middle, x_block, gain_one, gain_two_grad],
        "v" * 5,
        3,
    )
    two_sum = add_up([near_two, two_came])
    two_leave, near_one, far_one, messages, out_messages, ffn_other = step(
        (two_sum[1].astype(low), near_one, far_one, tuple(messages), out_messages, ffn_other)
    )

    one_came = swap(far_one, "ctx", 1)
    query_other = swap(two_leave, "ctx", 2)
    messages = step(to_owners(messages))
    owned = jnp.concatenate([message[:, :features] for message in messages])
    gain_sum = add_up([message[:, features:] for message in messages]).astype(low)
    owned = jnp.concatenate([owned, jnp.pad(gain_sum, ((0, 3 * quarter), (0, 0)))], axis=1)
    input_grad, gain_total = call(
        gradient_spread_kernel,
        [((4, rows, features), low), ((quarter, 256), wide)],
        [],
        places,
        [gathered_tp(owned)],
        "v",
        3,
    )
    one_sum = add_up([near_one, one_came])
    out_block = jnp.concatenate(
        [add_up([out_messages[n][:quarter], out_messages[n ^ 2][quarter:]]) for n in range(4)]
    ).astype(low)
    one_leave, input_grad, gain_total, query_other, out_block = step(
        (one_sum[1].astype(low), input_grad, gain_total, query_other, out_block)
    )

    key_other = swap(one_leave, "ctx", 2)
    block_out = call(
        spread_kernel, [((4, rows, features), low)], [], places, [gathered_tp(out_block)], "v", 2
    )[0]
    gain_total = gain_total + other_core(gain_total)
    gain_total = jnp.concatenate(
        [gain_total[: features // 128, :128], gain_total[: features // 128, 128:]]
    ).reshape(2, features)
    gain_total = lax.dynamic_slice_in_dim(gain_total, (core * 4 + chain) * depth, depth, axis=1)
    query_grads = two_sum[0] + query_other.astype(wide)
    key_grads = one_sum[0] + key_other.astype(wide)

    ffn_kept = jnp.concatenate([total[0] for total in ffn_sums], axis=1)
    ffn_other = jnp.concatenate(ffn_other, axis=1).astype(wide)

    def ffn_result(n):
        kept = ffn_kept[:, n * units : (n + 1) * units]
        came = ffn_other[:, n * units : (n + 1) * units]
        return jnp.concatenate(
            [jnp.where(upper == 1, came, kept), jnp.where(upper == 1, kept, came)], axis=1
        )

    return (
        block_out,
        input_grad,
        gain_total[0],
        query_grads[:, :width],
        key_grads[:, width : 2 * width],
        query_grads[:, width : 2 * width],
        key_grads[:, :width],
        key_grads[:, 2 * width : 2 * width + heads],
        query_grads[:, 2 * width :],
        gain_total[1],
        ffn_result(0),
        ffn_result(1),
        ffn_result(2),
    )


def shards(*args):
    sizes = [lax.axis_size(axis) for axis in ("fsdp", "ctx", "tp")]
    if sizes == [2, 4, 4] and args[0].shape[:2] == (4, 64):
        return whole_sequences(*args)
    return ring_of_groups(*args)


def solution(mesh):
    in_specs = (
        P("fsdp", "ctx", None),
        P("fsdp", "ctx"),
        P("fsdp", "ctx"),
        P(("fsdp", "ctx")),
        P(("fsdp", "ctx"), "tp"),
        P(("fsdp", "ctx"), "tp"),
        P(("fsdp", "ctx"), "tp"),
        P(("fsdp", "ctx"), "tp"),
        P(("fsdp", "ctx"), "tp"),
        P(("fsdp", "ctx"), "tp"),
        P(("fsdp", "ctx")),
        P(("fsdp", "ctx"), "tp"),
        P(("fsdp", "ctx"), "tp"),
        P(("fsdp", "ctx"), "tp"),
        P("fsdp", "ctx", None),
    )
    out_specs = (
        P("fsdp", "ctx", None),
        P("fsdp", "ctx", None),
        P(("fsdp", "ctx")),
        P(("fsdp", "ctx"), "tp"),
        P(("fsdp", "ctx"), "tp"),
        P(("fsdp", "ctx"), "tp"),
        P(("fsdp", "ctx"), "tp"),
        P(("fsdp", "ctx"), "tp"),
        P(("fsdp", "ctx"), "tp"),
        P(("fsdp", "ctx")),
        P(("fsdp", "ctx"), "tp"),
        P(("fsdp", "ctx"), "tp"),
        P(("fsdp", "ctx"), "tp"),
    )
    return jax.shard_map(shards, mesh=mesh, in_specs=in_specs, out_specs=out_specs, check_vma=False)
```
